32 devices in a mesh: dp: 16 (over z, y, x), tensor: 2 (over core).
Axes of the slice: x: 2, y: 2, z: 4, core: 2. Of those that a mesh axis runs over, the one named last changes fastest.
Arguments:
- tokens: bfloat16 [4, 16, 2048, 1024], P(None, 'dp', None, 'tensor'), may hold values from -40 to 40
- routed: int32 [4, 16, 256], P(None, 'dp'), may hold values from 0 to 2047, as said below
- w_query: bfloat16 [1024, 1024], P('dp', 'tensor'), may hold values from -0.1875 to 0.1875
- w_key: bfloat16 [1024, 1024], P('dp', 'tensor'), may hold values from -0.1875 to 0.1875
- w_value: bfloat16 [1024, 1024], P('dp', 'tensor'), may hold values from -0.1875 to 0.1875
- w_out: bfloat16 [1024, 1024], P('tensor', 'dp'), may hold values from -1 to 1
- w_up: bfloat16 [1024, 4096], P('dp', 'tensor'), may hold values from -0.1875 to 0.1875
- w_down: bfloat16 [4096, 1024], P('tensor', 'dp'), may hold values from -0.09375 to 0.09375
- w_route: bfloat16 [1024], P('dp'), may hold values from -0.09375 to 0.09375
- gain_attn: bfloat16 [1024], P('dp'), may hold values from 0.099609375 to 1.8984375
- gain_mlp: bfloat16 [1024], P('dp'), may hold values from 0.099609375 to 1.8984375
- cotangent: bfloat16 [4, 16, 2048, 1024], P(None, 'dp', None, 'tensor'), may hold values from -6 to 6
Outputs:
- output: bfloat16 [4, 16, 2048, 1024], P(None, 'dp', None, 'tensor')
- input_grad: bfloat16 [4, 16, 2048, 1024], P(None, 'dp', None, 'tensor')
- grad_query: float32 [1024, 1024], P('dp', 'tensor')
- grad_key: float32 [1024, 1024], P('dp', 'tensor')
- grad_value: float32 [1024, 1024], P('dp', 'tensor')
- grad_out: float32 [1024, 1024], P('tensor', 'dp')
- grad_up: float32 [1024, 4096], P('dp', 'tensor')
- grad_down: float32 [4096, 1024], P('tensor', 'dp')
- grad_route: float32 [1024], P('dp')
- grad_gain_attn: float32 [1024], P('dp')
- grad_gain_mlp: float32 [1024], P('dp')
The draws below stay inside these ranges and needn't reach their ends.
Inputs may be any that keep to these rules, and one draw needn't show every extreme that they name: Each row of routed holds 256 different positions of its sequence in rising order.
All inputs are finite; a program needn't handle non-finite values.
Results may differ from the reference program's by a relative error of at most 0.02.
Values may be sent and summed in bfloat16 or wider, within the bound.
A program may use at most 192 MiB of HBM per device.

```python
import math
import jax
import jax.numpy as jnp
from jax import lax

D = 1024
H = 16
HD = 64
FF = 4096
LEN = 2048
CAP = 256
MICRO = 4
SEQS = 16


def draw_tokens(key, part):
    base_key, row_key, col_key = jax.random.split(key, 3)
    shape = (MICRO, SEQS, LEN, D)
    row_scale = jnp.exp(jax.random.uniform(row_key, (MICRO, SEQS, LEN, 1), jnp.float32, math.log(0.3), math.log(3.0)))
    col_scale = jnp.exp(jax.random.uniform(col_key, (D,), jnp.float32, math.log(0.3), math.log(3.0)))
    base_draw = jnp.clip(jax.random.normal(base_key, shape, jnp.float32), -4.0, 4.0)
    return (base_draw * row_scale * col_scale).astype(jnp.bfloat16)


def draw_routed(key, part):
    row_keys = jax.random.split(key, MICRO * SEQS)

    def one_row(row_key):
        shuffled = jax.random.permutation(row_key, LEN)
        return jnp.sort(shuffled[:CAP])
    return jax.vmap(one_row)(row_keys).reshape(MICRO, SEQS, CAP).astype(jnp.int32)


def levels(own_key, shape, cuts, least, high):
    level = 1.0
    for dim, parts in cuts:
        steps = jax.random.uniform(jax.random.fold_in(jax.random.fold_in(own_key, 6), dim), (parts,), jnp.float32, least / len(cuts), high / len(cuts))
        level = level * jnp.repeat(jnp.exp(steps), shape[dim] // parts).reshape((-1,) + (1,) * (len(shape) - 1 - dim))
    return level


def bell_draw(stream_key, shape, spread, limit, pieces=(), held_as=jnp.bfloat16):
    level = levels(stream_key, shape, pieces, -0.22, 0.18) if pieces else 1.0
    drawn = jax.random.normal(stream_key, shape, jnp.float32) * spread * level
    return jnp.minimum(jnp.maximum(drawn, -limit), limit).astype(held_as)


def setup_inputs(seed: int = 0) -> dict:
    key_of = jax.random.split(jax.random.key(seed), 13)
    tokens = draw_tokens(jax.random.fold_in(key_of[12], 71), 0)
    routed = draw_routed(jax.random.fold_in(key_of[12], 71), 0)
    w_query = bell_draw(key_of[2], (D, D), D ** -0.5, 0.1875, ((0, 16), (1, 2)))
    w_key = bell_draw(key_of[3], (D, D), D ** -0.5, 0.1875, ((0, 16), (1, 2)))
    w_value = bell_draw(key_of[4], (D, D), D ** -0.5, 0.1875, ((0, 16), (1, 2)))
    w_out = bell_draw(key_of[5], (D, D), (D // 32) ** -0.5, 1.0, ((0, 2), (1, 16)))
    w_up = bell_draw(key_of[6], (D, FF), D ** -0.5, 0.1875, ((0, 16), (1, 2)))
    w_down = bell_draw(key_of[7], (FF, D), FF ** -0.5, 0.09375, ((0, 2), (1, 16)))
    w_route = bell_draw(key_of[8], (D,), (4 * D) ** -0.5, 0.09375, ((0, 16),))
    gain_attn = jnp.clip(1.0 + 0.18 * jax.random.normal(key_of[9], (D,), jnp.float32), 0.099609375, 1.8984375).astype(jnp.bfloat16)
    gain_mlp = jnp.clip(1.0 + 0.18 * jax.random.normal(key_of[10], (D,), jnp.float32), 0.099609375, 1.8984375).astype(jnp.bfloat16)
    cotangent = bell_draw(key_of[11], (MICRO, SEQS, LEN, D), 1.0, 6.0, ((1, 16), (3, 2)))
    return dict(tokens=tokens, routed=routed, w_query=w_query, w_key=w_key, w_value=w_value, w_out=w_out, w_up=w_up, w_down=w_down, w_route=w_route, gain_attn=gain_attn, gain_mlp=gain_mlp, cotangent=cotangent)


eps_norm = 1e-05

@jax.custom_vjp
def low(v):
    return lax.optimization_barrier(v.astype(jnp.bfloat16)).astype(jnp.float32)

@jax.custom_vjp
def low_back(v):
    return v

def low_keep(v):
    return (low(v), None)

def low_pass(kept, grad):
    return (grad,)

def back_keep(v):
    return (v, None)

def back_low(kept, grad):
    return (low(grad),)
low.defvjp(low_keep, low_pass)
low_back.defvjp(back_keep, back_low)

def matmul(left, right):
    return jnp.dot(left, right, precision=lax.Precision.HIGHEST, preferred_element_type=jnp.float32)

def rms_norm(values, gain):
    return values * lax.rsqrt(lax.optimization_barrier(jnp.mean(values * values, -1, keepdims=True)) + eps_norm) * gain

def routed_block(params, x_seq, chosen):
    w_query, w_key, w_value, w_out, w_up, w_down, w_route, gain_attn, gain_mlp = params
    capacity = chosen.shape[0]
    routed_rows = x_seq[chosen]
    route_gate = jax.nn.sigmoid(matmul(routed_rows, w_route))
    normed = low(rms_norm(routed_rows, gain_attn))
    queries = low(low_back(matmul(normed, w_query))).reshape(capacity, H, HD)
    key_rows = low(low_back(matmul(normed, w_key))).reshape(capacity, H, HD)
    value_rows = low(low_back(matmul(normed, w_value))).reshape(capacity, H, HD)
    causal = lax.broadcasted_iota(jnp.int32, (capacity, capacity), 0) >= lax.broadcasted_iota(jnp.int32, (capacity, capacity), 1)
    scores = low_back(jnp.einsum('qhd,khd->hqk', queries, key_rows, precision=lax.Precision.HIGHEST) * HD ** (-0.5))
    scores = jnp.where(causal[None], scores, -1e+30)
    attn_probs = jax.nn.softmax(scores, axis=-1)
    mixed_heads = jnp.einsum('hqk,khd->qhd', low(attn_probs), value_rows, precision=lax.Precision.HIGHEST)
    mixed_heads = low(low_back(mixed_heads)).reshape(capacity, D)
    attended = low_back(matmul(mixed_heads, w_out))
    hidden = routed_rows + attended
    normed2 = low(rms_norm(hidden, gain_mlp))
    up_proj = low_back(matmul(normed2, w_up))
    activated = low(jax.nn.gelu(up_proj))
    down_out = low_back(matmul(activated, w_down))
    branch = attended + down_out
    return x_seq.at[chosen].add(route_gate[:, None] * branch)

def reference(tokens, routed, w_query, w_key, w_value, w_out, w_up, w_down, w_route, gain_attn, gain_mlp, cotangent):
    params = tuple((weight.astype(jnp.float32) for weight in (w_query, w_key, w_value, w_out, w_up, w_down, w_route, gain_attn, gain_mlp)))
    flat_tokens = tokens.astype(jnp.float32).reshape(MICRO * SEQS, LEN, D)
    flat_routed = routed.reshape(MICRO * SEQS, CAP).astype(jnp.int32)
    step_fn = jax.checkpoint(routed_block)

    def forward(weights, inputs):
        return lax.map(lambda pair: step_fn(weights, pair[0], pair[1]), (inputs, flat_routed))
    result, pullback = jax.vjp(forward, params, flat_tokens)
    param_grads, token_grads = pullback(cotangent.astype(jnp.float32).reshape(MICRO * SEQS, LEN, D))
    output = result.astype(jnp.bfloat16).reshape(MICRO, SEQS, LEN, D)
    input_grad = token_grads.astype(jnp.bfloat16).reshape(MICRO, SEQS, LEN, D)
    return (output, input_grad, param_grads[0], param_grads[1], param_grads[2], param_grads[3], param_grads[4], param_grads[5], param_grads[6], param_grads[7], param_grads[8])
```

```python
import jax
import jax.numpy as jnp
from jax import lax
from jax.sharding import PartitionSpec as P

HD = 64
eps_norm = 1e-05


def dense(left, right):
    return jnp.dot(left, right, preferred_element_type=jnp.float32)


def dense_t(left, right):
    return lax.dot_general(
        left, right, (((1,), (1,)), ((), ())), preferred_element_type=jnp.float32
    )


def dense_g(left, right):
    return lax.dot_general(
        left, right, (((0,), (0,)), ((), ())), preferred_element_type=jnp.float32
    )


def rms_back(values, inv, gain, grad):
    grad_gain = jnp.sum(grad * values * inv, 0)
    scaled = grad * gain
    dot = jnp.mean(scaled * values, -1, keepdims=True)
    return inv * scaled - values * (inv * inv * inv) * dot, grad_gain


def shards(
    tokens,
    routed,
    w_query,
    w_key,
    w_value,
    w_out,
    w_up,
    w_down,
    w_route,
    gain_attn,
    gain_mlp,
    cotangent,
):
    micro, seqs, length, half_width = tokens.shape
    capacity = routed.shape[2]
    batch = micro * seqs
    total = batch * capacity
    cols = w_query.shape[1]
    hidden_cols = w_up.shape[1]
    width = half_width * lax.axis_size("tensor")
    offset = lax.axis_index("tensor") * half_width
    scale = HD ** (-0.5)
    swap = [(0, 1), (1, 0)]

    vec = jnp.stack([w_route, gain_attn, gain_mlp], 1)
    vec = jnp.pad(vec, ((0, 0), (0, 125)))
    packed = jnp.concatenate([w_query, w_key, w_value, w_up, w_out.T, w_down.T, vec], 1)
    gathered = lax.all_gather(packed, "dp", axis=0, tiled=True)
    b1, b2, b3 = cols, 2 * cols, 3 * cols
    b4 = b3 + hidden_cols
    b5 = b4 + w_out.shape[0]
    b6 = b5 + w_down.shape[0]
    fq = gathered[:, :b1]
    fk = gathered[:, b1:b2]
    fv = gathered[:, b2:b3]
    fup = gathered[:, b3:b4]
    foutT = gathered[:, b4:b5]
    fdownT = gathered[:, b5:b6]
    route = gathered[:, b6]
    route_f32 = route.astype(jnp.float32)
    gain1 = gathered[:, b6 + 1].astype(jnp.float32)
    gain2 = gathered[:, b6 + 2].astype(jnp.float32)

    tok = tokens.reshape(batch, length, half_width)
    cot = cotangent.reshape(batch, length, half_width)
    chosen = routed.reshape(batch, capacity)
    rows_half = jnp.take_along_axis(tok, chosen[:, :, None], axis=1).reshape(total, half_width)
    cot_half = jnp.take_along_axis(cot, chosen[:, :, None], axis=1).reshape(total, half_width)
    rows = lax.all_gather(rows_half, "tensor", axis=1, tiled=True)
    cot_rows = lax.all_gather(cot_half, "tensor", axis=1, tiled=True)

    rows_f = rows.astype(jnp.float32)
    cot_f = cot_rows.astype(jnp.float32)
    gate = jax.nn.sigmoid(dense(rows, route))
    inv1 = lax.rsqrt(jnp.mean(rows_f * rows_f, -1, keepdims=True) + eps_norm)
    normed = (rows_f * inv1 * gain1).astype(jnp.bfloat16)
    heads = cols // HD

    def split(x):
        return x.astype(jnp.bfloat16).reshape(batch, capacity, heads, HD).transpose(0, 2, 1, 3)

    def join(x):
        return x.transpose(0, 2, 1, 3).reshape(total, cols)

    q = split(dense(normed, fq))
    k = split(dense(normed, fk))
    v = split(dense(normed, fv))
    causal = lax.broadcasted_iota(jnp.int32, (capacity, capacity), 0) >= lax.broadcasted_iota(
        jnp.int32, (capacity, capacity), 1
    )
    scores = jnp.einsum("bhqd,bhkd->bhqk", q, k, preferred_element_type=jnp.float32) * scale
    scores = jnp.where(causal, scores, -1e30)
    peak = jnp.max(scores, -1, keepdims=True)
    expd = jnp.exp(scores - peak)
    probs = expd / jnp.sum(expd, -1, keepdims=True)
    probs_low = probs.astype(jnp.bfloat16)
    mixed = jnp.einsum("bhqk,bhkd->bhqd", probs_low, v, preferred_element_type=jnp.float32)
    mixed = join(mixed.astype(jnp.bfloat16))

    def pair_sum(x):
        low = x.astype(jnp.bfloat16)
        other = lax.ppermute(low, "tensor", swap)
        return low.astype(jnp.float32) + other.astype(jnp.float32)

    attended = pair_sum(dense_t(mixed, foutT))
    hidden = rows_f + attended
    inv2 = lax.rsqrt(jnp.mean(hidden * hidden, -1, keepdims=True) + eps_norm)
    normed2 = (hidden * inv2 * gain2).astype(jnp.bfloat16)
    up = dense(normed2, fup)
    act32, gelu_back = jax.vjp(jax.nn.gelu, up)
    act = act32.astype(jnp.bfloat16)
    down = pair_sum(dense_t(act, fdownT))
    branch = attended + down
    d_logit = jnp.sum(cot_f * branch, -1) * gate * (1.0 - gate)
    branch_half = lax.dynamic_slice_in_dim(branch, offset, half_width, 1)
    new_rows = (rows_half.astype(jnp.float32) + gate[:, None] * branch_half).astype(jnp.bfloat16)

    d_branch = gate[:, None] * cot_f
    d_down = d_branch.astype(jnp.bfloat16)
    g_downT = dense_g(d_down, act)
    d_act = dense(d_down, fdownT)
    d_upper = gelu_back(d_act)[0].astype(jnp.bfloat16)
    g_up = dense_g(normed2, d_upper)
    d_normed2 = pair_sum(dense_t(d_upper, fup))
    d_hidden, g_gain2 = rms_back(hidden, inv2, gain2, d_normed2)
    d_attended = (d_branch + d_hidden).astype(jnp.bfloat16)
    g_outT = dense_g(d_attended, mixed)
    d_mixed = split(dense(d_attended, foutT))
    d_values = jnp.einsum("bhqk,bhqd->bhkd", probs_low, d_mixed, preferred_element_type=jnp.float32)
    d_values = join(d_values.astype(jnp.bfloat16))
    d_probs = jnp.einsum("bhqd,bhkd->bhqk", d_mixed, v, preferred_element_type=jnp.float32)
    d_scores = probs * (d_probs - jnp.sum(d_probs * probs, -1, keepdims=True))
    d_scores = d_scores.astype(jnp.bfloat16)
    d_q = jnp.einsum("bhqk,bhkd->bhqd", d_scores, k, preferred_element_type=jnp.float32) * scale
    d_k = jnp.einsum("bhqk,bhqd->bhkd", d_scores, q, preferred_element_type=jnp.float32) * scale
    d_q = join(d_q.astype(jnp.bfloat16))
    d_k = join(d_k.astype(jnp.bfloat16))
    g_q = dense_g(normed, d_q)
    g_k = dense_g(normed, d_k)
    g_v = dense_g(normed, d_values)
    d_normed = pair_sum(dense_t(d_q, fq) + dense_t(d_k, fk) + dense_t(d_values, fv))
    d_rows, g_gain1 = rms_back(rows_f, inv1, gain1, d_normed)
    g_route = jnp.sum(rows_f * d_logit[:, None], 0)
    d_half = (
        lax.dynamic_slice_in_dim(d_hidden + d_rows, offset, half_width, 1)
        + d_logit[:, None] * lax.dynamic_slice_in_dim(route_f32, offset, half_width, 0)[None, :]
    )
    grad_rows = (cot_half.astype(jnp.float32) + d_half).astype(jnp.bfloat16)

    seq_ids = lax.broadcasted_iota(jnp.int32, (batch, capacity), 0)
    output = tok.at[seq_ids, chosen].set(
        new_rows.reshape(batch, capacity, half_width), unique_indices=True
    )
    input_grad = cot.at[seq_ids, chosen].set(
        grad_rows.reshape(batch, capacity, half_width), unique_indices=True
    )

    g_vec = jnp.pad(jnp.stack([g_route, g_gain1, g_gain2], 1), ((0, 0), (0, 125)))
    grads = jnp.concatenate(
        [x.astype(jnp.bfloat16) for x in (g_q, g_k, g_v, g_up, g_outT, g_downT, g_vec)], 1
    )
    own = lax.psum_scatter(grads, "dp", scatter_dimension=0, tiled=True).astype(jnp.float32)
    return (
        output.reshape(tokens.shape),
        input_grad.reshape(tokens.shape),
        own[:, :b1],
        own[:, b1:b2],
        own[:, b2:b3],
        own[:, b4:b5].T,
        own[:, b3:b4],
        own[:, b5:b6].T,
        own[:, b6],
        own[:, b6 + 1],
        own[:, b6 + 2],
    )


def solution(mesh):
    rows = P("dp", "tensor")
    columns = P("tensor", "dp")
    vector = P("dp")
    stored = P(None, "dp", None, "tensor")
    return jax.shard_map(
        shards,
        mesh=mesh,
        in_specs=(
            stored,
            P(None, "dp", None),
            rows,
            rows,
            rows,
            columns,
            rows,
            columns,
            vector,
            vector,
            vector,
            stored,
        ),
        out_specs=(
            stored,
            stored,
            rows,
            rows,
            rows,
            columns,
            rows,
            columns,
            vector,
            vector,
            vector,
        ),
        check_vma=False,
    )
```

```python
import jax
import jax.numpy as jnp
from jax import lax
from jax.sharding import PartitionSpec as P
from jax.experimental import pallas as pl
from jax.experimental.pallas import tpu as pltpu

MESH = pl.DeviceIdType.MESH
NB = 48
PATTERN = "XYZXYXYZ"
LAGS = (0, 3, 6, 9, 12, 15)

class Place:
    def __init__(self):
        me = lax.axis_index("dp")
        self.x = me % 2
        self.y = (me // 2) % 2
        self.z = me // 4
        self.nx = me + 1 - 2 * self.x
        self.ny = me + 2 - 4 * self.y
        self.up = me + 4
        self.dn = me - 4

def barrier(p, core=False):
    bar = pltpu.get_barrier_semaphore()
    def sig(d):
        pl.semaphore_signal(bar, inc=1, device_id=d, device_id_type=MESH)
    sig({"dp": p.nx}); sig({"dp": p.ny})
    if core: sig({"tensor": 1 - lax.axis_index("tensor")})
    @pl.when(p.z < 3)
    def _(): sig({"dp": p.up})
    @pl.when(p.z > 0)
    def _(): sig({"dp": p.dn})
    inner = jnp.logical_and(p.z > 0, p.z < 3)
    base = 3 if core else 2
    @pl.when(inner)
    def _(): pl.semaphore_wait(bar, base + 2)
    @pl.when(jnp.logical_not(inner))
    def _(): pl.semaphore_wait(bar, base + 1)

def both(a, b): return jnp.logical_and(a, b)

class Gather:
    def __init__(self, p, W, ss, rs):
        self.p, self.W, self.ss, self.rs = p, W, ss, rs
    def copy(self, ref, b, k, dev):
        return pltpu.make_async_remote_copy(ref, ref, self.ss.at[b, k], self.rs.at[b, k], device_id={"dp": dev}, device_id_type=MESH)
    def zref(self, b, c, zz):
        p = self.p
        zz = jnp.clip(zz, 0, 3)
        return self.W.at[b, zz] if c == "Z" else self.W.at[b, zz, p.y, p.x]
    def zsend(self, b, c, hop, act):
        p = self.p
        @pl.when(both(p.z - hop + 1 >= 0, p.z < 3))
        def _(): act(self.copy(self.zref(b, c, p.z - hop + 1), b, hop - 1, jnp.minimum(p.up, 15)))
        @pl.when(both(p.z + hop - 1 <= 3, p.z > 0))
        def _(): act(self.copy(self.zref(b, c, p.z + hop - 1), b, 2 + hop, jnp.maximum(p.dn, 0)))
    def zrecv(self, b, c, hop):
        p = self.p
        @pl.when(p.z - hop >= 0)
        def _(): self.copy(self.zref(b, c, p.z - hop), b, hop - 1, p.nx).wait_recv()
        @pl.when(p.z + hop <= 3)
        def _(): self.copy(self.zref(b, c, p.z + hop), b, 2 + hop, p.nx).wait_recv()
    def stage(self, b, c, j):
        p, W = self.p, self.W
        x, y, z = p.x, p.y, p.z
        if c == "X":
            seq = ["z1", "z2", "z3", ("y", W.at[b, :, y, x], W.at[b, :, 1 - y, x]), ("x", W.at[b, :, :, x], W.at[b, :, :, 1 - x])]
        elif c == "Y":
            seq = ["z1", "z2", "z3", ("x", W.at[b, :, y, x], W.at[b, :, y, 1 - x]), ("y", W.at[b, :, y], W.at[b, :, 1 - y])]
        else:
            seq = [("x", W.at[b, z, y, x], W.at[b, z, y, 1 - x]), ("y", W.at[b, z, y], W.at[b, z, 1 - y]), "z1", "z2", "z3"]
        return seq[j]
    def send(self, b, c, j, act=lambda d: d.start()):
        st = self.stage(b, c, j)
        if isinstance(st, str): self.zsend(b, c, int(st[1]), act)
        else:
            kind, dev = (6, self.p.ny) if st[0] == "y" else (7, self.p.nx)
            act(self.copy(st[1], b, kind, dev))
    def recv(self, b, c, j):
        st = self.stage(b, c, j)
        if isinstance(st, str): self.zrecv(b, c, int(st[1]))
        else:
            kind, dev = (6, self.p.ny) if st[0] == "y" else (7, self.p.nx)
            self.copy(st[2], b, kind, dev).wait_recv()
    def step(self, s, pos, static=None):
        for j in (5, 4, 3, 2, 1, 0):
            if static is not None and not (0 <= static - LAGS[j] < NB): continue
            b = s - LAGS[j]
            c = PATTERN[(pos - LAGS[j]) % 8]
            if j > 0: self.recv(b, c, j - 1)
            if j < 5: self.send(b, c, j)
    def drain(self):
        def body(r, _):
            for pos in range(8):
                for j in range(5):
                    self.send(r * 8 + pos, PATTERN[pos], j, act=lambda d: d.wait_send())
            return 0
        lax.fori_loop(0, NB // 8, body, 0)

class Scatter:
    def __init__(self, p, G, out, L8, L4, LZ, P4, P2, P1, ss, rs):
        self.p, self.G, self.out, self.ss, self.rs = p, G, out, ss, rs
        self.L8, self.L4, self.LZ, self.P4, self.P2, self.P1 = L8, L4, LZ, P4, P2, P1
    def slot(self, b, bp):
        r = b // 8
        c = PATTERN[bp]
        if c == "Z": return r * 2 + {2: 0, 7: 1}[bp]
        return r * 6 + {0: 0, 1: 1, 3: 2, 4: 3, 5: 4, 6: 5}[bp]
    def copy(self, src, dst, b, k, dev):
        return pltpu.make_async_remote_copy(src, dst, self.ss.at[b, k], self.rs.at[b, k], device_id={"dp": dev}, device_id_type=MESH)
    def gz(self, b, c, t):
        t = jnp.clip(t, 0, 3)
        return self.G.at[b, t] if c == "Z" else self.G.at[b, t, self.p.y, self.p.x]
    def lz(self, b, bp, k):
        i = self.slot(b, bp)
        return self.P4.at[i, k] if PATTERN[bp] == "Z" else self.LZ.at[i, k]
    def add(self, ref, land):
        ref[...] = (ref[...].astype(jnp.float32) + land[...].astype(jnp.float32)).astype(ref.dtype)
    def zsend(self, b, bp, hop, act):
        p, c = self.p, PATTERN[bp]
        @pl.when(both(p.z + hop <= 3, p.z < 3))
        def _(): act(self.copy(self.gz(b, c, p.z + hop), self.lz(b, bp, hop - 1), b, hop - 1, jnp.minimum(p.up, 15)))
        @pl.when(both(p.z - hop >= 0, p.z > 0))
        def _(): act(self.copy(self.gz(b, c, p.z - hop), self.lz(b, bp, 2 + hop), b, 2 + hop, jnp.maximum(p.dn, 0)))
    def zrecv(self, b, bp, hop, final):
        p, c = self.p, PATTERN[bp]
        def take(k, t):
            land = self.lz(b, bp, k)
            self.copy(land, land, b, k, p.nx).wait_recv()
            if not final: self.add(self.gz(b, c, t), land)
        lo = both(p.z >= 1, p.z - 1 + hop <= 3)
        hi = both(p.z <= 2, p.z + 1 - hop >= 0)
        if not final:
            @pl.when(lo)
            def _(): take(hop - 1, p.z - 1 + hop)
            @pl.when(hi)
            def _(): take(2 + hop, p.z + 1 - hop)
        else:
            own = self.G.at[b, p.z, p.y, p.x]
            a, d = self.lz(b, bp, 0), self.lz(b, bp, 3)
            f32 = jnp.float32
            @pl.when(p.z == 0)
            def _():
                take(3, p.z)
                self.out[b] = own[...].astype(f32) + d[...].astype(f32)
            @pl.when(p.z == 3)
            def _():
                take(0, p.z)
                self.out[b] = own[...].astype(f32) + a[...].astype(f32)
            @pl.when(both(p.z > 0, p.z < 3))
            def _():
                take(0, p.z); take(3, p.z)
                self.out[b] = own[...].astype(f32) + a[...].astype(f32) + d[...].astype(f32)
    def stage(self, b, bp, j):
        p, G = self.p, self.G
        x, y, z = p.x, p.y, p.z
        c = PATTERN[bp]; i = self.slot(b, bp)
        if c == "X":
            return [("x", G.at[b, :, :, 1 - x], self.L8.at[i], G.at[b, :, :, x]), ("y", G.at[b, :, 1 - y, x], self.L4.at[i], G.at[b, :, y, x]), "z3", "z2", "z1"][j]
        if c == "Y":
            return [("y", G.at[b, :, 1 - y], self.L8.at[i], G.at[b, :, y]), ("x", G.at[b, :, y, 1 - x], self.L4.at[i], G.at[b, :, y, x]), "z3", "z2", "z1"][j]
        return ["z3", "z2", "z1", ("y", G.at[b, z, 1 - y], self.P2.at[i], G.at[b, z, y]), ("x", G.at[b, z, y, 1 - x], self.P1.at[i], G.at[b, z, y, x])][j]
    def send(self, b, bp, j, act=lambda d: d.start()):
        st = self.stage(b, bp, j)
        if isinstance(st, str): self.zsend(b, bp, int(st[1]), act)
        else:
            kind, dev = (6, self.p.ny) if st[0] == "y" else (7, self.p.nx)
            act(self.copy(st[1], st[2], b, kind, dev))
    def recv(self, b, bp, j):
        st = self.stage(b, bp, j)
        if isinstance(st, str): self.zrecv(b, bp, int(st[1]), PATTERN[bp] != "Z" and j == 4)
        else:
            kind, dev = (6, self.p.ny) if st[0] == "y" else (7, self.p.nx)
            self.copy(st[2], st[2], b, kind, dev).wait_recv()
            if j == 4: self.out[b] = st[3][...].astype(jnp.float32) + st[2][...].astype(jnp.float32)
            else: self.add(st[3], st[2])
    def step(self, s, pos, static=None, nb=NB):
        live = [j for j in (5, 4, 3, 2, 1, 0) if static is None or 0 <= static - LAGS[j] < nb]
        for j in live:
            if j > 0: self.recv(s - LAGS[j], (pos - LAGS[j]) % 8, j - 1)
        for j in live:
            if j < 5: self.send(s - LAGS[j], (pos - LAGS[j]) % 8, j)
    def drain(self):
        def body(r, _):
            for pos in range(8):
                for j in range(5):
                    self.send(r * 8 + pos, pos, j, act=lambda d: d.wait_send())
            return 0
        lax.fori_loop(0, NB // 8, body, 0)
    @staticmethod
    def scratch():
        bf = jnp.bfloat16
        nx, nz = NB // 8 * 6, NB // 8 * 2
        return [pltpu.VMEM((nx, 4, 2, 64, 128), bf), pltpu.VMEM((nx, 4, 64, 128), bf), pltpu.VMEM((nx, 6, 64, 128), bf),
                pltpu.VMEM((nz, 6, 2, 2, 64, 128), bf), pltpu.VMEM((nz, 2, 64, 128), bf), pltpu.VMEM((nz, 64, 128), bf),
                pltpu.SemaphoreType.DMA((NB, 8)), pltpu.SemaphoreType.DMA((NB, 8))]


def run_steps(steps):
    for s in range(16):
        steps.step(s, s % 8, static=s)

    def body(r, _):
        for pos in range(8):
            steps.step(r * 8 + pos, pos)
        return 0

    lax.fori_loop(2, NB // 8, body, 0)
    for s in range(NB, NB + LAGS[5] + 1):
        steps.step(s, s % 8, static=s)
    steps.drain()


def gather_kernel(w_ref, o_ref, W, ss, rs, ls):
    p = Place()
    first = pltpu.make_async_copy(w_ref, W.at[:, p.z, p.y, p.x], ls.at[0])
    first.start()
    barrier(p)
    first.wait()
    run_steps(Gather(p, W, ss, rs))
    last = pltpu.make_async_copy(W, o_ref, ls.at[0])
    last.start()
    last.wait()


def scatter_kernel(g_ref, o_ref, G, ls, *rest):
    p = Place()
    first = pltpu.make_async_copy(g_ref, G, ls.at[0])
    first.start()
    barrier(p)
    first.wait()
    run_steps(Scatter(p, G, o_ref, *rest))


def gather_blocks(packed):
    if lax.axis_size("dp") != 16:
        return lax.all_gather(packed, "dp", axis=1, tiled=True)
    out = pl.pallas_call(
        gather_kernel,
        out_shape=jax.ShapeDtypeStruct((NB, 4, 2, 2, 64, 128), jnp.bfloat16),
        in_specs=[pl.BlockSpec(memory_space=pl.ANY)],
        out_specs=pl.BlockSpec(memory_space=pl.ANY),
        scratch_shapes=[
            pltpu.VMEM((NB, 4, 2, 2, 64, 128), jnp.bfloat16),
            pltpu.SemaphoreType.DMA((NB, 8)),
            pltpu.SemaphoreType.DMA((NB, 8)),
            pltpu.SemaphoreType.DMA((1,)),
        ],
        compiler_params=pltpu.CompilerParams(
            collective_id=1, has_side_effects=True, vmem_limit_bytes=60 * 1024 * 1024
        ),
        name="gather_weights",
    )(packed)
    return out.reshape(NB, 1024, 128)


def scatter_blocks(grads):
    if lax.axis_size("dp") != 16:
        return lax.psum_scatter(grads, "dp", scatter_dimension=1, tiled=True).astype(jnp.float32)
    return pl.pallas_call(
        scatter_kernel,
        out_shape=jax.ShapeDtypeStruct((NB, 64, 128), jnp.float32),
        in_specs=[pl.BlockSpec(memory_space=pl.ANY)],
        out_specs=pl.BlockSpec(memory_space=pltpu.VMEM),
        scratch_shapes=[
            pltpu.VMEM((NB, 4, 2, 2, 64, 128), jnp.bfloat16),
            pltpu.SemaphoreType.DMA((1,)),
        ]
        + Scatter.scratch(),
        compiler_params=pltpu.CompilerParams(
            collective_id=2, has_side_effects=True, vmem_limit_bytes=63 * 1024 * 1024
        ),
        name="scatter_grads",
    )(grads.reshape(NB, 4, 2, 2, 64, 128))


def to_blocks(x):
    rows, cols = x.shape
    return x.reshape(rows, cols // 128, 128).transpose(1, 0, 2)


def from_blocks(x):
    return x.transpose(1, 0, 2).reshape(x.shape[1], -1)


HD = 64
eps_norm = 1e-05


def dense(left, right):
    return jnp.dot(left, right, preferred_element_type=jnp.float32)


def dense_t(left, right):
    return lax.dot_general(
        left, right, (((1,), (1,)), ((), ())), preferred_element_type=jnp.float32
    )


def dense_g(left, right):
    return lax.dot_general(
        left, right, (((0,), (0,)), ((), ())), preferred_element_type=jnp.float32
    )


def rms_back(values, inv, gain, grad):
    grad_gain = jnp.sum(grad * values * inv, 0)
    scaled = grad * gain
    dot = jnp.mean(scaled * values, -1, keepdims=True)
    return inv * scaled - values * (inv * inv * inv) * dot, grad_gain


def shards(
    tokens,
    routed,
    w_query,
    w_key,
    w_value,
    w_out,
    w_up,
    w_down,
    w_route,
    gain_attn,
    gain_mlp,
    cotangent,
):
    micro, seqs, length, half_width = tokens.shape
    capacity = routed.shape[2]
    batch = micro * seqs
    total = batch * capacity
    cols = w_query.shape[1]
    hidden_cols = w_up.shape[1]
    width = half_width * lax.axis_size("tensor")
    offset = lax.axis_index("tensor") * half_width
    scale = HD ** (-0.5)
    swap = [(0, 1), (1, 0)]

    vec = jnp.stack([w_route, gain_attn, gain_mlp], 0)
    vec = lax.all_gather(vec, "dp", axis=1, tiled=True)
    route = vec[0]
    route_f32 = route.astype(jnp.float32)
    gain1 = vec[1].astype(jnp.float32)
    gain2 = vec[2].astype(jnp.float32)
    mlp = jnp.concatenate(
        [
            to_blocks(w_up).reshape(8, 2, -1, 128),
            to_blocks(w_down.T).reshape(8, 2, -1, 128),
        ],
        1,
    ).reshape(32, -1, 128)
    packed = jnp.concatenate([to_blocks(x) for x in (w_query, w_key, w_value, w_out.T)] + [mlp])
    blocks = gather_blocks(packed)
    fq, fk, fv, foutT = [from_blocks(blocks[4 * i : 4 * i + 4]) for i in range(4)]
    mlp = blocks[16:].reshape(8, 2, 2, -1, 128)
    fup = from_blocks(mlp[:, 0].reshape(16, -1, 128))
    fdownT = from_blocks(mlp[:, 1].reshape(16, -1, 128))

    tok = tokens.reshape(batch, length, half_width)
    cot = cotangent.reshape(batch, length, half_width)
    chosen = routed.reshape(batch, capacity)
    rows_half = jnp.take_along_axis(tok, chosen[:, :, None], axis=1).reshape(total, half_width)
    cot_half = jnp.take_along_axis(cot, chosen[:, :, None], axis=1).reshape(total, half_width)
    rows = lax.all_gather(rows_half, "tensor", axis=1, tiled=True)
    cot_rows = lax.all_gather(cot_half, "tensor", axis=1, tiled=True)

    rows_f = rows.astype(jnp.float32)
    cot_f = cot_rows.astype(jnp.float32)
    gate = jax.nn.sigmoid(dense(rows, route))
    inv1 = lax.rsqrt(jnp.mean(rows_f * rows_f, -1, keepdims=True) + eps_norm)
    normed = (rows_f * inv1 * gain1).astype(jnp.bfloat16)
    heads = cols // HD

    def split(x):
        return x.astype(jnp.bfloat16).reshape(batch, capacity, heads, HD).transpose(0, 2, 1, 3)

    def join(x):
        return x.transpose(0, 2, 1, 3).reshape(total, cols)

    q = split(dense(normed, fq))
    k = split(dense(normed, fk))
    v = split(dense(normed, fv))
    causal = lax.broadcasted_iota(jnp.int32, (capacity, capacity), 0) >= lax.broadcasted_iota(
        jnp.int32, (capacity, capacity), 1
    )
    scores = jnp.einsum("bhqd,bhkd->bhqk", q, k, preferred_element_type=jnp.float32) * scale
    scores = jnp.where(causal, scores, -1e30)
    peak = jnp.max(scores, -1, keepdims=True)
    expd = jnp.exp(scores - peak)
    probs = expd / jnp.sum(expd, -1, keepdims=True)
    probs_low = probs.astype(jnp.bfloat16)
    mixed = jnp.einsum("bhqk,bhkd->bhqd", probs_low, v, preferred_element_type=jnp.float32)
    mixed = join(mixed.astype(jnp.bfloat16))

    def pair_sum(x):
        low = x.astype(jnp.bfloat16)
        other = lax.ppermute(low, "tensor", swap)
        return low.astype(jnp.float32) + other.astype(jnp.float32)

    attended = pair_sum(dense_t(mixed, foutT))
    hidden = rows_f + attended
    inv2 = lax.rsqrt(jnp.mean(hidden * hidden, -1, keepdims=True) + eps_norm)
    normed2 = (hidden * inv2 * gain2).astype(jnp.bfloat16)
    up = dense(normed2, fup)
    act32, gelu_back = jax.vjp(jax.nn.gelu, up)
    act = act32.astype(jnp.bfloat16)
    down = pair_sum(dense_t(act, fdownT))
    branch = attended + down
    d_logit = jnp.sum(cot_f * branch, -1) * gate * (1.0 - gate)
    branch_half = lax.dynamic_slice_in_dim(branch, offset, half_width, 1)
    new_rows = (rows_half.astype(jnp.float32) + gate[:, None] * branch_half).astype(jnp.bfloat16)

    d_branch = gate[:, None] * cot_f
    d_down = d_branch.astype(jnp.bfloat16)
    g_downT = dense_g(d_down, act)
    d_act = dense(d_down, fdownT)
    d_upper = gelu_back(d_act)[0].astype(jnp.bfloat16)
    g_up = dense_g(normed2, d_upper)
    d_normed2 = pair_sum(dense_t(d_upper, fup))
    d_hidden, g_gain2 = rms_back(hidden, inv2, gain2, d_normed2)
    d_attended = (d_branch + d_hidden).astype(jnp.bfloat16)
    g_outT = dense_g(d_attended, mixed)
    d_mixed = split(dense(d_attended, foutT))
    d_values = jnp.einsum("bhqk,bhqd->bhkd", probs_low, d_mixed, preferred_element_type=jnp.float32)
    d_values = join(d_values.astype(jnp.bfloat16))
    d_probs = jnp.einsum("bhqd,bhkd->bhqk", d_mixed, v, preferred_element_type=jnp.float32)
    d_scores = probs * (d_probs - jnp.sum(d_probs * probs, -1, keepdims=True))
    d_scores = d_scores.astype(jnp.bfloat16)
    d_q = jnp.einsum("bhqk,bhkd->bhqd", d_scores, k, preferred_element_type=jnp.float32) * scale
    d_k = jnp.einsum("bhqk,bhqd->bhkd", d_scores, q, preferred_element_type=jnp.float32) * scale
    d_q = join(d_q.astype(jnp.bfloat16))
    d_k = join(d_k.astype(jnp.bfloat16))
    g_q = dense_g(normed, d_q)
    g_k = dense_g(normed, d_k)
    g_v = dense_g(normed, d_values)
    d_normed = pair_sum(dense_t(d_q, fq) + dense_t(d_k, fk) + dense_t(d_values, fv))
    d_rows, g_gain1 = rms_back(rows_f, inv1, gain1, d_normed)
    g_route = jnp.sum(rows_f * d_logit[:, None], 0)
    d_half = (
        lax.dynamic_slice_in_dim(d_hidden + d_rows, offset, half_width, 1)
        + d_logit[:, None] * lax.dynamic_slice_in_dim(route_f32, offset, half_width, 0)[None, :]
    )
    grad_rows = (cot_half.astype(jnp.float32) + d_half).astype(jnp.bfloat16)

    seq_ids = lax.broadcasted_iota(jnp.int32, (batch, capacity), 0)
    output = tok.at[seq_ids, chosen].set(
        new_rows.reshape(batch, capacity, half_width), unique_indices=True
    )
    input_grad = cot.at[seq_ids, chosen].set(
        grad_rows.reshape(batch, capacity, half_width), unique_indices=True
    )

    g_vec = lax.psum_scatter(
        jnp.stack([g_route, g_gain1, g_gain2], 0), "dp", scatter_dimension=1, tiled=True
    )
    low = [to_blocks(x.astype(jnp.bfloat16)) for x in (g_q, g_k, g_v, g_outT, g_up, g_downT)]
    mlp = jnp.concatenate([x.reshape(8, 2, -1, 128) for x in low[4:]], 1).reshape(32, -1, 128)
    own = scatter_blocks(jnp.concatenate(low[:4] + [mlp]))
    o_q, o_k, o_v, o_out = [from_blocks(own[4 * i : 4 * i + 4]) for i in range(4)]
    mlp = own[16:].reshape(8, 2, 2, -1, 128)
    o_up = from_blocks(mlp[:, 0].reshape(16, -1, 128))
    o_down = from_blocks(mlp[:, 1].reshape(16, -1, 128))
    return (
        output.reshape(tokens.shape),
        input_grad.reshape(tokens.shape),
        o_q,
        o_k,
        o_v,
        o_out.T,
        o_up,
        o_down.T,
        g_vec[0],
        g_vec[1],
        g_vec[2],
    )


def solution(mesh):
    rows = P("dp", "tensor")
    columns = P("tensor", "dp")
    vector = P("dp")
    stored = P(None, "dp", None, "tensor")
    return jax.shard_map(
        shards,
        mesh=mesh,
        in_specs=(
            stored,
            P(None, "dp", None),
            rows,
            rows,
            rows,
            columns,
            rows,
            columns,
            vector,
            vector,
            vector,
            stored,
        ),
        out_specs=(
            stored,
            stored,
            rows,
            rows,
            rows,
            columns,
            rows,
            columns,
            vector,
            vector,
            vector,
        ),
        check_vma=False,
    )
```

```python
import jax
import jax.numpy as jnp
from jax import lax
from jax.experimental import pallas as pl
from jax.experimental.pallas import tpu as pltpu
from jax.sharding import PartitionSpec as P

HD = 64
eps_norm = 1e-05


def dense(left, right):
    return jnp.dot(left, right, preferred_element_type=jnp.float32)


def dense_t(left, right):
    return lax.dot_general(
        left, right, (((1,), (1,)), ((), ())), preferred_element_type=jnp.float32
    )


def dense_g(left, right):
    return lax.dot_general(
        left, right, (((0,), (0,)), ((), ())), preferred_element_type=jnp.float32
    )


def rms_back(values, inv, gain, grad):
    grad_gain = jnp.sum(grad * values * inv, 0)
    scaled = grad * gain
    dot = jnp.mean(scaled * values, -1, keepdims=True)
    return inv * scaled - values * (inv * inv * inv) * dot, grad_gain


def plain(
    tokens,
    routed,
    w_query,
    w_key,
    w_value,
    w_out,
    w_up,
    w_down,
    w_route,
    gain_attn,
    gain_mlp,
    cotangent,
):
    micro, seqs, length, half_width = tokens.shape
    capacity = routed.shape[2]
    batch = micro * seqs
    total = batch * capacity
    cols = w_query.shape[1]
    hidden_cols = w_up.shape[1]
    width = half_width * lax.axis_size("tensor")
    offset = lax.axis_index("tensor") * half_width
    scale = HD ** (-0.5)
    swap = [(0, 1), (1, 0)]

    vec = jnp.stack([w_route, gain_attn, gain_mlp], 1)
    vec = jnp.pad(vec, ((0, 0), (0, 125)))
    packed = jnp.concatenate([w_query, w_key, w_value, w_up, w_out.T, w_down.T, vec], 1)
    gathered = lax.all_gather(packed, "dp", axis=0, tiled=True)
    b1, b2, b3 = cols, 2 * cols, 3 * cols
    b4 = b3 + hidden_cols
    b5 = b4 + w_out.shape[0]
    b6 = b5 + w_down.shape[0]
    fq = gathered[:, :b1]
    fk = gathered[:, b1:b2]
    fv = gathered[:, b2:b3]
    fup = gathered[:, b3:b4]
    foutT = gathered[:, b4:b5]
    fdownT = gathered[:, b5:b6]
    route = gathered[:, b6]
    route_f32 = route.astype(jnp.float32)
    gain1 = gathered[:, b6 + 1].astype(jnp.float32)
    gain2 = gathered[:, b6 + 2].astype(jnp.float32)

    tok = tokens.reshape(batch, length, half_width)
    cot = cotangent.reshape(batch, length, half_width)
    chosen = routed.reshape(batch, capacity)
    rows_half = jnp.take_along_axis(tok, chosen[:, :, None], axis=1).reshape(total, half_width)
    cot_half = jnp.take_along_axis(cot, chosen[:, :, None], axis=1).reshape(total, half_width)
    rows = lax.all_gather(rows_half, "tensor", axis=1, tiled=True)
    cot_rows = lax.all_gather(cot_half, "tensor", axis=1, tiled=True)

    rows_f = rows.astype(jnp.float32)
    cot_f = cot_rows.astype(jnp.float32)
    gate = jax.nn.sigmoid(dense(rows, route))
    inv1 = lax.rsqrt(jnp.mean(rows_f * rows_f, -1, keepdims=True) + eps_norm)
    normed = (rows_f * inv1 * gain1).astype(jnp.bfloat16)
    heads = cols // HD

    def split(x):
        return x.astype(jnp.bfloat16).reshape(batch, capacity, heads, HD).transpose(0, 2, 1, 3)

    def join(x):
        return x.transpose(0, 2, 1, 3).reshape(total, cols)

    q = split(dense(normed, fq))
    k = split(dense(normed, fk))
    v = split(dense(normed, fv))
    causal = lax.broadcasted_iota(jnp.int32, (capacity, capacity), 0) >= lax.broadcasted_iota(
        jnp.int32, (capacity, capacity), 1
    )
    scores = jnp.einsum("bhqd,bhkd->bhqk", q, k, preferred_element_type=jnp.float32) * scale
    scores = jnp.where(causal, scores, -1e30)
    peak = jnp.max(scores, -1, keepdims=True)
    expd = jnp.exp(scores - peak)
    probs = expd / jnp.sum(expd, -1, keepdims=True)
    probs_low = probs.astype(jnp.bfloat16)
    mixed = jnp.einsum("bhqk,bhkd->bhqd", probs_low, v, preferred_element_type=jnp.float32)
    mixed = join(mixed.astype(jnp.bfloat16))

    def pair_sum(x):
        low = x.astype(jnp.bfloat16)
        other = lax.ppermute(low, "tensor", swap)
        return low.astype(jnp.float32) + other.astype(jnp.float32)

    attended = pair_sum(dense_t(mixed, foutT))
    hidden = rows_f + attended
    inv2 = lax.rsqrt(jnp.mean(hidden * hidden, -1, keepdims=True) + eps_norm)
    normed2 = (hidden * inv2 * gain2).astype(jnp.bfloat16)
    up = dense(normed2, fup)
    act32, gelu_back = jax.vjp(jax.nn.gelu, up)
    act = act32.astype(jnp.bfloat16)
    down = pair_sum(dense_t(act, fdownT))
    branch = attended + down
    d_logit = jnp.sum(cot_f * branch, -1) * gate * (1.0 - gate)
    branch_half = lax.dynamic_slice_in_dim(branch, offset, half_width, 1)
    new_rows = (rows_half.astype(jnp.float32) + gate[:, None] * branch_half).astype(jnp.bfloat16)

    d_branch = gate[:, None] * cot_f
    d_down = d_branch.astype(jnp.bfloat16)
    g_downT = dense_g(d_down, act)
    d_act = dense(d_down, fdownT)
    d_upper = gelu_back(d_act)[0].astype(jnp.bfloat16)
    g_up = dense_g(normed2, d_upper)
    d_normed2 = pair_sum(dense_t(d_upper, fup))
    d_hidden, g_gain2 = rms_back(hidden, inv2, gain2, d_normed2)
    d_attended = (d_branch + d_hidden).astype(jnp.bfloat16)
    g_outT = dense_g(d_attended, mixed)
    d_mixed = split(dense(d_attended, foutT))
    d_values = jnp.einsum("bhqk,bhqd->bhkd", probs_low, d_mixed, preferred_element_type=jnp.float32)
    d_values = join(d_values.astype(jnp.bfloat16))
    d_probs = jnp.einsum("bhqd,bhkd->bhqk", d_mixed, v, preferred_element_type=jnp.float32)
    d_scores = probs * (d_probs - jnp.sum(d_probs * probs, -1, keepdims=True))
    d_scores = d_scores.astype(jnp.bfloat16)
    d_q = jnp.einsum("bhqk,bhkd->bhqd", d_scores, k, preferred_element_type=jnp.float32) * scale
    d_k = jnp.einsum("bhqk,bhqd->bhkd", d_scores, q, preferred_element_type=jnp.float32) * scale
    d_q = join(d_q.astype(jnp.bfloat16))
    d_k = join(d_k.astype(jnp.bfloat16))
    g_q = dense_g(normed, d_q)
    g_k = dense_g(normed, d_k)
    g_v = dense_g(normed, d_values)
    d_normed = pair_sum(dense_t(d_q, fq) + dense_t(d_k, fk) + dense_t(d_values, fv))
    d_rows, g_gain1 = rms_back(rows_f, inv1, gain1, d_normed)
    g_route = jnp.sum(rows_f * d_logit[:, None], 0)
    d_half = (
        lax.dynamic_slice_in_dim(d_hidden + d_rows, offset, half_width, 1)
        + d_logit[:, None] * lax.dynamic_slice_in_dim(route_f32, offset, half_width, 0)[None, :]
    )
    grad_rows = (cot_half.astype(jnp.float32) + d_half).astype(jnp.bfloat16)

    seq_ids = lax.broadcasted_iota(jnp.int32, (batch, capacity), 0)
    output = tok.at[seq_ids, chosen].set(
        new_rows.reshape(batch, capacity, half_width), unique_indices=True
    )
    input_grad = cot.at[seq_ids, chosen].set(
        grad_rows.reshape(batch, capacity, half_width), unique_indices=True
    )

    g_vec = jnp.pad(jnp.stack([g_route, g_gain1, g_gain2], 1), ((0, 0), (0, 125)))
    grads = jnp.concatenate(
        [x.astype(jnp.bfloat16) for x in (g_q, g_k, g_v, g_up, g_outT, g_downT, g_vec)], 1
    )
    own = lax.psum_scatter(grads, "dp", scatter_dimension=0, tiled=True).astype(jnp.float32)
    return (
        output.reshape(tokens.shape),
        input_grad.reshape(tokens.shape),
        own[:, :b1],
        own[:, b1:b2],
        own[:, b2:b3],
        own[:, b4:b5].T,
        own[:, b3:b4],
        own[:, b5:b6].T,
        own[:, b6],
        own[:, b6 + 1],
        own[:, b6 + 2],
    )


MESH = pl.DeviceIdType.MESH
NB = 48
PATTERN = "XYZX"
PER = 4
LAGS = (0, 3, 6, 9, 12, 15)


class Place:
    def __init__(self):
        me = lax.axis_index("dp")
        self.x = me % 2
        self.y = (me // 2) % 2
        self.z = me // 4
        self.nx = me + 1 - 2 * self.x
        self.ny = me + 2 - 4 * self.y
        self.up = jnp.minimum(me + 4, 15)
        self.dn = jnp.maximum(me - 4, 0)
        self.t = lax.axis_index("tensor")


def both(a, b):
    return jnp.logical_and(a, b)


def barrier(p, core):
    bar = pltpu.get_barrier_semaphore()

    def greet(dev):
        pl.semaphore_signal(bar, inc=1, device_id=dev, device_id_type=MESH)

    greet({"dp": p.nx})
    greet({"dp": p.ny})
    if core:
        greet({"tensor": 1 - p.t})

    @pl.when(p.z < 3)
    def _():
        greet({"dp": p.up})

    @pl.when(p.z > 0)
    def _():
        greet({"dp": p.dn})

    inner = both(p.z > 0, p.z < 3)
    base = 4 if core else 3

    @pl.when(inner)
    def _():
        pl.semaphore_wait(bar, base + 1)

    @pl.when(jnp.logical_not(inner))
    def _():
        pl.semaphore_wait(bar, base)


class Steps:
    def step(self, s, pos, static=None, guard=False):
        live = [j for j in (5, 4, 3, 2, 1, 0) if static is None or 0 <= static - LAGS[j] < NB]

        def do(j, act):
            b = s - LAGS[j]
            if guard:
                pl.when(b < NB)(lambda: act(b, (pos - LAGS[j]) % PER, j))
            else:
                act(b, (pos - LAGS[j]) % PER, j)

        for j in live:
            if j > 0:
                do(j, lambda b, q, j: self.recv(b, q, j - 1))
        for j in live:
            if j < 5:
                do(j, self.send)

    def drain(self, nb=NB):
        def body(r, _):
            for pos in range(PER):
                for j in range(5):
                    self.send(r * PER + pos, pos, j, act=lambda d: d.wait_send())
            return 0

        lax.fori_loop(0, nb // PER, body, 0)


class Gather(Steps):
    def __init__(self, p, W, ss, rs):
        self.p, self.W, self.ss, self.rs = p, W, ss, rs

    def copy(self, ref, b, k, dev):
        return pltpu.make_async_remote_copy(
            ref, ref, self.ss.at[b, k], self.rs.at[b, k], device_id={"dp": dev}, device_id_type=MESH
        )

    def zref(self, b, c, zz):
        zz = jnp.clip(zz, 0, 3)
        return self.W.at[b, zz] if c == "Z" else self.W.at[b, zz, self.p.y, self.p.x]

    def zsend(self, b, c, hop, act):
        p = self.p

        @pl.when(both(p.z - hop + 1 >= 0, p.z < 3))
        def _():
            act(self.copy(self.zref(b, c, p.z - hop + 1), b, hop - 1, p.up))

        @pl.when(both(p.z + hop - 1 <= 3, p.z > 0))
        def _():
            act(self.copy(self.zref(b, c, p.z + hop - 1), b, 2 + hop, p.dn))

    def zrecv(self, b, c, hop):
        p = self.p

        @pl.when(p.z - hop >= 0)
        def _():
            self.copy(self.zref(b, c, p.z - hop), b, hop - 1, p.nx).wait_recv()

        @pl.when(p.z + hop <= 3)
        def _():
            self.copy(self.zref(b, c, p.z + hop), b, 2 + hop, p.nx).wait_recv()

    def stage(self, b, c, j):
        W = self.W
        x, y, z = self.p.x, self.p.y, self.p.z
        if c == "X":
            line = (7, W.at[b, :, :, x], W.at[b, :, :, 1 - x])
            return (1, 2, 3, (6, W.at[b, :, y, x], W.at[b, :, 1 - y, x]), line)[j]
        if c == "Y":
            line = (6, W.at[b, :, y], W.at[b, :, 1 - y])
            return (1, 2, 3, (7, W.at[b, :, y, x], W.at[b, :, y, 1 - x]), line)[j]
        line = (7, W.at[b, z, y, x], W.at[b, z, y, 1 - x])
        return (line, (6, W.at[b, z, y], W.at[b, z, 1 - y]), 1, 2, 3)[j]

    def send(self, b, pos, j, act=lambda d: d.start()):
        c = PATTERN[pos]
        st = self.stage(b, c, j)
        if isinstance(st, int):
            self.zsend(b, c, st, act)
        else:
            act(self.copy(st[1], b, st[0], self.p.ny if st[0] == 6 else self.p.nx))

    def recv(self, b, pos, j):
        c = PATTERN[pos]
        st = self.stage(b, c, j)
        if isinstance(st, int):
            self.zrecv(b, c, st)
        else:
            self.copy(st[2], b, st[0], self.p.nx).wait_recv()


class Scatter(Steps):
    def __init__(self, p, G, out, L8, L4, LZ, P4, P2, P1, ss, rs):
        self.p, self.G, self.out, self.ss, self.rs = p, G, out, ss, rs
        self.L8, self.L4, self.LZ, self.P4, self.P2, self.P1 = L8, L4, LZ, P4, P2, P1

    def slot(self, b, pos):
        r = b // PER
        return r if PATTERN[pos] == "Z" else r * 3 + {0: 0, 1: 1, 3: 2}[pos]

    def copy(self, src, dst, b, k, dev):
        return pltpu.make_async_remote_copy(
            src, dst, self.ss.at[b, k], self.rs.at[b, k], device_id={"dp": dev}, device_id_type=MESH
        )

    def gz(self, b, c, t):
        t = jnp.clip(t, 0, 3)
        return self.G.at[b, t] if c == "Z" else self.G.at[b, t, self.p.y, self.p.x]

    def lz(self, b, pos, k):
        i = self.slot(b, pos)
        return self.P4.at[i, k] if PATTERN[pos] == "Z" else self.LZ.at[i, k]

    def add(self, ref, land):
        ref[...] = (ref[...].astype(jnp.float32) + land[...].astype(jnp.float32)).astype(ref.dtype)

    def zsend(self, b, pos, hop, act):
        p, c = self.p, PATTERN[pos]

        @pl.when(p.z + hop <= 3)
        def _():
            act(self.copy(self.gz(b, c, p.z + hop), self.lz(b, pos, hop - 1), b, hop - 1, p.up))

        @pl.when(p.z - hop >= 0)
        def _():
            act(self.copy(self.gz(b, c, p.z - hop), self.lz(b, pos, 2 + hop), b, 2 + hop, p.dn))

    def zrecv(self, b, pos, hop, final):
        p, c = self.p, PATTERN[pos]

        def take(k, t):
            land = self.lz(b, pos, k)
            self.copy(land, land, b, k, p.nx).wait_recv()
            if not final:
                self.add(self.gz(b, c, t), land)

        if not final:

            @pl.when(both(p.z >= 1, p.z - 1 + hop <= 3))
            def _():
                take(hop - 1, p.z - 1 + hop)

            @pl.when(both(p.z <= 2, p.z + 1 - hop >= 0))
            def _():
                take(2 + hop, p.z + 1 - hop)

            return
        own = self.G.at[b, p.z, p.y, p.x]
        below, above = self.lz(b, pos, 0), self.lz(b, pos, 3)
        f32 = jnp.float32

        @pl.when(p.z == 0)
        def _():
            take(3, p.z)
            self.out[b] = own[...].astype(f32) + above[...].astype(f32)

        @pl.when(p.z == 3)
        def _():
            take(0, p.z)
            self.out[b] = own[...].astype(f32) + below[...].astype(f32)

        @pl.when(both(p.z > 0, p.z < 3))
        def _():
            take(0, p.z)
            take(3, p.z)
            self.out[b] = own[...].astype(f32) + below[...].astype(f32) + above[...].astype(f32)

    def stage(self, b, pos, j):
        G = self.G
        x, y, z = self.p.x, self.p.y, self.p.z
        c, i = PATTERN[pos], self.slot(b, pos)
        if c == "X":
            first = (7, G.at[b, :, :, 1 - x], self.L8.at[i], G.at[b, :, :, x])
            return (first, (6, G.at[b, :, 1 - y, x], self.L4.at[i], G.at[b, :, y, x]), 3, 2, 1)[j]
        if c == "Y":
            first = (6, G.at[b, :, 1 - y], self.L8.at[i], G.at[b, :, y])
            return (first, (7, G.at[b, :, y, 1 - x], self.L4.at[i], G.at[b, :, y, x]), 3, 2, 1)[j]
        last = (7, G.at[b, z, y, 1 - x], self.P1.at[i], G.at[b, z, y, x])
        return (3, 2, 1, (6, G.at[b, z, 1 - y], self.P2.at[i], G.at[b, z, y]), last)[j]

    def send(self, b, pos, j, act=lambda d: d.start()):
        st = self.stage(b, pos, j)
        if isinstance(st, int):
            self.zsend(b, pos, st, act)
        else:
            act(self.copy(st[1], st[2], b, st[0], self.p.ny if st[0] == 6 else self.p.nx))

    def recv(self, b, pos, j):
        st = self.stage(b, pos, j)
        if isinstance(st, int):
            self.zrecv(b, pos, st, PATTERN[pos] != "Z" and j == 4)
        else:
            self.copy(st[2], st[2], b, st[0], self.p.nx).wait_recv()
            if j == 4:
                self.out[b] = st[3][...].astype(jnp.float32) + st[2][...].astype(jnp.float32)
            else:
                self.add(st[3], st[2])

    @staticmethod
    def landing(blocks, tail, dtype):
        n, m = blocks // PER * 3, blocks // PER
        return [
            pltpu.VMEM(shape + tail, dtype)
            for shape in ((n, 4, 2), (n, 4), (n, 6), (m, 6, 2, 2), (m, 2), (m,))
        ] + [pltpu.SemaphoreType.DMA((blocks, 8))] * 2
EPS = 1e-05
SEQ = 4
CAP = 256
ROWS = SEQ * CAP
HBM = pl.ANY


def dot(a, b):
    return jnp.dot(a, b, preferred_element_type=jnp.float32)


def dot_nt(a, b):
    return lax.dot_general(a, b, (((1,), (1,)), ((), ())), preferred_element_type=jnp.float32)


def halves(ref, rs):
    return jnp.concatenate([ref[0, rs, :], ref[1, rs, :]], 1).astype(jnp.float32)


def wblocks(W, first, count):
    return jnp.concatenate([W[first + i].reshape(1024, 128) for i in range(count)], 1)


def seq_rows(i):
    return pl.ds(i * CAP, CAP)


def cut(i, n):
    return pl.ds(pl.multiple_of(i * n, n), n)


def head_masks():
    lane = lax.broadcasted_iota(jnp.int32, (CAP, 128), 1)
    one = jnp.where(lane < HD, 1.0, 0.0)
    return [one.astype(jnp.bfloat16), (1.0 - one).astype(jnp.bfloat16)], lane < HD


def causal_mask():
    shape = (CAP, CAP)
    return lax.broadcasted_iota(jnp.int32, shape, 0) >= lax.broadcasted_iota(jnp.int32, shape, 1)


def softmax_rows(q, k, mask):
    s = jnp.where(mask, dot_nt(q, k) * (HD**-0.5), -1e30)
    e = jnp.exp(s - jnp.max(s, -1, keepdims=True))
    return e * (1.0 / jnp.sum(e, -1, keepdims=True))


def inv_rms(v):
    return lax.rsqrt(jnp.mean(v * v, -1, keepdims=True) + EPS)


def gate_of(rows_f, route):
    return jax.nn.sigmoid(jnp.sum(rows_f * route, -1, keepdims=True))


def own_slot(p, W, b):
    return W.at[b, p.z, p.y, p.x]


def forward_kernel(
    idx_ref,
    tile_ref,
    tok_ref,
    cot_ref,
    wq,
    wk,
    wv,
    wo,
    wu,
    wd,
    o_rows,
    o_cot,
    o_nT,
    o_qkv,
    o_mix,
    o_P,
    o_R,
    o_down,
    o_back,
    o_W,
    o_G,
    o_vec,
    W,
    VB,
    vecs,
    rows,
    cot,
    tokbuf,
    onehot,
    nrm,
    nT,
    dd,
    ddT,
    qkv,
    mixed,
    P,
    R,
    dacc,
    nacc,
    act,
    dup,
    u32,
    d32,
    Gst,
    ss,
    rs,
    vss,
    vrs,
    hs,
    hr,
    asnd,
    arcv,
    first,
    load,
    outs,
    gout,
):
    p = Place()
    t = p.t
    other = {"tensor": 1 - t}
    f32, bf = jnp.float32, jnp.bfloat16

    own = [pltpu.make_async_copy(tile_ref, own_slot(p, VB, 0), first.at[NB])]
    for b in range(16):
        src = (wq, wk, wv, wo)[b // 4]
        own.append(
            pltpu.make_async_copy(
                src.at[:, pl.ds(b % 4 * 128, 128)], own_slot(p, W, b), first.at[b]
            )
        )
    for b in range(32):
        src = (wu, wd)[b % 4 // 2]
        own.append(
            pltpu.make_async_copy(
                src.at[:, pl.ds((b // 4 * 2 + b % 2) * 128, 128)],
                own_slot(p, W, 16 + b),
                first.at[16 + b],
            )
        )
    for c in own:
        c.start()

    units = [(a, i) for i in range(SEQ) for a in (0, 1)]

    def loader(u):
        a, i = units[u]
        return pltpu.make_async_copy((tok_ref, cot_ref)[a].at[i], tokbuf.at[u % 2], load.at[u % 2])

    loader(0).start()
    loader(1).start()
    barrier(p, True)
    for c in own:
        c.wait()
    W_steps = Gather(p, W, ss, rs)
    V_steps = Gather(p, VB, vss, vrs)

    def tick(s, guard=False):
        if isinstance(s, int):
            W_steps.step(s, s % PER, static=s)
            if s in LAGS:
                j = LAGS.index(s)
                if j > 0:
                    V_steps.recv(0, 0, j - 1)
                if j < 5:
                    V_steps.send(0, 0, j)

    def half_copy(u):
        a, i = units[u]
        ref = (rows, cot)[a].at[t, seq_rows(i)]
        return pltpu.make_async_remote_copy(
            ref, ref, hs.at[u], hr.at[u], device_id=other, device_id_type=MESH
        )

    def half_wait(u):
        a, i = units[u]
        ref = (rows, cot)[a].at[1 - t, seq_rows(i)]
        pltpu.make_async_remote_copy(
            ref, ref, hs.at[u], hr.at[u], device_id=other, device_id_type=MESH
        ).wait_recv()

    for u, (a, i) in enumerate(units):
        tick(2 * u)
        if a == 0:
            spot = idx_ref[seq_rows(i), :]
            hit = lax.broadcasted_iota(jnp.int32, (CAP, 2048), 1) == spot
            onehot[...] = jnp.where(hit, 1.0, 0.0).astype(bf)
        loader(u).wait()
        (rows, cot)[a][t, seq_rows(i), :] = dot(onehot[...], tokbuf[u % 2]).astype(bf)
        if u + 2 < 8:
            loader(u + 2).start()
        tick(2 * u + 1)
        if u > 0:
            half_copy(u - 1).start()
    half_copy(7).start()

    for z in range(4):
        for y in range(2):
            vecs[:, pl.ds((z * 2 + y) * 128, 128)] = VB[0, z, y, 0] + VB[0, z, y, 1]

    def saver(k, src, dst):
        return pltpu.make_async_copy(src, dst, outs.at[k])

    saved = [saver(0, vecs, o_vec)]
    saved[0].start()

    dacc[...] = jnp.zeros_like(dacc)
    nacc[...] = jnp.zeros_like(nacc)

    for i in range(SEQ):
        tick(16 + i)
        half_wait(2 * i)
        half_wait(2 * i + 1)

        def norm_part(n, _):
            rs_ = cut(i * 8 + n, 32)
            r = halves(rows, rs_)
            nrm[rs_, :] = (r * inv_rms(r) * vecs[1:2, :]).astype(bf)
            dd[rs_, :] = (gate_of(r, vecs[0:1, :]) * halves(cot, rs_)).astype(bf)
            return 0

        lax.fori_loop(0, 8, norm_part, 0)
        for c in range(4):
            cs = pl.ds(c * 256, 256)
            nT[cs, seq_rows(i)] = nrm[seq_rows(i), cs].T
            ddT[cs, seq_rows(i)] = dd[seq_rows(i), cs].T
    later = [saver(1, rows, o_rows), saver(2, cot, o_cot), saver(3, nT, o_nT)]
    for c in later:
        c.start()
    saved += later[:2]
    nT_saved = later[2]

    def project(j):
        y = dot(nrm[...], wblocks(W, 2 * j, 2)).astype(bf)
        qkv[2 * j] = y[:, :128]
        qkv[2 * j + 1] = y[:, 128:]

    def project_part(n, _):
        s = 20 + 4 * n
        W_steps.step(s, 0)
        W_steps.step(s + 1, 1)
        project(3 * n)
        W_steps.step(s + 2, 2)
        project(3 * n + 1)
        W_steps.step(s + 3, 3)
        project(3 * n + 2)
        return 0

    lax.fori_loop(0, 2, project_part, 0)
    saved.append(saver(4, qkv, o_qkv))
    saved[-1].start()

    masks, low_half = head_masks()
    mask = causal_mask()

    def attend(i, hp):
        r_ = cut(i, CAP)
        q, k, v = qkv[hp, r_, :], qkv[4 + hp, r_, :], qkv[8 + hp, r_, :]
        mix = [dot(softmax_rows(q * masks[h], k, mask).astype(bf), v) for h in (0, 1)]
        mixed[hp, r_, :] = jnp.where(low_half, mix[0], mix[1]).astype(bf)

    def attend_part(n, _):
        for q in range(4):
            W_steps.step(28 + 4 * n + q, q)

            def pair(e, _):
                attend(2 * n + q // 2, q % 2 * 2 + e)
                return 0

            lax.fori_loop(0, 2, pair, 0)
        return 0

    lax.fori_loop(0, 2, attend_part, 0)
    saved.append(saver(5, mixed, o_mix))
    saved[-1].start()

    def att_copy(i):
        return pltpu.make_async_remote_copy(
            P.at[seq_rows(i)],
            R.at[seq_rows(i)],
            asnd.at[i],
            arcv.at[i],
            device_id=other,
            device_id_type=MESH,
        )

    for i in range(SEQ):
        W_steps.step(36 + i, i)
        mix = jnp.concatenate([mixed[h, seq_rows(i), :] for h in range(4)], 1)
        P[seq_rows(i), :] = dot_nt(mix, wblocks(W, 12, 4)).astype(bf)
        if i > 0:
            att_copy(i - 1).start()
    nT_saved.wait()
    saved.append(saver(6, W.at[pl.ds(0, 16)], o_W))
    saved[-1].start()
    att_copy(3).start()
    for i in range(SEQ):
        att_copy(i).wait_recv()

        def norm_part(n, _):
            rs_ = cut(i * 8 + n, 32)
            h = halves(rows, rs_) + (P[rs_, :].astype(f32) + R[rs_, :].astype(f32))
            nrm[rs_, :] = (h * inv_rms(h) * vecs[2:3, :]).astype(bf)
            return 0

        lax.fori_loop(0, 8, norm_part, 0)
        for c in range(4):
            cs = pl.ds(c * 256, 256)
            nT[cs, seq_rows(i)] = nrm[seq_rows(i), cs].T
    later = [saver(7, P, o_P), saver(8, R, o_R)]
    for c in later:
        c.start()
    saved += later

    def g_copy(m):
        slot = lax.rem(m, 2)
        return pltpu.make_async_copy(Gst.at[slot], o_G.at[pl.ds(m * 4, 4)], gout.at[slot])

    def mlp_part(m, _):
        slot = lax.rem(m, 2)
        s = 40 + 4 * m
        up_w = wblocks(W, 16 + 4 * m, 2)
        down_w = wblocks(W, 18 + 4 * m, 2)
        for ht in range(2):
            hs_ = pl.ds(ht * 512, 512)
            W_steps.step(s + 2 * ht, 2 * ht, guard=True)
            u32[...] = dot(nrm[hs_, :], up_w)
            d32[...] = dot(dd[hs_, :], down_w)

            def gelu_part(n, _):
                rs_ = cut(n, 32)
                out_ = pl.ds(pl.multiple_of(ht * 512 + n * 32, 32), 32)
                u = u32[rs_, :]
                c0 = 0.7978845608028654
                u2 = u * u
                th = jnp.tanh(c0 * (u + 0.044715 * (u * u2)))
                cdf = 0.5 * (1.0 + th)
                act[out_, :] = (u * cdf).astype(bf)
                slope = cdf + 0.5 * u * (1.0 - th * th) * (c0 + (3 * 0.044715 * c0) * u2)
                dup[out_, :] = (d32[rs_, :] * slope).astype(bf)
                return 0

            lax.fori_loop(0, 16, gelu_part, 0)
            W_steps.step(s + 2 * ht + 1, 2 * ht + 1, guard=True)
            dacc[hs_, :] += dot_nt(act[hs_, :], down_w)
            nacc[hs_, :] += dot_nt(dup[hs_, :], up_w)

        @pl.when(m >= 2)
        def _():
            g_copy(m - 2).wait()

        for ht in range(2):
            hs_ = pl.ds(ht * 512, 512)
            gu = dot(nT[hs_, :], dup[...]).astype(bf)
            Gst[slot, 0, hs_, :] = gu[:, :128]
            Gst[slot, 1, hs_, :] = gu[:, 128:]
            gd = dot(ddT[hs_, :], act[...]).astype(bf)
            Gst[slot, 2, hs_, :] = gd[:, :128]
            Gst[slot, 3, hs_, :] = gd[:, 128:]
        g_copy(m).start()
        return 0

    lax.fori_loop(0, 8, mlp_part, 0)
    for e in range(2):
        for c in range(2):
            tokbuf[e, pl.ds(c * 1024, 1024), :] = (dacc, nacc)[e][:, c * 512 : c * 512 + 512].astype(bf)
            saved.append(
                saver(9 + 2 * e + c, tokbuf.at[e, pl.ds(c * 1024, 1024)], (o_down, o_back)[e].at[c])
            )
            saved[-1].start()
    for u in range(8):
        half_copy(u).wait_send()
    for i in range(SEQ):
        att_copy(i).wait_send()
    W_steps.drain()
    for j in range(5):
        V_steps.send(0, 0, j, act=lambda d: d.wait_send())
    g_copy(6).wait()
    g_copy(7).wait()
    for c in saved:
        c.wait()


def forward_call(chosen, tile, tok, cotangent, weights):
    bf, f32 = jnp.bfloat16, jnp.float32
    S = jax.ShapeDtypeStruct
    DMA = pltpu.SemaphoreType.DMA
    any_ = pl.BlockSpec(memory_space=HBM)
    vm = pltpu.VMEM
    return pl.pallas_call(
        forward_kernel,
        out_shape=(
            S((2, ROWS, 512), bf),
            S((2, ROWS, 512), bf),
            S((1024, ROWS), bf),
            S((12, ROWS, 128), bf),
            S((4, ROWS, 128), bf),
            S((ROWS, 1024), bf),
            S((ROWS, 1024), bf),
            S((2, ROWS, 512), bf),
            S((2, ROWS, 512), bf),
            S((16, 4, 2, 2, 64, 128), bf),
            S((32, 1024, 128), bf),
            S((8, 1024), f32),
        ),
        in_specs=[pl.BlockSpec(memory_space=pltpu.VMEM)] + [any_] * 9,
        out_specs=[any_] * 12,
        scratch_shapes=[
            vm((NB, 4, 2, 2, 64, 128), bf),
            vm((1, 4, 2, 2, 8, 128), f32),
            vm((8, 1024), f32),
            vm((2, ROWS, 512), bf),
            vm((2, ROWS, 512), bf),
            vm((2, 2048, 512), bf),
            vm((CAP, 2048), bf),
            vm((ROWS, 1024), bf),
            vm((1024, ROWS), bf),
            vm((ROWS, 1024), bf),
            vm((1024, ROWS), bf),
            vm((12, ROWS, 128), bf),
            vm((4, ROWS, 128), bf),
            vm((ROWS, 1024), bf),
            vm((ROWS, 1024), bf),
            vm((ROWS, 1024), f32),
            vm((ROWS, 1024), f32),
            vm((ROWS, 256), bf),
            vm((ROWS, 256), bf),
            vm((512, 256), f32),
            vm((512, 256), f32),
            vm((2, 4, 1024, 128), bf),
            DMA((NB, 8)),
            DMA((NB, 8)),
            DMA((1, 8)),
            DMA((1, 8)),
            DMA((8,)),
            DMA((8,)),
            DMA((4,)),
            DMA((4,)),
            DMA((NB + 1,)),
            DMA((2,)),
            DMA((13,)),
            DMA((2,)),
        ],
        compiler_params=pltpu.CompilerParams(
            collective_id=1, has_side_effects=True, vmem_limit_bytes=63 * 1024 * 1024
        ),
        name="forward",
    )(chosen, tile, tok, cotangent, *weights)


def backward_kernel(
    spot_ref,
    rows,
    cot,
    nT_in,
    qkv_in,
    mix_in,
    P_in,
    R_in,
    down_in,
    back_in,
    W_in,
    G_in,
    vec_in,
    tok_ref,
    cot_ref,
    o_tok,
    o_cot,
    o_sum,
    o_vec,
    G,
    Wa,
    qkv,
    mixed,
    nT,
    vecs,
    DR,
    NR,
    R1,
    bufs,
    buf2,
    da,
    daT,
    dmix,
    newr,
    newg,
    dhid,
    dlog,
    accs,
    GV,
    base,
    gsem,
    lsem,
    psem,
    prcv,
    qsem,
    qrcv,
    tin,
    tout,
    *landing,
):
    p = Place()
    t = p.t
    other = {"tensor": 1 - t}
    f32, bf = jnp.float32, jnp.bfloat16
    wide, small = landing[:8], landing[8:]

    g_loads = [
        pltpu.make_async_copy(G_in.at[pl.ds(4 * c, 4)], G.at[pl.ds(4 * c, 4)], gsem.at[c])
        for c in range(8)
    ]
    g_loads[0].start()

    def stream(s, names):
        q = s % 2
        out = []
        for k in names:
            if k < 2:
                src = (P_in, R_in)[k].at[seq_rows(s)]
                dst = buf2.at[q, k]
            else:
                src = (rows, cot, down_in, back_in)[k - 2].at[:, seq_rows(s)]
                dst = bufs.at[q, k - 2]
            out.append(pltpu.make_async_copy(src, dst, lsem.at[q, k]))
        return out

    everything = (0, 1, 2, 3, 4, 5)
    for c in stream(0, everything):
        c.start()
    fixed = [
        pltpu.make_async_copy(a, b, base.at[i])
        for i, (a, b) in enumerate(
            ((vec_in, vecs), (W_in, Wa), (qkv_in, qkv), (mix_in, mixed), (nT_in, nT))
        )
    ]
    for c in fixed[:1]:
        c.start()
    for c in g_loads[1:]:
        c.start()
    barrier(p, True)

    def pair_copy(s, e):
        return pltpu.make_async_remote_copy(
            (down_in, back_in)[e].at[:, seq_rows(s)],
            (DR, NR)[e].at[:, seq_rows(s)],
            psem.at[s, e],
            prcv.at[s, e],
            device_id=other,
            device_id_type=MESH,
        )

    for s in range(SEQ):
        for e in range(2):
            pair_copy(s, e).start()
    for c in fixed[1:]:
        c.start()
    steps = Scatter(p, G, o_sum, *wide)
    v_steps = Scatter(p, GV, o_vec, *small)

    def tick(s):
        if s < 32 and s % 4 == 0:
            g_loads[s // 4].wait()
        steps.step(s, s % PER, static=s)

    accs[...] = jnp.zeros_like(accs)

    def fold(v):
        return jnp.sum(v.reshape(4, 8, 1024), 0)

    def pick(v):
        return jnp.where(t == 0, v[:, :512], v[:, 512:])

    masks, low_half = head_masks()
    seen = lax.broadcasted_iota(jnp.int32, (CAP, CAP), 0) <= lax.broadcasted_iota(
        jnp.int32, (CAP, CAP), 1
    )

    for s in range(SEQ):
        tick(4 * s)
        q = s % 2
        if s + 1 < SEQ:
            for c in stream(s + 1, everything):
                c.start()
        if s == 0:
            fixed[0].wait()
        for c in stream(s, everything):
            c.wait()
        for e in range(2):
            pair_copy(s, e).wait_recv()

        def part(n, _):
            rs_ = cut(n, 32)
            as_ = pl.ds(pl.multiple_of(s * CAP + n * 32, 32), 32)

            def mine(k):
                return jnp.concatenate([bufs[q, k, 0, rs_, :], bufs[q, k, 1, rs_, :]], 1).astype(f32)

            r, c = mine(0), mine(1)
            att = buf2[q, 0, rs_, :].astype(f32) + buf2[q, 1, rs_, :].astype(f32)
            h = r + att
            branch = att + (mine(2) + halves(DR, as_))
            dn = mine(3) + halves(NR, as_)
            inv = inv_rms(h)
            sc = dn * vecs[2:3, :]
            dh = inv * sc - h * (inv * inv * inv * jnp.mean(sc * h, -1, keepdims=True))
            gate = gate_of(r, vecs[0:1, :])
            dl = jnp.sum(c * branch, -1, keepdims=True) * (gate * (1.0 - gate))
            da[rs_, :] = (gate * c + dh).astype(bf)
            accs[2] += fold(dn * (h * inv))
            accs[0] += fold(r * dl)
            newr[as_, :] = pick(r + gate * branch).astype(bf)
            dhid[as_, :] = pick(dh)
            dlog[as_, :] = jnp.broadcast_to(dl, (32, 128))
            return 0

        lax.fori_loop(0, 8, part, 0)
        tick(4 * s + 1)
        for c in range(4):
            cs = pl.ds(c * 256, 256)
            daT[cs, seq_rows(s)] = da[:, cs].T
        if s == 0:
            for c in fixed[1:]:
                c.wait()
        dm = dot(da[...], wblocks(Wa, 12, 4)).astype(bf)
        for h in range(4):
            dmix[h] = dm[:, h * 128 : h * 128 + 128]

        def pair_back(hp):
            r_ = seq_rows(s)
            qh, kh, vh, dmh = qkv[hp, r_, :], qkv[4 + hp, r_, :], qkv[8 + hp, r_, :], dmix[hp]
            outs = []
            for h in (0, 1):
                sc = jnp.where(seen, dot_nt(kh, qh * masks[h]) * (HD**-0.5), -1e30)
                e = jnp.exp(sc - jnp.max(sc, 0, keepdims=True))
                pr = e * (1.0 / jnp.sum(e, 0, keepdims=True))
                dv = dot(pr.astype(bf), dmh)
                dp = dot_nt(vh * masks[h], dmh)
                ds = (pr * (dp - jnp.sum(dp * pr, 0, keepdims=True))).astype(bf)
                outs.append((dot(ds.T, kh), dot(ds, qh), dv))
            scale = HD**-0.5
            for i, (a, b) in enumerate(zip(*outs)):
                v = jnp.where(low_half, a, b)
                qkv[4 * i + hp, r_, :] = (v if i == 2 else v * scale).astype(bf)

        for half in range(2):
            tick(4 * s + 2 + half)

            def pair_part(e, _):
                pair_back(2 * half + e)
                return 0

            lax.fori_loop(0, 2, pair_part, 0)

    def grad_unit(leftT, a, b, first):
        y = jnp.concatenate([a, b], 1)
        for ht in range(2):
            g = dot(leftT[pl.ds(ht * 512, 512), :], y).astype(bf)
            for c in range(2):
                G[first + c, pl.ds(ht * 2, 2)] = g[:, c * 128 : c * 128 + 128].reshape(
                    2, 2, 2, 64, 128
                )

    def back_copy(s):
        return pltpu.make_async_remote_copy(
            DR.at[:, seq_rows(s)],
            R1.at[:, seq_rows(s)],
            qsem.at[s],
            qrcv.at[s],
            device_id=other,
            device_id_type=MESH,
        )

    for c in stream(0, (2, 3)):
        c.start()
    for c in stream(1, (2, 3)):
        c.start()
    for s in range(SEQ):
        tick(16 + s)
        x = jnp.concatenate([qkv[i, seq_rows(s), :] for i in range(12)], 1)
        y = dot_nt(x, wblocks(Wa, 0, 12)).astype(bf)
        DR[0, seq_rows(s), :] = y[:, :512]
        DR[1, seq_rows(s), :] = y[:, 512:]
        if s > 0:
            back_copy(s - 1).start()
    tick(20)
    back_copy(3).start()
    grad_unit(daT, mixed[0], mixed[1], 32)
    tick(21)
    grad_unit(daT, mixed[2], mixed[3], 34)
    for g_load in g_loads[6:]:
        g_load.wait()

    def grad_part(n, _):
        for e in range(2):
            sn = 22 + 4 * n + 2 * e
            steps.step(sn, (2 + 2 * e) % 4)
            steps.step(sn + 1, (3 + 2 * e) % 4)
            j = 2 * n + e
            grad_unit(nT, qkv[2 * j], qkv[2 * j + 1], 36 + 2 * j)
        return 0

    lax.fori_loop(0, 2, grad_part, 0)
    for e in range(2):
        grad_unit(nT, qkv[8 + 2 * e], qkv[9 + 2 * e], 44 + 2 * e)
        steps.step(30 + e, 2 + e)

    route_half = jnp.where(t == 0, vecs[0:1, :512], vecs[0:1, 512:])
    for s in range(SEQ):
        steps.step(32 + 2 * s, 2 * s % 4)
        steps.step(33 + 2 * s, (2 * s + 1) % 4)
        q = s % 2
        for c in stream(s, (2, 3)):
            c.wait()
        back_copy(s).wait_recv()

        def part(n, _):
            rs_ = cut(n, 32)
            as_ = pl.ds(pl.multiple_of(s * CAP + n * 32, 32), 32)
            r = jnp.concatenate([bufs[q, 0, 0, rs_, :], bufs[q, 0, 1, rs_, :]], 1).astype(f32)
            dn = halves(DR, as_) + halves(R1, as_)
            inv = inv_rms(r)
            sc = dn * vecs[1:2, :]
            dr = inv * sc - r * (inv * inv * inv * jnp.mean(sc * r, -1, keepdims=True))
            accs[1] += fold(dn * (r * inv))
            dl = dlog[as_, :]
            dl = jnp.concatenate([dl, dl, dl, dl], 1)
            ch = bufs[q, 1, t, rs_, :].astype(f32)
            newg[as_, :] = (ch + (dhid[as_, :] + pick(dr) + dl * route_half)).astype(bf)
            return 0

        lax.fori_loop(0, 8, part, 0)
        if s + 2 < SEQ:
            for c in stream(s + 2, (2, 3)):
                c.start()

    for z in range(4):
        for y in range(2):
            cs = pl.ds((z * 2 + y) * 128, 128)
            tile = jnp.concatenate(
                [jnp.sum(accs[k, :, cs], 0, keepdims=True) for k in range(3)]
                + [jnp.zeros((5, 128), f32)],
                0,
            )
            GV[0, z, y, 0] = tile
            GV[0, z, y, 1] = tile
    for s in range(SEQ):
        back_copy(s).wait_send()

    def tok_in(n, a):
        return pltpu.make_async_copy(
            (tok_ref, cot_ref)[a].at[n // 4, cut(n % 4, 512)],
            NR.at[a, cut(n % 2, 512)],
            tin.at[a, n % 2],
        )

    def tok_out(n, a):
        return pltpu.make_async_copy(
            DR.at[a, cut(n % 2, 512)],
            (o_tok, o_cot)[a].at[n // 4, cut(n % 4, 512)],
            tout.at[a, n % 2],
        )

    for n in range(2):
        for a in range(2):
            tok_in(n, a).start()
    v_steps.send(0, 0, 0)
    ones = jnp.ones((CAP, 128), bf)

    def place_part(m, _):
        for e in range(4):
            n = 4 * m + e
            steps.step(40 + n, e, guard=True)
            place = lax.broadcasted_iota(jnp.int32, (512, CAP), 0) + e * 512
            hit = jnp.where(place == spot_ref[m], 1.0, 0.0).astype(bf)
            there = dot(hit, ones)
            there = jnp.concatenate([there, there, there, there], 1) > 0.5
            for a in range(2):
                tok_in(n, a).wait()
                new = dot(hit, (newr, newg)[a][cut(m, CAP), :])
                slot = pl.ds(e % 2 * 512, 512)
                old = NR[a, slot, :].astype(f32)
                if e >= 2:
                    tok_out(n - 2, a).wait()
                else:
                    pl.when(m > 0)(lambda: tok_out(n - 2, a).wait())
                DR[a, slot, :] = jnp.where(there, new, old).astype(bf)
                tok_out(n, a).start()
                if e < 2:
                    tok_in(n + 2, a).start()
                else:
                    pl.when(m < 3)(lambda: tok_in(n + 2, a).start())
        return 0

    lax.fori_loop(0, 4, place_part, 0)
    for k, s in enumerate(range(56, 64)):
        tick(s)
        if k in (0, 2, 3, 5, 7):
            j = (0, 2, 3, 5, 7).index(k) + 1
            v_steps.recv(0, 0, j - 1)
            if j < 5:
                v_steps.send(0, 0, j)
    for n in (14, 15):
        for a in range(2):
            tok_out(n, a).wait()
    for s in range(SEQ):
        for e in range(2):
            pair_copy(s, e).wait_send()
    for j in range(5):
        v_steps.send(0, 0, j, act=lambda d: d.wait_send())
    steps.drain()


def backward_call(spot, kept, tok, cotangent):
    bf, f32 = jnp.bfloat16, jnp.float32
    S = jax.ShapeDtypeStruct
    DMA = pltpu.SemaphoreType.DMA
    any_ = pl.BlockSpec(memory_space=HBM)
    vspec = pl.BlockSpec(memory_space=pltpu.VMEM)
    vm = pltpu.VMEM
    return pl.pallas_call(
        backward_kernel,
        out_shape=(
            S((SEQ, 2048, 512), bf),
            S((SEQ, 2048, 512), bf),
            S((NB, 64, 128), f32),
            S((1, 8, 128), f32),
        ),
        in_specs=[vspec] + [any_] * 14,
        out_specs=[any_, any_, vspec, vspec],
        scratch_shapes=[
            vm((NB, 4, 2, 2, 64, 128), bf),
            vm((16, 4, 2, 2, 64, 128), bf),
            vm((12, ROWS, 128), bf),
            vm((4, ROWS, 128), bf),
            vm((1024, ROWS), bf),
            vm((8, 1024), f32),
            vm((2, ROWS, 512), bf),
            vm((2, ROWS, 512), bf),
            vm((2, ROWS, 512), bf),
            vm((2, 4, 2, CAP, 512), bf),
            vm((2, 2, CAP, 1024), bf),
            vm((CAP, 1024), bf),
            vm((1024, ROWS), bf),
            vm((4, CAP, 128), bf),
            vm((ROWS, 512), bf),
            vm((ROWS, 512), bf),
            vm((ROWS, 512), f32),
            vm((ROWS, 128), f32),
            vm((3, 8, 1024), f32),
            vm((1, 4, 2, 2, 8, 128), f32),
            DMA((5,)),
            DMA((8,)),
            DMA((2, 6)),
            DMA((4, 2)),
            DMA((4, 2)),
            DMA((4,)),
            DMA((4,)),
            DMA((2, 2)),
            DMA((2, 2)),
        ]
        + Scatter.landing(NB, (64, 128), bf)
        + Scatter.landing(PER, (8, 128), f32),
        compiler_params=pltpu.CompilerParams(
            collective_id=2, has_side_effects=True, vmem_limit_bytes=63 * 1024 * 1024
        ),
        name="backward",
    )(spot, *kept, tok, cotangent)


def to_tile(w_route, gain_attn, gain_mlp):
    v = jnp.stack([w_route, gain_attn, gain_mlp]).astype(jnp.float32)
    v = jnp.pad(v, ((0, 5), (0, 0)))
    z = jnp.zeros_like(v)
    odd = lax.axis_index("dp") % 2
    return jnp.where(odd == 0, jnp.concatenate([v, z], 1), jnp.concatenate([z, v], 1))


def from_blocks(x):
    return x.transpose(1, 0, 2).reshape(x.shape[1], -1)


def fused(
    tokens,
    routed,
    w_query,
    w_key,
    w_value,
    w_out,
    w_up,
    w_down,
    w_route,
    gain_attn,
    gain_mlp,
    cotangent,
):
    tok = tokens.reshape(SEQ, 2048, 512)
    cot = cotangent.reshape(SEQ, 2048, 512)
    tile = to_tile(w_route, gain_attn, gain_mlp)
    weights = (w_query, w_key, w_value, w_out.T, w_up, w_down.T)
    kept = list(forward_call(routed.reshape(ROWS, 1), tile, tok, cot, weights))
    kept[10] = kept[10].reshape(32, 4, 2, 2, 64, 128)
    output, grad, own, vec = backward_call(routed.reshape(SEQ, 1, CAP), kept, tok, cot)
    mlp = own[:32].reshape(8, 2, 2, 64, 128)
    odd = lax.axis_index("dp") % 2
    vec = jnp.where(odd == 0, vec[0, :3, :64], vec[0, :3, 64:])
    return (
        output.reshape(tokens.shape),
        grad.reshape(tokens.shape),
        from_blocks(own[36:40]),
        from_blocks(own[40:44]),
        from_blocks(own[44:48]),
        from_blocks(own[32:36]).T,
        from_blocks(mlp[:, 0].reshape(16, 64, 128)),
        from_blocks(mlp[:, 1].reshape(16, 64, 128)).T,
        vec[0],
        vec[1],
        vec[2],
    )


def shards(tokens, routed, *rest):
    sizes = (lax.axis_size("dp"), lax.axis_size("tensor"))
    here = tokens.shape == (4, 1, 2048, 512) and routed.shape == (4, 1, 256)
    if sizes == (16, 2) and here:
        return fused(tokens, routed, *rest)
    return plain(tokens, routed, *rest)


def solution(mesh):
    rows = P("dp", "tensor")
    columns = P("tensor", "dp")
    vector = P("dp")
    stored = P(None, "dp", None, "tensor")
    return jax.shard_map(
        shards,
        mesh=mesh,
        in_specs=(
            stored,
            P(None, "dp", None),
            rows,
            rows,
            rows,
            columns,
            rows,
            columns,
            vector,
            vector,
            vector,
            stored,
        ),
        out_specs=(
            stored,
            stored,
            rows,
            rows,
            rows,
            columns,
            rows,
            columns,
            vector,
            vector,
            vector,
        ),
        check_vma=False,
    )
```

```python
import jax
import jax.numpy as jnp
from jax import lax
from jax.experimental import pallas as pl
from jax.experimental.pallas import tpu as pltpu
from jax.sharding import PartitionSpec as P

HD = 64
eps_norm = 1e-05


def dense(left, right):
    return jnp.dot(left, right, preferred_element_type=jnp.float32)


def dense_t(left, right):
    return lax.dot_general(
        left, right, (((1,), (1,)), ((), ())), preferred_element_type=jnp.float32
    )


def dense_g(left, right):
    return lax.dot_general(
        left, right, (((0,), (0,)), ((), ())), preferred_element_type=jnp.float32
    )


def rms_back(values, inv, gain, grad):
    grad_gain = jnp.sum(grad * values * inv, 0)
    scaled = grad * gain
    dot = jnp.mean(scaled * values, -1, keepdims=True)
    return inv * scaled - values * (inv * inv * inv) * dot, grad_gain


def plain(
    tokens,
    routed,
    w_query,
    w_key,
    w_value,
    w_out,
    w_up,
    w_down,
    w_route,
    gain_attn,
    gain_mlp,
    cotangent,
):
    micro, seqs, length, half_width = tokens.shape
    capacity = routed.shape[2]
    batch = micro * seqs
    total = batch * capacity
    cols = w_query.shape[1]
    hidden_cols = w_up.shape[1]
    width = half_width * lax.axis_size("tensor")
    offset = lax.axis_index("tensor") * half_width
    scale = HD ** (-0.5)
    swap = [(0, 1), (1, 0)]

    vec = jnp.stack([w_route, gain_attn, gain_mlp], 1)
    vec = jnp.pad(vec, ((0, 0), (0, 125)))
    packed = jnp.concatenate([w_query, w_key, w_value, w_up, w_out.T, w_down.T, vec], 1)
    gathered = lax.all_gather(packed, "dp", axis=0, tiled=True)
    b1, b2, b3 = cols, 2 * cols, 3 * cols
    b4 = b3 + hidden_cols
    b5 = b4 + w_out.shape[0]
    b6 = b5 + w_down.shape[0]
    fq = gathered[:, :b1]
    fk = gathered[:, b1:b2]
    fv = gathered[:, b2:b3]
    fup = gathered[:, b3:b4]
    foutT = gathered[:, b4:b5]
    fdownT = gathered[:, b5:b6]
    route = gathered[:, b6]
    route_f32 = route.astype(jnp.float32)
    gain1 = gathered[:, b6 + 1].astype(jnp.float32)
    gain2 = gathered[:, b6 + 2].astype(jnp.float32)

    tok = tokens.reshape(batch, length, half_width)
    cot = cotangent.reshape(batch, length, half_width)
    chosen = routed.reshape(batch, capacity)
    rows_half = jnp.take_along_axis(tok, chosen[:, :, None], axis=1).reshape(total, half_width)
    cot_half = jnp.take_along_axis(cot, chosen[:, :, None], axis=1).reshape(total, half_width)
    rows = lax.all_gather(rows_half, "tensor", axis=1, tiled=True)
    cot_rows = lax.all_gather(cot_half, "tensor", axis=1, tiled=True)

    rows_f = rows.astype(jnp.float32)
    cot_f = cot_rows.astype(jnp.float32)
    gate = jax.nn.sigmoid(dense(rows, route))
    inv1 = lax.rsqrt(jnp.mean(rows_f * rows_f, -1, keepdims=True) + eps_norm)
    normed = (rows_f * inv1 * gain1).astype(jnp.bfloat16)
    heads = cols // HD

    def split(x):
        return x.astype(jnp.bfloat16).reshape(batch, capacity, heads, HD).transpose(0, 2, 1, 3)

    def join(x):
        return x.transpose(0, 2, 1, 3).reshape(total, cols)

    q = split(dense(normed, fq))
    k = split(dense(normed, fk))
    v = split(dense(normed, fv))
    causal = lax.broadcasted_iota(jnp.int32, (capacity, capacity), 0) >= lax.broadcasted_iota(
        jnp.int32, (capacity, capacity), 1
    )
    scores = jnp.einsum("bhqd,bhkd->bhqk", q, k, preferred_element_type=jnp.float32) * scale
    scores = jnp.where(causal, scores, -1e30)
    peak = jnp.max(scores, -1, keepdims=True)
    expd = jnp.exp(scores - peak)
    probs = expd / jnp.sum(expd, -1, keepdims=True)
    probs_low = probs.astype(jnp.bfloat16)
    mixed = jnp.einsum("bhqk,bhkd->bhqd", probs_low, v, preferred_element_type=jnp.float32)
    mixed = join(mixed.astype(jnp.bfloat16))

    def pair_sum(x):
        low = x.astype(jnp.bfloat16)
        other = lax.ppermute(low, "tensor", swap)
        return low.astype(jnp.float32) + other.astype(jnp.float32)

    attended = pair_sum(dense_t(mixed, foutT))
    hidden = rows_f + attended
    inv2 = lax.rsqrt(jnp.mean(hidden * hidden, -1, keepdims=True) + eps_norm)
    normed2 = (hidden * inv2 * gain2).astype(jnp.bfloat16)
    up = dense(normed2, fup)
    act32, gelu_back = jax.vjp(jax.nn.gelu, up)
    act = act32.astype(jnp.bfloat16)
    down = pair_sum(dense_t(act, fdownT))
    branch = attended + down
    d_logit = jnp.sum(cot_f * branch, -1) * gate * (1.0 - gate)
    branch_half = lax.dynamic_slice_in_dim(branch, offset, half_width, 1)
    new_rows = (rows_half.astype(jnp.float32) + gate[:, None] * branch_half).astype(jnp.bfloat16)

    d_branch = gate[:, None] * cot_f
    d_down = d_branch.astype(jnp.bfloat16)
    g_downT = dense_g(d_down, act)
    d_act = dense(d_down, fdownT)
    d_upper = gelu_back(d_act)[0].astype(jnp.bfloat16)
    g_up = dense_g(normed2, d_upper)
    d_normed2 = pair_sum(dense_t(d_upper, fup))
    d_hidden, g_gain2 = rms_back(hidden, inv2, gain2, d_normed2)
    d_attended = (d_branch + d_hidden).astype(jnp.bfloat16)
    g_outT = dense_g(d_attended, mixed)
    d_mixed = split(dense(d_attended, foutT))
    d_values = jnp.einsum("bhqk,bhqd->bhkd", probs_low, d_mixed, preferred_element_type=jnp.float32)
    d_values = join(d_values.astype(jnp.bfloat16))
    d_probs = jnp.einsum("bhqd,bhkd->bhqk", d_mixed, v, preferred_element_type=jnp.float32)
    d_scores = probs * (d_probs - jnp.sum(d_probs * probs, -1, keepdims=True))
    d_scores = d_scores.astype(jnp.bfloat16)
    d_q = jnp.einsum("bhqk,bhkd->bhqd", d_scores, k, preferred_element_type=jnp.float32) * scale
    d_k = jnp.einsum("bhqk,bhqd->bhkd", d_scores, q, preferred_element_type=jnp.float32) * scale
    d_q = join(d_q.astype(jnp.bfloat16))
    d_k = join(d_k.astype(jnp.bfloat16))
    g_q = dense_g(normed, d_q)
    g_k = dense_g(normed, d_k)
    g_v = dense_g(normed, d_values)
    d_normed = pair_sum(dense_t(d_q, fq) + dense_t(d_k, fk) + dense_t(d_values, fv))
    d_rows, g_gain1 = rms_back(rows_f, inv1, gain1, d_normed)
    g_route = jnp.sum(rows_f * d_logit[:, None], 0)
    d_half = (
        lax.dynamic_slice_in_dim(d_hidden + d_rows, offset, half_width, 1)
        + d_logit[:, None] * lax.dynamic_slice_in_dim(route_f32, offset, half_width, 0)[None, :]
    )
    grad_rows = (cot_half.astype(jnp.float32) + d_half).astype(jnp.bfloat16)

    seq_ids = lax.broadcasted_iota(jnp.int32, (batch, capacity), 0)
    output = tok.at[seq_ids, chosen].set(
        new_rows.reshape(batch, capacity, half_width), unique_indices=True
    )
    input_grad = cot.at[seq_ids, chosen].set(
        grad_rows.reshape(batch, capacity, half_width), unique_indices=True
    )

    g_vec = jnp.pad(jnp.stack([g_route, g_gain1, g_gain2], 1), ((0, 0), (0, 125)))
    grads = jnp.concatenate(
        [x.astype(jnp.bfloat16) for x in (g_q, g_k, g_v, g_up, g_outT, g_downT, g_vec)], 1
    )
    own = lax.psum_scatter(grads, "dp", scatter_dimension=0, tiled=True).astype(jnp.float32)
    return (
        output.reshape(tokens.shape),
        input_grad.reshape(tokens.shape),
        own[:, :b1],
        own[:, b1:b2],
        own[:, b2:b3],
        own[:, b4:b5].T,
        own[:, b3:b4],
        own[:, b5:b6].T,
        own[:, b6],
        own[:, b6 + 1],
        own[:, b6 + 2],
    )


MESH = pl.DeviceIdType.MESH
NB = 48
PATTERN = "XYZX"
PER = 4
GATHER_LAGS = {
    "X": (0, 3, 6, 9, 12, 18),
    "Y": (0, 3, 6, 9, 13, 18),
    "Z": (0, 3, 7, 11, 14, 17),
}
SCATTER_LAGS = {
    "X": (0, 4, 7, 9, 13, 18),
    "Y": (0, 5, 8, 10, 14, 17),
    "Z": (0, 1, 6, 10, 13, 18),
}
VECTOR_STEPS = (0, 3, 6, 9, 12, 15)


class Place:
    def __init__(self):
        me = lax.axis_index("dp")
        self.x = me % 2
        self.y = (me // 2) % 2
        self.z = me // 4
        self.nx = me + 1 - 2 * self.x
        self.ny = me + 2 - 4 * self.y
        self.up = jnp.minimum(me + 4, 15)
        self.dn = jnp.maximum(me - 4, 0)
        self.t = lax.axis_index("tensor")


def both(a, b):
    return jnp.logical_and(a, b)


def barrier(p, core):
    bar = pltpu.get_barrier_semaphore()

    def greet(dev):
        pl.semaphore_signal(bar, inc=1, device_id=dev, device_id_type=MESH)

    greet({"dp": p.nx})
    greet({"dp": p.ny})
    if core:
        greet({"tensor": 1 - p.t})

    @pl.when(p.z < 3)
    def _():
        greet({"dp": p.up})

    @pl.when(p.z > 0)
    def _():
        greet({"dp": p.dn})

    inner = both(p.z > 0, p.z < 3)
    base = 4 if core else 3

    @pl.when(inner)
    def _():
        pl.semaphore_wait(bar, base + 1)

    @pl.when(jnp.logical_not(inner))
    def _():
        pl.semaphore_wait(bar, base)


class Steps:
    def step(self, s, pos, static=None, guard=False):
        live = []
        for c, lags in self.lags.items():
            for j in range(6):
                q = (pos - lags[j]) % PER
                if PATTERN[q] == c and (static is None or 0 <= static - lags[j] < NB):
                    live.append((j, lags[j], q))
        live.sort(reverse=True)

        def do(j, lag, q, act):
            b = s - lag
            if guard:
                pl.when(b < NB)(lambda: act(b, q, j))
            else:
                act(b, q, j)

        for j, lag, q in live:
            if j > 0:
                do(j, lag, q, lambda b, q, j: self.recv(b, q, j - 1))
        for j, lag, q in live:
            if j < 5:
                do(j, lag, q, self.send)

    def drain(self, nb=NB):
        def body(r, _):
            for pos in range(PER):
                for j in range(5):
                    self.send(r * PER + pos, pos, j, act=lambda d: d.wait_send())
            return 0

        lax.fori_loop(0, nb // PER, body, 0)


class Gather(Steps):
    lags = GATHER_LAGS

    def __init__(self, p, W, ss, rs):
        self.p, self.W, self.ss, self.rs = p, W, ss, rs

    def copy(self, ref, b, k, dev):
        return pltpu.make_async_remote_copy(
            ref, ref, self.ss.at[b, k], self.rs.at[b, k], device_id={"dp": dev}, device_id_type=MESH
        )

    def zref(self, b, c, zz):
        zz = jnp.clip(zz, 0, 3)
        return self.W.at[b, zz] if c == "Z" else self.W.at[b, zz, self.p.y, self.p.x]

    def zsend(self, b, c, hop, act):
        p = self.p

        @pl.when(both(p.z - hop + 1 >= 0, p.z < 3))
        def _():
            act(self.copy(self.zref(b, c, p.z - hop + 1), b, hop - 1, p.up))

        @pl.when(both(p.z + hop - 1 <= 3, p.z > 0))
        def _():
            act(self.copy(self.zref(b, c, p.z + hop - 1), b, 2 + hop, p.dn))

    def zrecv(self, b, c, hop):
        p = self.p

        @pl.when(p.z - hop >= 0)
        def _():
            self.copy(self.zref(b, c, p.z - hop), b, hop - 1, p.nx).wait_recv()

        @pl.when(p.z + hop <= 3)
        def _():
            self.copy(self.zref(b, c, p.z + hop), b, 2 + hop, p.nx).wait_recv()

    def stage(self, b, c, j):
        W = self.W
        x, y, z = self.p.x, self.p.y, self.p.z
        if c == "X":
            line = (7, W.at[b, :, :, x], W.at[b, :, :, 1 - x])
            return (1, 2, 3, (6, W.at[b, :, y, x], W.at[b, :, 1 - y, x]), line)[j]
        if c == "Y":
            line = (6, W.at[b, :, y], W.at[b, :, 1 - y])
            return (1, 2, 3, (7, W.at[b, :, y, x], W.at[b, :, y, 1 - x]), line)[j]
        line = (7, W.at[b, z, y, x], W.at[b, z, y, 1 - x])
        return (line, (6, W.at[b, z, y], W.at[b, z, 1 - y]), 1, 2, 3)[j]

    def send(self, b, pos, j, act=lambda d: d.start()):
        c = PATTERN[pos]
        st = self.stage(b, c, j)
        if isinstance(st, int):
            self.zsend(b, c, st, act)
        else:
            act(self.copy(st[1], b, st[0], self.p.ny if st[0] == 6 else self.p.nx))

    def recv(self, b, pos, j):
        c = PATTERN[pos]
        st = self.stage(b, c, j)
        if isinstance(st, int):
            self.zrecv(b, c, st)
        else:
            self.copy(st[2], b, st[0], self.p.nx).wait_recv()


class Scatter(Steps):
    lags = SCATTER_LAGS

    def __init__(self, p, G, out, L8, L4, LZ, P4, P2, P1, ss, rs):
        self.p, self.G, self.out, self.ss, self.rs = p, G, out, ss, rs
        self.L8, self.L4, self.LZ, self.P4, self.P2, self.P1 = L8, L4, LZ, P4, P2, P1

    def slot(self, b, pos):
        r = b // PER
        return r if PATTERN[pos] == "Z" else r * 3 + {0: 0, 1: 1, 3: 2}[pos]

    def copy(self, src, dst, b, k, dev):
        return pltpu.make_async_remote_copy(
            src, dst, self.ss.at[b, k], self.rs.at[b, k], device_id={"dp": dev}, device_id_type=MESH
        )

    def gz(self, b, c, t):
        t = jnp.clip(t, 0, 3)
        return self.G.at[b, t] if c == "Z" else self.G.at[b, t, self.p.y, self.p.x]

    def lz(self, b, pos, k):
        i = self.slot(b, pos)
        return self.P4.at[i, k] if PATTERN[pos] == "Z" else self.LZ.at[i, k]

    def add(self, ref, land):
        ref[...] = (ref[...].astype(jnp.float32) + land[...].astype(jnp.float32)).astype(ref.dtype)

    def zsend(self, b, pos, hop, act):
        p, c = self.p, PATTERN[pos]

        @pl.when(p.z + hop <= 3)
        def _():
            act(self.copy(self.gz(b, c, p.z + hop), self.lz(b, pos, hop - 1), b, hop - 1, p.up))

        @pl.when(p.z - hop >= 0)
        def _():
            act(self.copy(self.gz(b, c, p.z - hop), self.lz(b, pos, 2 + hop), b, 2 + hop, p.dn))

    def zrecv(self, b, pos, hop, final):
        p, c = self.p, PATTERN[pos]

        def take(k, t):
            land = self.lz(b, pos, k)
            self.copy(land, land, b, k, p.nx).wait_recv()
            if not final:
                self.add(self.gz(b, c, t), land)

        if not final:

            @pl.when(both(p.z >= 1, p.z - 1 + hop <= 3))
            def _():
                take(hop - 1, p.z - 1 + hop)

            @pl.when(both(p.z <= 2, p.z + 1 - hop >= 0))
            def _():
                take(2 + hop, p.z + 1 - hop)

            return
        own = self.G.at[b, p.z, p.y, p.x]
        below, above = self.lz(b, pos, 0), self.lz(b, pos, 3)
        f32 = jnp.float32

        @pl.when(p.z == 0)
        def _():
            take(3, p.z)
            self.out[b] = own[...].astype(f32) + above[...].astype(f32)

        @pl.when(p.z == 3)
        def _():
            take(0, p.z)
            self.out[b] = own[...].astype(f32) + below[...].astype(f32)

        @pl.when(both(p.z > 0, p.z < 3))
        def _():
            take(0, p.z)
            take(3, p.z)
            self.out[b] = own[...].astype(f32) + below[...].astype(f32) + above[...].astype(f32)

    def stage(self, b, pos, j):
        G = self.G
        x, y, z = self.p.x, self.p.y, self.p.z
        c, i = PATTERN[pos], self.slot(b, pos)
        if c == "X":
            first = (7, G.at[b, :, :, 1 - x], self.L8.at[i], G.at[b, :, :, x])
            return (first, (6, G.at[b, :, 1 - y, x], self.L4.at[i], G.at[b, :, y, x]), 3, 2, 1)[j]
        if c == "Y":
            first = (6, G.at[b, :, 1 - y], self.L8.at[i], G.at[b, :, y])
            return (first, (7, G.at[b, :, y, 1 - x], self.L4.at[i], G.at[b, :, y, x]), 3, 2, 1)[j]
        last = (7, G.at[b, z, y, 1 - x], self.P1.at[i], G.at[b, z, y, x])
        return (3, 2, 1, (6, G.at[b, z, 1 - y], self.P2.at[i], G.at[b, z, y]), last)[j]

    def send(self, b, pos, j, act=lambda d: d.start()):
        st = self.stage(b, pos, j)
        if isinstance(st, int):
            self.zsend(b, pos, st, act)
        else:
            act(self.copy(st[1], st[2], b, st[0], self.p.ny if st[0] == 6 else self.p.nx))

    def recv(self, b, pos, j):
        st = self.stage(b, pos, j)
        if isinstance(st, int):
            self.zrecv(b, pos, st, PATTERN[pos] != "Z" and j == 4)
        else:
            self.copy(st[2], st[2], b, st[0], self.p.nx).wait_recv()
            if j == 4:
                self.out[b] = st[3][...].astype(jnp.float32) + st[2][...].astype(jnp.float32)
            else:
                self.add(st[3], st[2])

    @staticmethod
    def landing(blocks, tail, dtype):
        n, m = blocks // PER * 3, blocks // PER
        return [
            pltpu.VMEM(shape + tail, dtype)
            for shape in ((n, 4, 2), (n, 4), (n, 6), (m, 6, 2, 2), (m, 2), (m,))
        ] + [pltpu.SemaphoreType.DMA((blocks, 8))] * 2
EPS = 1e-05
SEQ = 4
CAP = 256
ROWS = SEQ * CAP
HBM = pl.ANY


def dot(a, b):
    return jnp.dot(a, b, preferred_element_type=jnp.float32)


def dot_nt(a, b):
    return lax.dot_general(a, b, (((1,), (1,)), ((), ())), preferred_element_type=jnp.float32)


def halves(ref, rs):
    return jnp.concatenate([ref[0, rs, :], ref[1, rs, :]], 1).astype(jnp.float32)


def wblocks(W, first, count):
    return jnp.concatenate([W[first + i].reshape(1024, 128) for i in range(count)], 1)


def seq_rows(i):
    return pl.ds(i * CAP, CAP)


def cut(i, n):
    return pl.ds(pl.multiple_of(i * n, n), n)


def head_masks():
    lane = lax.broadcasted_iota(jnp.int32, (CAP, 128), 1)
    one = jnp.where(lane < HD, 1.0, 0.0)
    return [one.astype(jnp.bfloat16), (1.0 - one).astype(jnp.bfloat16)], lane < HD


def causal_mask():
    shape = (CAP, CAP)
    return lax.broadcasted_iota(jnp.int32, shape, 0) >= lax.broadcasted_iota(jnp.int32, shape, 1)


def softmax_rows(q, k, mask):
    s = jnp.where(mask, dot_nt(q, k) * (HD**-0.5), -1e30)
    e = jnp.exp(s - jnp.max(s, -1, keepdims=True))
    return e * (1.0 / jnp.sum(e, -1, keepdims=True))


def inv_rms(v):
    return lax.rsqrt(jnp.mean(v * v, -1, keepdims=True) + EPS)


def gate_of(rows_f, route):
    return jax.nn.sigmoid(jnp.sum(rows_f * route, -1, keepdims=True))


def own_slot(p, W, b):
    return W.at[b, p.z, p.y, p.x]


def forward_kernel(
    idx_ref,
    tile_ref,
    tok_ref,
    cot_ref,
    wq,
    wk,
    wv,
    wo,
    wu,
    wd,
    o_rows,
    o_cot,
    o_nT,
    o_qkv,
    o_mix,
    o_P,
    o_R,
    o_down,
    o_back,
    o_W,
    o_G,
    o_vec,
    W,
    VB,
    vecs,
    rows,
    cot,
    tokbuf,
    onehot,
    nrm,
    nT,
    dd,
    ddT,
    qkv,
    mixed,
    P,
    R,
    dacc,
    nacc,
    act,
    dup,
    Gst,
    ss,
    rs,
    vss,
    vrs,
    hs,
    hr,
    asnd,
    arcv,
    first,
    load,
    outs,
    gout,
):
    p = Place()
    t = p.t
    other = {"tensor": 1 - t}
    f32, bf = jnp.float32, jnp.bfloat16

    own = [pltpu.make_async_copy(tile_ref, own_slot(p, VB, 0), first.at[NB])]
    for b in range(16):
        src, col = ((wq, wk, wv)[b % 3], b // 3) if b < 12 else (wo, b - 12)
        own.append(
            pltpu.make_async_copy(src.at[:, pl.ds(col * 128, 128)], own_slot(p, W, b), first.at[b])
        )
    for b in range(32):
        src = (wu, wd)[b % 4 // 2]
        own.append(
            pltpu.make_async_copy(
                src.at[:, pl.ds((b // 4 * 2 + b % 2) * 128, 128)],
                own_slot(p, W, 16 + b),
                first.at[16 + b],
            )
        )
    for c in own:
        c.start()

    units = [(a, i) for i in range(SEQ) for a in (0, 1)]

    def loader(u):
        a, i = units[u]
        return pltpu.make_async_copy((tok_ref, cot_ref)[a].at[i], tokbuf.at[u % 2], load.at[u % 2])

    loader(0).start()
    loader(1).start()
    barrier(p, True)
    for c in own:
        c.wait()
    W_steps = Gather(p, W, ss, rs)
    V_steps = Gather(p, VB, vss, vrs)

    def tick(s, guard=False):
        if isinstance(s, int):
            W_steps.step(s, s % PER, static=s)
            if s in VECTOR_STEPS:
                j = VECTOR_STEPS.index(s)
                if j > 0:
                    V_steps.recv(0, 0, j - 1)
                if j < 5:
                    V_steps.send(0, 0, j)

    def half_copy(u):
        a, i = units[u]
        ref = (rows, cot)[a].at[t, seq_rows(i)]
        return pltpu.make_async_remote_copy(
            ref, ref, hs.at[u], hr.at[u], device_id=other, device_id_type=MESH
        )

    def half_wait(u):
        a, i = units[u]
        ref = (rows, cot)[a].at[1 - t, seq_rows(i)]
        pltpu.make_async_remote_copy(
            ref, ref, hs.at[u], hr.at[u], device_id=other, device_id_type=MESH
        ).wait_recv()

    for u, (a, i) in enumerate(units):
        tick(2 * u)
        if a == 0:
            spot = idx_ref[seq_rows(i), :]
            hit = lax.broadcasted_iota(jnp.int32, (CAP, 2048), 1) == spot
            onehot[...] = jnp.where(hit, 1.0, 0.0).astype(bf)
        loader(u).wait()
        (rows, cot)[a][t, seq_rows(i), :] = dot(onehot[...], tokbuf[u % 2]).astype(bf)
        if u + 2 < 8:
            loader(u + 2).start()
        tick(2 * u + 1)
        if u > 0:
            half_copy(u - 1).start()
    half_copy(7).start()

    for z in range(4):
        for y in range(2):
            vecs[:, pl.ds((z * 2 + y) * 128, 128)] = VB[0, z, y, 0] + VB[0, z, y, 1]

    def saver(k, src, dst):
        return pltpu.make_async_copy(src, dst, outs.at[k])

    saved = [saver(0, vecs, o_vec)]
    saved[0].start()

    dacc[...] = jnp.zeros_like(dacc)
    nacc[...] = jnp.zeros_like(nacc)

    for i in range(SEQ):
        tick(16 + i)
        half_wait(2 * i)
        half_wait(2 * i + 1)

        def norm_part(n, _):
            rs_ = cut(i * 8 + n, 32)
            r = halves(rows, rs_)
            nrm[rs_, :] = (r * inv_rms(r) * vecs[1:2, :]).astype(bf)
            dd[rs_, :] = (gate_of(r, vecs[0:1, :]) * halves(cot, rs_)).astype(bf)
            return 0

        lax.fori_loop(0, 8, norm_part, 0)
        for c in range(4):
            cs = pl.ds(c * 256, 256)
            nT[cs, seq_rows(i)] = nrm[seq_rows(i), cs].T
            ddT[cs, seq_rows(i)] = dd[seq_rows(i), cs].T
    later = [saver(1, rows, o_rows), saver(2, cot, o_cot), saver(3, nT, o_nT)]
    for c in later:
        c.start()
    saved += later[:2]
    nT_saved = later[2]

    masks, low_half = head_masks()
    mask = causal_mask()

    def attend(i, hp):
        r_ = seq_rows(i)
        q, k, v = qkv[3 * hp, r_, :], qkv[3 * hp + 1, r_, :], qkv[3 * hp + 2, r_, :]
        mix = [dot(softmax_rows(q * masks[h], k, mask).astype(bf), v) for h in (0, 1)]
        mixed[hp, r_, :] = jnp.where(low_half, mix[0], mix[1]).astype(bf)

    def pair_part(hp, _):
        y = dot(nrm[...], wblocks(W, 3 * hp, 3)).astype(bf)
        for c in range(3):
            qkv[3 * hp + c] = y[:, c * 128 : c * 128 + 128]
        for i in range(SEQ):
            W_steps.step(20 + 4 * hp + i, i)
            attend(i, hp)
        return 0

    lax.fori_loop(0, 4, pair_part, 0)
    later = [saver(4, qkv, o_qkv), saver(5, mixed, o_mix)]
    for c in later:
        c.start()
    saved += later

    def att_copy(i):
        return pltpu.make_async_remote_copy(
            P.at[seq_rows(i)],
            R.at[seq_rows(i)],
            asnd.at[i],
            arcv.at[i],
            device_id=other,
            device_id_type=MESH,
        )

    def norm_mlp(i):
        att_copy(i).wait_recv()

        def norm_part(n, _):
            rs_ = cut(i * 8 + n, 32)
            h = halves(rows, rs_) + (P[rs_, :].astype(f32) + R[rs_, :].astype(f32))
            nrm[rs_, :] = (h * inv_rms(h) * vecs[2:3, :]).astype(bf)
            return 0

        lax.fori_loop(0, 8, norm_part, 0)
        for c in range(4):
            cs = pl.ds(c * 256, 256)
            nT[cs, seq_rows(i)] = nrm[seq_rows(i), cs].T

    out_w = wblocks(W, 12, 4)

    def project_out(i):
        mix = jnp.concatenate([mixed[h, seq_rows(i), :] for h in range(4)], 1)
        P[seq_rows(i), :] = dot_nt(mix, out_w).astype(bf)

    W_steps.step(36, 0)
    project_out(0)
    project_out(1)
    att_copy(0).start()
    W_steps.step(37, 1)
    project_out(2)
    att_copy(1).start()
    project_out(3)
    att_copy(2).start()
    nT_saved.wait()
    W_steps.step(38, 2)
    norm_mlp(0)
    att_copy(3).start()
    norm_mlp(1)
    W_steps.step(39, 3)
    norm_mlp(2)
    norm_mlp(3)
    saved.append(saver(6, W.at[pl.ds(0, 16)], o_W))
    saved[-1].start()
    later = [saver(7, P, o_P), saver(8, R, o_R)]
    for c in later:
        c.start()
    saved += later

    def g_copy(m):
        slot = lax.rem(m, 2)
        return pltpu.make_async_copy(Gst.at[slot], o_G.at[pl.ds(m * 4, 4)], gout.at[slot])

    def mlp_part(m, _):
        slot = lax.rem(m, 2)
        s = 40 + 4 * m
        up_w = wblocks(W, 16 + 4 * m, 2)
        down_w = wblocks(W, 18 + 4 * m, 2)
        for ht in range(2):
            hs_ = pl.ds(ht * 512, 512)
            W_steps.step(s + ht, ht, guard=True)
            u = dot(nrm[hs_, :], up_w)
            d = dot(dd[hs_, :], down_w)
            c0 = 0.7978845608028654
            u2 = u * u
            s1 = 1.0 + jnp.tanh(u * (c0 + (c0 * 0.044715) * u2))
            h = 0.5 * u
            act[hs_, :] = (h * s1).astype(bf)
            slope = s1 * (0.5 + h * (2.0 - s1) * (c0 + (3 * 0.044715 * c0) * u2))
            dup[hs_, :] = (d * slope).astype(bf)
        W_steps.step(s + 2, 2, guard=True)
        for ht in range(2):
            hs_ = pl.ds(ht * 512, 512)
            dacc[hs_, :] += dot_nt(act[hs_, :], down_w)
            nacc[hs_, :] += dot_nt(dup[hs_, :], up_w)
        W_steps.step(s + 3, 3, guard=True)

        @pl.when(m >= 2)
        def _():
            g_copy(m - 2).wait()

        for ht in range(2):
            hs_ = pl.ds(ht * 512, 512)
            gu = dot(nT[hs_, :], dup[...]).astype(bf)
            Gst[slot, 0, hs_, :] = gu[:, :128]
            Gst[slot, 1, hs_, :] = gu[:, 128:]
            gd = dot(ddT[hs_, :], act[...]).astype(bf)
            Gst[slot, 2, hs_, :] = gd[:, :128]
            Gst[slot, 3, hs_, :] = gd[:, 128:]
        g_copy(m).start()
        return 0

    lax.fori_loop(0, 8, mlp_part, 0)
    for e in range(2):
        for c in range(2):
            tokbuf[e, pl.ds(c * 1024, 1024), :] = (dacc, nacc)[e][:, c * 512 : c * 512 + 512].astype(bf)
            saved.append(
                saver(9 + 2 * e + c, tokbuf.at[e, pl.ds(c * 1024, 1024)], (o_down, o_back)[e].at[c])
            )
            saved[-1].start()
    for u in range(8):
        half_copy(u).wait_send()
    for i in range(SEQ):
        att_copy(i).wait_send()
    W_steps.drain()
    for j in range(5):
        V_steps.send(0, 0, j, act=lambda d: d.wait_send())
    g_copy(6).wait()
    g_copy(7).wait()
    for c in saved:
        c.wait()


def forward_call(chosen, tile, tok, cotangent, weights):
    bf, f32 = jnp.bfloat16, jnp.float32
    S = jax.ShapeDtypeStruct
    DMA = pltpu.SemaphoreType.DMA
    any_ = pl.BlockSpec(memory_space=HBM)
    vm = pltpu.VMEM
    return pl.pallas_call(
        forward_kernel,
        out_shape=(
            S((2, ROWS, 512), bf),
            S((2, ROWS, 512), bf),
            S((1024, ROWS), bf),
            S((12, ROWS, 128), bf),
            S((4, ROWS, 128), bf),
            S((ROWS, 1024), bf),
            S((ROWS, 1024), bf),
            S((2, ROWS, 512), bf),
            S((2, ROWS, 512), bf),
            S((16, 4, 2, 2, 64, 128), bf),
            S((32, 1024, 128), bf),
            S((8, 1024), f32),
        ),
        in_specs=[pl.BlockSpec(memory_space=pltpu.VMEM)] + [any_] * 9,
        out_specs=[any_] * 12,
        scratch_shapes=[
            vm((NB, 4, 2, 2, 64, 128), bf),
            vm((1, 4, 2, 2, 8, 128), f32),
            vm((8, 1024), f32),
            vm((2, ROWS, 512), bf),
            vm((2, ROWS, 512), bf),
            vm((2, 2048, 512), bf),
            vm((CAP, 2048), bf),
            vm((ROWS, 1024), bf),
            vm((1024, ROWS), bf),
            vm((ROWS, 1024), bf),
            vm((1024, ROWS), bf),
            vm((12, ROWS, 128), bf),
            vm((4, ROWS, 128), bf),
            vm((ROWS, 1024), bf),
            vm((ROWS, 1024), bf),
            vm((ROWS, 1024), f32),
            vm((ROWS, 1024), f32),
            vm((ROWS, 256), bf),
            vm((ROWS, 256), bf),
            vm((2, 4, 1024, 128), bf),
            DMA((NB, 8)),
            DMA((NB, 8)),
            DMA((1, 8)),
            DMA((1, 8)),
            DMA((8,)),
            DMA((8,)),
            DMA((4,)),
            DMA((4,)),
            DMA((NB + 1,)),
            DMA((2,)),
            DMA((13,)),
            DMA((2,)),
        ],
        compiler_params=pltpu.CompilerParams(
            collective_id=1, has_side_effects=True, vmem_limit_bytes=63 * 1024 * 1024
        ),
        name="forward",
    )(chosen, tile, tok, cotangent, *weights)


def backward_kernel(
    rows,
    cot,
    nT_in,
    qkv_in,
    mix_in,
    P_in,
    R_in,
    down_in,
    back_in,
    W_in,
    G_in,
    vec_in,
    o_newr,
    o_newg,
    o_sum,
    o_vec,
    G,
    Wa,
    qkv,
    mixed,
    nT,
    vecs,
    DR,
    NR,
    R1,
    bufs,
    buf2,
    da,
    daT,
    dmix,
    newr,
    newg,
    dhid,
    dlog,
    accs,
    GV,
    base,
    gsem,
    lsem,
    psem,
    prcv,
    qsem,
    qrcv,
    tout,
    *landing,
):
    p = Place()
    t = p.t
    other = {"tensor": 1 - t}
    f32, bf = jnp.float32, jnp.bfloat16
    wide, small = landing[:8], landing[8:]

    g_loads = [
        pltpu.make_async_copy(G_in.at[pl.ds(4 * c, 4)], G.at[pl.ds(4 * c, 4)], gsem.at[c])
        for c in range(8)
    ]
    g_loads[0].start()

    def stream(s, names):
        q = s % 2
        out = []
        for k in names:
            if k < 2:
                src = (P_in, R_in)[k].at[seq_rows(s)]
                dst = buf2.at[q, k]
            else:
                src = (rows, cot, down_in, back_in)[k - 2].at[:, seq_rows(s)]
                dst = bufs.at[q, k - 2]
            out.append(pltpu.make_async_copy(src, dst, lsem.at[q, k]))
        return out

    everything = (0, 1, 2, 3, 4, 5)
    for c in stream(0, everything):
        c.start()
    fixed = [
        pltpu.make_async_copy(a, b, base.at[i])
        for i, (a, b) in enumerate(
            ((vec_in, vecs), (W_in, Wa), (qkv_in, qkv), (mix_in, mixed), (nT_in, nT))
        )
    ]
    for c in fixed[:1]:
        c.start()
    for c in g_loads[1:]:
        c.start()
    barrier(p, True)

    def pair_copy(s, e):
        return pltpu.make_async_remote_copy(
            (down_in, back_in)[e].at[:, seq_rows(s)],
            (DR, NR)[e].at[:, seq_rows(s)],
            psem.at[s, e],
            prcv.at[s, e],
            device_id=other,
            device_id_type=MESH,
        )

    for s in range(SEQ):
        for e in range(2):
            pair_copy(s, e).start()
    for c in fixed[1:]:
        c.start()
    steps = Scatter(p, G, o_sum, *wide)
    v_steps = Scatter(p, GV, o_vec, *small)

    def tick(s):
        if s < 32 and s % 4 == 0:
            g_loads[s // 4].wait()
        steps.step(s, s % PER, static=s)

    accs[...] = jnp.zeros_like(accs)

    def fold(v):
        return jnp.sum(v.reshape(4, 8, 1024), 0)

    def pick(v):
        return jnp.where(t == 0, v[:, :512], v[:, 512:])

    masks, low_half = head_masks()
    seen = lax.broadcasted_iota(jnp.int32, (CAP, CAP), 0) <= lax.broadcasted_iota(
        jnp.int32, (CAP, CAP), 1
    )

    for s in range(SEQ):
        tick(4 * s)
        q = s % 2
        if s + 1 < SEQ:
            for c in stream(s + 1, everything):
                c.start()
        if s == 0:
            fixed[0].wait()
        for c in stream(s, everything):
            c.wait()
        for e in range(2):
            pair_copy(s, e).wait_recv()

        def part(n, _):
            rs_ = cut(n, 32)
            as_ = pl.ds(pl.multiple_of(s * CAP + n * 32, 32), 32)

            def mine(k):
                return jnp.concatenate([bufs[q, k, 0, rs_, :], bufs[q, k, 1, rs_, :]], 1).astype(f32)

            r, c = mine(0), mine(1)
            att = buf2[q, 0, rs_, :].astype(f32) + buf2[q, 1, rs_, :].astype(f32)
            h = r + att
            branch = att + (mine(2) + halves(DR, as_))
            dn = mine(3) + halves(NR, as_)
            inv = inv_rms(h)
            sc = dn * vecs[2:3, :]
            dh = inv * sc - h * (inv * inv * inv * jnp.mean(sc * h, -1, keepdims=True))
            gate = gate_of(r, vecs[0:1, :])
            dl = jnp.sum(c * branch, -1, keepdims=True) * (gate * (1.0 - gate))
            da[rs_, :] = (gate * c + dh).astype(bf)
            accs[2] += fold(dn * (h * inv))
            accs[0] += fold(r * dl)
            newr[as_, :] = pick(r + gate * branch).astype(bf)
            dhid[as_, :] = pick(dh)
            dlog[as_, :] = jnp.broadcast_to(dl, (32, 128))
            return 0

        lax.fori_loop(0, 8, part, 0)
        tick(4 * s + 1)
        for c in range(4):
            cs = pl.ds(c * 256, 256)
            daT[cs, seq_rows(s)] = da[:, cs].T
        if s == 0:
            for c in fixed[1:]:
                c.wait()
        dm = dot(da[...], wblocks(Wa, 12, 4)).astype(bf)
        for h in range(4):
            dmix[h] = dm[:, h * 128 : h * 128 + 128]

        def pair_back(hp):
            r_ = seq_rows(s)
            qh, kh, vh = [qkv[3 * hp + c, r_, :] for c in range(3)]
            dmh = dmix[hp]
            outs = []
            for h in (0, 1):
                sc = jnp.where(seen, dot_nt(kh, qh * masks[h]) * (HD**-0.5), -1e30)
                e = jnp.exp(sc - jnp.max(sc, 0, keepdims=True))
                pr = e * (1.0 / jnp.sum(e, 0, keepdims=True))
                dv = dot(pr.astype(bf), dmh)
                dp = dot_nt(vh * masks[h], dmh)
                ds = (pr * (dp - jnp.sum(dp * pr, 0, keepdims=True))).astype(bf)
                outs.append((dot(ds.T, kh), dot(ds, qh), dv))
            scale = HD**-0.5
            for i, (a, b) in enumerate(zip(*outs)):
                v = jnp.where(low_half, a, b)
                qkv[3 * hp + i, r_, :] = (v if i == 2 else v * scale).astype(bf)

        for half in range(2):
            tick(4 * s + 2 + half)

            def pair_part(e, _):
                pair_back(2 * half + e)
                return 0

            lax.fori_loop(0, 2, pair_part, 0)

    row_outs = [pltpu.make_async_copy(newr, o_newr, tout.at[0])]
    row_outs[0].start()

    def grad_unit(leftT, a, b, first):
        y = jnp.concatenate([a, b], 1)
        for ht in range(2):
            g = dot(leftT[pl.ds(ht * 512, 512), :], y).astype(bf)
            for c in range(2):
                G[first + c, pl.ds(ht * 2, 2)] = g[:, c * 128 : c * 128 + 128].reshape(
                    2, 2, 2, 64, 128
                )

    def back_copy(s):
        return pltpu.make_async_remote_copy(
            DR.at[:, seq_rows(s)],
            R1.at[:, seq_rows(s)],
            qsem.at[s],
            qrcv.at[s],
            device_id=other,
            device_id_type=MESH,
        )

    for c in stream(0, (2, 3)):
        c.start()
    for c in stream(1, (2, 3)):
        c.start()
    for s in range(SEQ):
        tick(16 + s)
        x = jnp.concatenate([qkv[i, seq_rows(s), :] for i in range(12)], 1)
        y = dot_nt(x, wblocks(Wa, 0, 12)).astype(bf)
        DR[0, seq_rows(s), :] = y[:, :512]
        DR[1, seq_rows(s), :] = y[:, 512:]
        if s > 0:
            back_copy(s - 1).start()
    tick(20)
    back_copy(3).start()
    grad_unit(daT, mixed[0], mixed[1], 32)
    tick(21)
    grad_unit(daT, mixed[2], mixed[3], 34)
    for g_load in g_loads[6:]:
        g_load.wait()

    def grad_part(n, _):
        for e in range(2):
            sn = 22 + 4 * n + 2 * e
            steps.step(sn, (2 + 2 * e) % 4)
            steps.step(sn + 1, (3 + 2 * e) % 4)
            j = 2 * n + e
            grad_unit(nT, qkv[2 * j], qkv[2 * j + 1], 36 + 2 * j)
        return 0

    lax.fori_loop(0, 2, grad_part, 0)
    for e in range(2):
        grad_unit(nT, qkv[8 + 2 * e], qkv[9 + 2 * e], 44 + 2 * e)
        steps.step(30 + e, 2 + e)

    route_half = jnp.where(t == 0, vecs[0:1, :512], vecs[0:1, 512:])
    for s in range(SEQ):
        steps.step(32 + 2 * s, 2 * s % 4)
        steps.step(33 + 2 * s, (2 * s + 1) % 4)
        q = s % 2
        for c in stream(s, (2, 3)):
            c.wait()
        back_copy(s).wait_recv()

        def part(n, _):
            rs_ = cut(n, 32)
            as_ = pl.ds(pl.multiple_of(s * CAP + n * 32, 32), 32)
            r = jnp.concatenate([bufs[q, 0, 0, rs_, :], bufs[q, 0, 1, rs_, :]], 1).astype(f32)
            dn = halves(DR, as_) + halves(R1, as_)
            inv = inv_rms(r)
            sc = dn * vecs[1:2, :]
            dr = inv * sc - r * (inv * inv * inv * jnp.mean(sc * r, -1, keepdims=True))
            accs[1] += fold(dn * (r * inv))
            dl = dlog[as_, :]
            dl = jnp.concatenate([dl, dl, dl, dl], 1)
            ch = bufs[q, 1, t, rs_, :].astype(f32)
            newg[as_, :] = (ch + (dhid[as_, :] + pick(dr) + dl * route_half)).astype(bf)
            return 0

        lax.fori_loop(0, 8, part, 0)
        if s + 2 < SEQ:
            for c in stream(s + 2, (2, 3)):
                c.start()

    for z in range(4):
        for y in range(2):
            cs = pl.ds((z * 2 + y) * 128, 128)
            tile = jnp.concatenate(
                [jnp.sum(accs[k, :, cs], 0, keepdims=True) for k in range(3)]
                + [jnp.zeros((5, 128), f32)],
                0,
            )
            GV[0, z, y, 0] = tile
            GV[0, z, y, 1] = tile
    for s in range(SEQ):
        back_copy(s).wait_send()
    row_outs.append(pltpu.make_async_copy(newg, o_newg, tout.at[1]))
    row_outs[1].start()
    v_steps.send(0, 0, 0)

    def rest(m, _):
        for e in range(4):
            steps.step(40 + 4 * m + e, e, guard=True)
        return 0

    lax.fori_loop(0, 4, rest, 0)
    for k, s in enumerate(range(56, 67)):
        tick(s)
        if k in (0, 2, 3, 5, 7):
            j = (0, 2, 3, 5, 7).index(k) + 1
            v_steps.recv(0, 0, j - 1)
            if j < 5:
                v_steps.send(0, 0, j)
    for c in row_outs:
        c.wait()
    for s in range(SEQ):
        for e in range(2):
            pair_copy(s, e).wait_send()
    for j in range(5):
        v_steps.send(0, 0, j, act=lambda d: d.wait_send())
    steps.drain()


def backward_call(kept):
    bf, f32 = jnp.bfloat16, jnp.float32
    S = jax.ShapeDtypeStruct
    DMA = pltpu.SemaphoreType.DMA
    any_ = pl.BlockSpec(memory_space=HBM)
    vspec = pl.BlockSpec(memory_space=pltpu.VMEM)
    vm = pltpu.VMEM
    return pl.pallas_call(
        backward_kernel,
        out_shape=(
            S((ROWS, 512), bf),
            S((ROWS, 512), bf),
            S((NB, 64, 128), f32),
            S((1, 8, 128), f32),
        ),
        in_specs=[any_] * 12,
        out_specs=[any_, any_, vspec, vspec],
        scratch_shapes=[
            vm((NB, 4, 2, 2, 64, 128), bf),
            vm((16, 4, 2, 2, 64, 128), bf),
            vm((12, ROWS, 128), bf),
            vm((4, ROWS, 128), bf),
            vm((1024, ROWS), bf),
            vm((8, 1024), f32),
            vm((2, ROWS, 512), bf),
            vm((2, ROWS, 512), bf),
            vm((2, ROWS, 512), bf),
            vm((2, 4, 2, CAP, 512), bf),
            vm((2, 2, CAP, 1024), bf),
            vm((CAP, 1024), bf),
            vm((1024, ROWS), bf),
            vm((4, CAP, 128), bf),
            vm((ROWS, 512), bf),
            vm((ROWS, 512), bf),
            vm((ROWS, 512), f32),
            vm((ROWS, 128), f32),
            vm((3, 8, 1024), f32),
            vm((1, 4, 2, 2, 8, 128), f32),
            DMA((5,)),
            DMA((8,)),
            DMA((2, 6)),
            DMA((4, 2)),
            DMA((4, 2)),
            DMA((4,)),
            DMA((4,)),
            DMA((2,)),
        ]
        + Scatter.landing(NB, (64, 128), bf)
        + Scatter.landing(PER, (8, 128), f32),
        compiler_params=pltpu.CompilerParams(
            collective_id=2, has_side_effects=True, vmem_limit_bytes=63 * 1024 * 1024
        ),
        name="backward",
    )(*kept)


def place_kernel(
    spot_ref,
    own_ref,
    newr,
    newg,
    tok,
    cot,
    o_tok,
    o_cot,
    g_q,
    g_k,
    g_v,
    g_out,
    g_up,
    g_down,
    old,
    out,
    new,
    came,
    went,
    nsem,
    gsem,
):
    bf = jnp.bfloat16

    def piece(n):
        return n // (2048 // SIZE), cut(n % (2048 // SIZE), SIZE)

    def load(n, a):
        i, rs = piece(n)
        return pltpu.make_async_copy((tok, cot)[a].at[i, rs], old.at[a, n], came.at[a, n])

    def store(n, a):
        i, rs = piece(n)
        return pltpu.make_async_copy(out.at[a, n], (o_tok, o_cot)[a].at[i, rs], went.at[a, n])

    pieces = SEQ * 2048 // SIZE
    news = [pltpu.make_async_copy((newr, newg)[a], new.at[a], nsem.at[a]) for a in range(2)]
    for c in news:
        c.start()

    def start(n, _):
        load(n, 0).start()
        load(n, 1).start()
        return 0

    lax.fori_loop(0, pieces, start, 0)

    moves = []
    for b in range(NB):
        if b < 32:
            ref, k = (g_up, g_down)[b % 4 // 2], b // 4 * 2 + b % 2
        else:
            ref, k = (g_out, b - 32) if b < 36 else ((g_q, g_k, g_v)[b % 3], (b - 36) // 3)
        moves.append(
            pltpu.make_async_copy(own_ref.at[b], ref.at[:, pl.ds(k * 128, 128)], gsem.at[b])
        )
    for c in moves:
        c.start()
    for c in news:
        c.wait()
    ones = jnp.ones((CAP, 128), bf)

    def place(n, _):
        i, _rs = piece(n)
        row = lax.broadcasted_iota(jnp.int32, (SIZE, CAP), 0) + n % (2048 // SIZE) * SIZE
        hit = jnp.where(row == spot_ref[i], 1.0, 0.0).astype(bf)
        kept = 1.0 - dot(hit, ones)
        kept = jnp.concatenate([kept, kept, kept, kept], 1).astype(bf)
        for a in range(2):
            moved = dot(hit, new[a, cut(i, CAP), :]).astype(bf)
            load(n, a).wait()
            out[a, n] = old[a, n] * kept + moved
            store(n, a).start()
        return 0

    lax.fori_loop(0, pieces, place, 0)

    def finish(n, _):
        store(n, 0).wait()
        store(n, 1).wait()
        return 0

    lax.fori_loop(0, pieces, finish, 0)
    for c in moves:
        c.wait()


SIZE = 1024


def place_call(spot, own, newr, newg, tok, cotangent):
    bf, f32 = jnp.bfloat16, jnp.float32
    S = jax.ShapeDtypeStruct
    DMA = pltpu.SemaphoreType.DMA
    any_ = pl.BlockSpec(memory_space=HBM)
    pieces = SEQ * 2048 // SIZE
    return pl.pallas_call(
        place_kernel,
        out_shape=(
            S((SEQ, 2048, 512), bf),
            S((SEQ, 2048, 512), bf),
            S((64, 512), f32),
            S((64, 512), f32),
            S((64, 512), f32),
            S((64, 512), f32),
            S((64, 2048), f32),
            S((64, 2048), f32),
        ),
        in_specs=[pl.BlockSpec(memory_space=pltpu.VMEM), any_, any_, any_, any_, any_],
        out_specs=[any_] * 8,
        scratch_shapes=[
            pltpu.VMEM((2, pieces, SIZE, 512), bf),
            pltpu.VMEM((2, pieces, SIZE, 512), bf),
            pltpu.VMEM((2, ROWS, 512), bf),
            DMA((2, pieces)),
            DMA((2, pieces)),
            DMA((2,)),
            DMA((NB,)),
        ],
        compiler_params=pltpu.CompilerParams(vmem_limit_bytes=48 * 1024 * 1024),
        name="place_rows",
    )(spot, own, newr, newg, tok, cotangent)


def to_tile(w_route, gain_attn, gain_mlp):
    v = jnp.stack([w_route, gain_attn, gain_mlp]).astype(jnp.float32)
    v = jnp.pad(v, ((0, 5), (0, 0)))
    z = jnp.zeros_like(v)
    odd = lax.axis_index("dp") % 2
    return jnp.where(odd == 0, jnp.concatenate([v, z], 1), jnp.concatenate([z, v], 1))


def fused(
    tokens,
    routed,
    w_query,
    w_key,
    w_value,
    w_out,
    w_up,
    w_down,
    w_route,
    gain_attn,
    gain_mlp,
    cotangent,
):
    tok = tokens.reshape(SEQ, 2048, 512)
    cot = cotangent.reshape(SEQ, 2048, 512)
    tile = to_tile(w_route, gain_attn, gain_mlp)
    weights = (w_query, w_key, w_value, w_out.T, w_up, w_down.T)
    kept = list(forward_call(routed.reshape(ROWS, 1), tile, tok, cot, weights))
    kept[10] = kept[10].reshape(32, 4, 2, 2, 64, 128)
    newr, newg, own, vec = backward_call(kept)
    odd = lax.axis_index("dp") % 2
    vec = jnp.where(odd == 0, vec[0, :3, :64], vec[0, :3, 64:])
    output, grad, g_q, g_k, g_v, g_out, g_up, g_down = place_call(
        routed.reshape(SEQ, 1, CAP), own, newr, newg, tok, cot
    )
    return (
        output.reshape(tokens.shape),
        grad.reshape(tokens.shape),
        g_q,
        g_k,
        g_v,
        g_out.T,
        g_up,
        g_down.T,
        vec[0],
        vec[1],
        vec[2],
    )


def shards(tokens, routed, *rest):
    sizes = (lax.axis_size("dp"), lax.axis_size("tensor"))
    here = tokens.shape == (4, 1, 2048, 512) and routed.shape == (4, 1, 256)
    if sizes == (16, 2) and here:
        return fused(tokens, routed, *rest)
    return plain(tokens, routed, *rest)


def solution(mesh):
    rows = P("dp", "tensor")
    columns = P("tensor", "dp")
    vector = P("dp")
    stored = P(None, "dp", None, "tensor")
    return jax.shard_map(
        shards,
        mesh=mesh,
        in_specs=(
            stored,
            P(None, "dp", None),
            rows,
            rows,
            rows,
            columns,
            rows,
            columns,
            vector,
            vector,
            vector,
            stored,
        ),
        out_specs=(
            stored,
            stored,
            rows,
            rows,
            rows,
            columns,
            rows,
            columns,
            vector,
            vector,
            vector,
        ),
        check_vma=False,
    )
```

```python
import jax
import jax.numpy as jnp
from jax import lax
from jax.experimental import pallas as pl
from jax.experimental.pallas import tpu as pltpu
from jax.sharding import PartitionSpec as P

HD = 64
eps_norm = 1e-05


def dense(left, right):
    return jnp.dot(left, right, preferred_element_type=jnp.float32)


def dense_t(left, right):
    return lax.dot_general(
        left, right, (((1,), (1,)), ((), ())), preferred_element_type=jnp.float32
    )


def dense_g(left, right):
    return lax.dot_general(
        left, right, (((0,), (0,)), ((), ())), preferred_element_type=jnp.float32
    )


def rms_back(values, inv, gain, grad):
    grad_gain = jnp.sum(grad * values * inv, 0)
    scaled = grad * gain
    dot = jnp.mean(scaled * values, -1, keepdims=True)
    return inv * scaled - values * (inv * inv * inv) * dot, grad_gain


def plain(
    tokens,
    routed,
    w_query,
    w_key,
    w_value,
    w_out,
    w_up,
    w_down,
    w_route,
    gain_attn,
    gain_mlp,
    cotangent,
):
    micro, seqs, length, half_width = tokens.shape
    capacity = routed.shape[2]
    batch = micro * seqs
    total = batch * capacity
    cols = w_query.shape[1]
    hidden_cols = w_up.shape[1]
    width = half_width * lax.axis_size("tensor")
    offset = lax.axis_index("tensor") * half_width
    scale = HD ** (-0.5)
    swap = [(0, 1), (1, 0)]

    vec = jnp.stack([w_route, gain_attn, gain_mlp], 1)
    vec = jnp.pad(vec, ((0, 0), (0, 125)))
    packed = jnp.concatenate([w_query, w_key, w_value, w_up, w_out.T, w_down.T, vec], 1)
    gathered = lax.all_gather(packed, "dp", axis=0, tiled=True)
    b1, b2, b3 = cols, 2 * cols, 3 * cols
    b4 = b3 + hidden_cols
    b5 = b4 + w_out.shape[0]
    b6 = b5 + w_down.shape[0]
    fq = gathered[:, :b1]
    fk = gathered[:, b1:b2]
    fv = gathered[:, b2:b3]
    fup = gathered[:, b3:b4]
    foutT = gathered[:, b4:b5]
    fdownT = gathered[:, b5:b6]
    route = gathered[:, b6]
    route_f32 = route.astype(jnp.float32)
    gain1 = gathered[:, b6 + 1].astype(jnp.float32)
    gain2 = gathered[:, b6 + 2].astype(jnp.float32)

    tok = tokens.reshape(batch, length, half_width)
    cot = cotangent.reshape(batch, length, half_width)
    chosen = routed.reshape(batch, capacity)
    rows_half = jnp.take_along_axis(tok, chosen[:, :, None], axis=1).reshape(total, half_width)
    cot_half = jnp.take_along_axis(cot, chosen[:, :, None], axis=1).reshape(total, half_width)
    rows = lax.all_gather(rows_half, "tensor", axis=1, tiled=True)
    cot_rows = lax.all_gather(cot_half, "tensor", axis=1, tiled=True)

    rows_f = rows.astype(jnp.float32)
    cot_f = cot_rows.astype(jnp.float32)
    gate = jax.nn.sigmoid(dense(rows, route))
    inv1 = lax.rsqrt(jnp.mean(rows_f * rows_f, -1, keepdims=True) + eps_norm)
    normed = (rows_f * inv1 * gain1).astype(jnp.bfloat16)
    heads = cols // HD

    def split(x):
        return x.astype(jnp.bfloat16).reshape(batch, capacity, heads, HD).transpose(0, 2, 1, 3)

    def join(x):
        return x.transpose(0, 2, 1, 3).reshape(total, cols)

    q = split(dense(normed, fq))
    k = split(dense(normed, fk))
    v = split(dense(normed, fv))
    causal = lax.broadcasted_iota(jnp.int32, (capacity, capacity), 0) >= lax.broadcasted_iota(
        jnp.int32, (capacity, capacity), 1
    )
    scores = jnp.einsum("bhqd,bhkd->bhqk", q, k, preferred_element_type=jnp.float32) * scale
    scores = jnp.where(causal, scores, -1e30)
    peak = jnp.max(scores, -1, keepdims=True)
    expd = jnp.exp(scores - peak)
    probs = expd / jnp.sum(expd, -1, keepdims=True)
    probs_low = probs.astype(jnp.bfloat16)
    mixed = jnp.einsum("bhqk,bhkd->bhqd", probs_low, v, preferred_element_type=jnp.float32)
    mixed = join(mixed.astype(jnp.bfloat16))

    def pair_sum(x):
        low = x.astype(jnp.bfloat16)
        other = lax.ppermute(low, "tensor", swap)
        return low.astype(jnp.float32) + other.astype(jnp.float32)

    attended = pair_sum(dense_t(mixed, foutT))
    hidden = rows_f + attended
    inv2 = lax.rsqrt(jnp.mean(hidden * hidden, -1, keepdims=True) + eps_norm)
    normed2 = (hidden * inv2 * gain2).astype(jnp.bfloat16)
    up = dense(normed2, fup)
    act32, gelu_back = jax.vjp(jax.nn.gelu, up)
    act = act32.astype(jnp.bfloat16)
    down = pair_sum(dense_t(act, fdownT))
    branch = attended + down
    d_logit = jnp.sum(cot_f * branch, -1) * gate * (1.0 - gate)
    branch_half = lax.dynamic_slice_in_dim(branch, offset, half_width, 1)
    new_rows = (rows_half.astype(jnp.float32) + gate[:, None] * branch_half).astype(jnp.bfloat16)

    d_branch = gate[:, None] * cot_f
    d_down = d_branch.astype(jnp.bfloat16)
    g_downT = dense_g(d_down, act)
    d_act = dense(d_down, fdownT)
    d_upper = gelu_back(d_act)[0].astype(jnp.bfloat16)
    g_up = dense_g(normed2, d_upper)
    d_normed2 = pair_sum(dense_t(d_upper, fup))
    d_hidden, g_gain2 = rms_back(hidden, inv2, gain2, d_normed2)
    d_attended = (d_branch + d_hidden).astype(jnp.bfloat16)
    g_outT = dense_g(d_attended, mixed)
    d_mixed = split(dense(d_attended, foutT))
    d_values = jnp.einsum("bhqk,bhqd->bhkd", probs_low, d_mixed, preferred_element_type=jnp.float32)
    d_values = join(d_values.astype(jnp.bfloat16))
    d_probs = jnp.einsum("bhqd,bhkd->bhqk", d_mixed, v, preferred_element_type=jnp.float32)
    d_scores = probs * (d_probs - jnp.sum(d_probs * probs, -1, keepdims=True))
    d_scores = d_scores.astype(jnp.bfloat16)
    d_q = jnp.einsum("bhqk,bhkd->bhqd", d_scores, k, preferred_element_type=jnp.float32) * scale
    d_k = jnp.einsum("bhqk,bhqd->bhkd", d_scores, q, preferred_element_type=jnp.float32) * scale
    d_q = join(d_q.astype(jnp.bfloat16))
    d_k = join(d_k.astype(jnp.bfloat16))
    g_q = dense_g(normed, d_q)
    g_k = dense_g(normed, d_k)
    g_v = dense_g(normed, d_values)
    d_normed = pair_sum(dense_t(d_q, fq) + dense_t(d_k, fk) + dense_t(d_values, fv))
    d_rows, g_gain1 = rms_back(rows_f, inv1, gain1, d_normed)
    g_route = jnp.sum(rows_f * d_logit[:, None], 0)
    d_half = (
        lax.dynamic_slice_in_dim(d_hidden + d_rows, offset, half_width, 1)
        + d_logit[:, None] * lax.dynamic_slice_in_dim(route_f32, offset, half_width, 0)[None, :]
    )
    grad_rows = (cot_half.astype(jnp.float32) + d_half).astype(jnp.bfloat16)

    seq_ids = lax.broadcasted_iota(jnp.int32, (batch, capacity), 0)
    output = tok.at[seq_ids, chosen].set(
        new_rows.reshape(batch, capacity, half_width), unique_indices=True
    )
    input_grad = cot.at[seq_ids, chosen].set(
        grad_rows.reshape(batch, capacity, half_width), unique_indices=True
    )

    g_vec = jnp.pad(jnp.stack([g_route, g_gain1, g_gain2], 1), ((0, 0), (0, 125)))
    grads = jnp.concatenate(
        [x.astype(jnp.bfloat16) for x in (g_q, g_k, g_v, g_up, g_outT, g_downT, g_vec)], 1
    )
    own = lax.psum_scatter(grads, "dp", scatter_dimension=0, tiled=True).astype(jnp.float32)
    return (
        output.reshape(tokens.shape),
        input_grad.reshape(tokens.shape),
        own[:, :b1],
        own[:, b1:b2],
        own[:, b2:b3],
        own[:, b4:b5].T,
        own[:, b3:b4],
        own[:, b5:b6].T,
        own[:, b6],
        own[:, b6 + 1],
        own[:, b6 + 2],
    )


MESH = pl.DeviceIdType.MESH
NB = 48
PATTERN = "XYZX"
PER = 4
GATHER_LAGS = {
    "X": (0, 3, 6, 9, 12, 19),
    "Y": (0, 3, 7, 9, 13, 17),
    "Z": (0, 3, 8, 11, 14, 17),
}
SCATTER_LAGS = {
    "X": (0, 4, 8, 9, 13, 18),
    "Y": (0, 5, 8, 9, 13, 18),
    "Z": (0, 2, 5, 9, 13, 18),
}
VECTOR_STEPS = (0, 3, 6, 9, 12, 15)


class Place:
    def __init__(self):
        me = lax.axis_index("dp")
        self.x = me % 2
        self.y = (me // 2) % 2
        self.z = me // 4
        self.nx = me + 1 - 2 * self.x
        self.ny = me + 2 - 4 * self.y
        self.up = jnp.minimum(me + 4, 15)
        self.dn = jnp.maximum(me - 4, 0)
        self.t = lax.axis_index("tensor")


def both(a, b):
    return jnp.logical_and(a, b)


def barrier(p, core):
    bar = pltpu.get_barrier_semaphore()

    def greet(dev):
        pl.semaphore_signal(bar, inc=1, device_id=dev, device_id_type=MESH)

    greet({"dp": p.nx})
    greet({"dp": p.ny})
    if core:
        greet({"tensor": 1 - p.t})

    @pl.when(p.z < 3)
    def _():
        greet({"dp": p.up})

    @pl.when(p.z > 0)
    def _():
        greet({"dp": p.dn})

    inner = both(p.z > 0, p.z < 3)
    base = 4 if core else 3

    @pl.when(inner)
    def _():
        pl.semaphore_wait(bar, base + 1)

    @pl.when(jnp.logical_not(inner))
    def _():
        pl.semaphore_wait(bar, base)


class Steps:
    def step(self, s, pos, static=None, low=False, high=False):
        live = []
        for c, lags in self.lags.items():
            for j in range(6):
                q = (pos - lags[j]) % PER
                if PATTERN[q] == c and (static is None or 0 <= static - lags[j] < NB):
                    live.append((j, lags[j], q))
        live.sort(reverse=True)

        def do(j, lag, q, act):
            b = s - lag
            if low:
                pl.when(b >= 0)(lambda: act(b, q, j))
            elif high:
                pl.when(b < NB)(lambda: act(b, q, j))
            else:
                act(b, q, j)

        for j, lag, q in live:
            if j > 0:
                do(j, lag, q, lambda b, q, j: self.recv(b, q, j - 1))
        for j, lag, q in live:
            if j < 5:
                do(j, lag, q, self.send)

    def drain(self, first, last):
        def body(r, _):
            for pos in range(PER):
                for j in range(5):
                    self.send(r * PER + pos, pos, j, act=lambda d: d.wait_send())
            return 0

        lax.fori_loop(first, last, body, 0)


class Gather(Steps):
    lags = GATHER_LAGS

    def __init__(self, p, W, ss, rs):
        self.p, self.W, self.ss, self.rs = p, W, ss, rs

    def copy(self, ref, b, k, dev):
        return pltpu.make_async_remote_copy(
            ref, ref, self.ss.at[b, k], self.rs.at[b, k], device_id={"dp": dev}, device_id_type=MESH
        )

    def zref(self, b, c, zz):
        zz = jnp.clip(zz, 0, 3)
        return self.W.at[b, zz] if c == "Z" else self.W.at[b, zz, self.p.y, self.p.x]

    def zsend(self, b, c, hop, act):
        p = self.p

        @pl.when(both(p.z - hop + 1 >= 0, p.z < 3))
        def _():
            act(self.copy(self.zref(b, c, p.z - hop + 1), b, hop - 1, p.up))

        @pl.when(both(p.z + hop - 1 <= 3, p.z > 0))
        def _():
            act(self.copy(self.zref(b, c, p.z + hop - 1), b, 2 + hop, p.dn))

    def zrecv(self, b, c, hop):
        p = self.p

        @pl.when(p.z - hop >= 0)
        def _():
            self.copy(self.zref(b, c, p.z - hop), b, hop - 1, p.nx).wait_recv()

        @pl.when(p.z + hop <= 3)
        def _():
            self.copy(self.zref(b, c, p.z + hop), b, 2 + hop, p.nx).wait_recv()

    def stage(self, b, c, j):
        W = self.W
        x, y, z = self.p.x, self.p.y, self.p.z
        if c == "X":
            line = (7, W.at[b, :, :, x], W.at[b, :, :, 1 - x])
            return (1, 2, 3, (6, W.at[b, :, y, x], W.at[b, :, 1 - y, x]), line)[j]
        if c == "Y":
            line = (6, W.at[b, :, y], W.at[b, :, 1 - y])
            return (1, 2, 3, (7, W.at[b, :, y, x], W.at[b, :, y, 1 - x]), line)[j]
        line = (7, W.at[b, z, y, x], W.at[b, z, y, 1 - x])
        return (line, (6, W.at[b, z, y], W.at[b, z, 1 - y]), 1, 2, 3)[j]

    def send(self, b, pos, j, act=lambda d: d.start()):
        c = PATTERN[pos]
        st = self.stage(b, c, j)
        if isinstance(st, int):
            self.zsend(b, c, st, act)
        else:
            act(self.copy(st[1], b, st[0], self.p.ny if st[0] == 6 else self.p.nx))

    def recv(self, b, pos, j):
        c = PATTERN[pos]
        st = self.stage(b, c, j)
        if isinstance(st, int):
            self.zrecv(b, c, st)
        else:
            self.copy(st[2], b, st[0], self.p.nx).wait_recv()


class Scatter(Steps):
    lags = SCATTER_LAGS

    def __init__(self, p, G, out, L8, L4, LZ, P4, P2, P1, ss, rs):
        self.p, self.G, self.out, self.ss, self.rs = p, G, out, ss, rs
        self.L8, self.L4, self.LZ, self.P4, self.P2, self.P1 = L8, L4, LZ, P4, P2, P1

    def slot(self, b, pos):
        r = b // PER
        return r if PATTERN[pos] == "Z" else r * 3 + {0: 0, 1: 1, 3: 2}[pos]

    def copy(self, src, dst, b, k, dev):
        return pltpu.make_async_remote_copy(
            src, dst, self.ss.at[b, k], self.rs.at[b, k], device_id={"dp": dev}, device_id_type=MESH
        )

    def gz(self, b, c, t):
        t = jnp.clip(t, 0, 3)
        return self.G.at[b, t] if c == "Z" else self.G.at[b, t, self.p.y, self.p.x]

    def lz(self, b, pos, k):
        i = self.slot(b, pos)
        return self.P4.at[i, k] if PATTERN[pos] == "Z" else self.LZ.at[i, k]

    def add(self, ref, land):
        ref[...] = (ref[...].astype(jnp.float32) + land[...].astype(jnp.float32)).astype(ref.dtype)

    def zsend(self, b, pos, hop, act):
        p, c = self.p, PATTERN[pos]

        @pl.when(p.z + hop <= 3)
        def _():
            act(self.copy(self.gz(b, c, p.z + hop), self.lz(b, pos, hop - 1), b, hop - 1, p.up))

        @pl.when(p.z - hop >= 0)
        def _():
            act(self.copy(self.gz(b, c, p.z - hop), self.lz(b, pos, 2 + hop), b, 2 + hop, p.dn))

    def zrecv(self, b, pos, hop, final):
        p, c = self.p, PATTERN[pos]

        def take(k, t):
            land = self.lz(b, pos, k)
            self.copy(land, land, b, k, p.nx).wait_recv()
            if not final:
                self.add(self.gz(b, c, t), land)

        if not final:

            @pl.when(both(p.z >= 1, p.z - 1 + hop <= 3))
            def _():
                take(hop - 1, p.z - 1 + hop)

            @pl.when(both(p.z <= 2, p.z + 1 - hop >= 0))
            def _():
                take(2 + hop, p.z + 1 - hop)

            return
        own = self.G.at[b, p.z, p.y, p.x]
        below, above = self.lz(b, pos, 0), self.lz(b, pos, 3)
        f32 = jnp.float32

        @pl.when(p.z == 0)
        def _():
            take(3, p.z)
            self.out[b] = own[...].astype(f32) + above[...].astype(f32)

        @pl.when(p.z == 3)
        def _():
            take(0, p.z)
            self.out[b] = own[...].astype(f32) + below[...].astype(f32)

        @pl.when(both(p.z > 0, p.z < 3))
        def _():
            take(0, p.z)
            take(3, p.z)
            self.out[b] = own[...].astype(f32) + below[...].astype(f32) + above[...].astype(f32)

    def stage(self, b, pos, j):
        G = self.G
        x, y, z = self.p.x, self.p.y, self.p.z
        c, i = PATTERN[pos], self.slot(b, pos)
        if c == "X":
            first = (7, G.at[b, :, :, 1 - x], self.L8.at[i], G.at[b, :, :, x])
            return (first, (6, G.at[b, :, 1 - y, x], self.L4.at[i], G.at[b, :, y, x]), 3, 2, 1)[j]
        if c == "Y":
            first = (6, G.at[b, :, 1 - y], self.L8.at[i], G.at[b, :, y])
            return (first, (7, G.at[b, :, y, 1 - x], self.L4.at[i], G.at[b, :, y, x]), 3, 2, 1)[j]
        last = (7, G.at[b, z, y, 1 - x], self.P1.at[i], G.at[b, z, y, x])
        return (3, 2, 1, (6, G.at[b, z, 1 - y], self.P2.at[i], G.at[b, z, y]), last)[j]

    def send(self, b, pos, j, act=lambda d: d.start()):
        st = self.stage(b, pos, j)
        if isinstance(st, int):
            self.zsend(b, pos, st, act)
        else:
            act(self.copy(st[1], st[2], b, st[0], self.p.ny if st[0] == 6 else self.p.nx))

    def recv(self, b, pos, j):
        st = self.stage(b, pos, j)
        if isinstance(st, int):
            self.zrecv(b, pos, st, PATTERN[pos] != "Z" and j == 4)
        else:
            self.copy(st[2], st[2], b, st[0], self.p.nx).wait_recv()
            if j == 4:
                self.out[b] = st[3][...].astype(jnp.float32) + st[2][...].astype(jnp.float32)
            else:
                self.add(st[3], st[2])

    @staticmethod
    def landing(blocks, tail, dtype):
        n, m = blocks // PER * 3, blocks // PER
        return [
            pltpu.VMEM(shape + tail, dtype)
            for shape in ((n, 4, 2), (n, 4), (n, 6), (m, 6, 2, 2), (m, 2), (m,))
        ] + [pltpu.SemaphoreType.DMA((blocks, 8))] * 2
EPS = 1e-05
SEQ = 4
CAP = 256
ROWS = SEQ * CAP
HBM = pl.ANY


def dot(a, b):
    return jnp.dot(a, b, preferred_element_type=jnp.float32)


def dot_nt(a, b):
    return lax.dot_general(a, b, (((1,), (1,)), ((), ())), preferred_element_type=jnp.float32)


def halves(ref, rs):
    return jnp.concatenate([ref[0, rs, :], ref[1, rs, :]], 1).astype(jnp.float32)


def wblocks(W, first, count):
    return jnp.concatenate([W[first + i].reshape(1024, 128) for i in range(count)], 1)


def seq_rows(i):
    return pl.ds(i * CAP, CAP)


def cut(i, n):
    return pl.ds(pl.multiple_of(i * n, n), n)


def head_masks():
    lane = lax.broadcasted_iota(jnp.int32, (CAP, 128), 1)
    one = jnp.where(lane < HD, 1.0, 0.0)
    return [one.astype(jnp.bfloat16), (1.0 - one).astype(jnp.bfloat16)], lane < HD


def causal_mask():
    shape = (CAP, CAP)
    return lax.broadcasted_iota(jnp.int32, shape, 0) >= lax.broadcasted_iota(jnp.int32, shape, 1)


def softmax_rows(q, k, mask):
    s = jnp.where(mask, dot_nt(q, k) * (HD**-0.5), -1e30)
    e = jnp.exp(s - jnp.max(s, -1, keepdims=True))
    return e * (1.0 / jnp.sum(e, -1, keepdims=True))


def inv_rms(v):
    return lax.rsqrt(jnp.mean(v * v, -1, keepdims=True) + EPS)


def gate_of(rows_f, route):
    return jax.nn.sigmoid(jnp.sum(rows_f * route, -1, keepdims=True))


def own_slot(p, W, b):
    return W.at[b, p.z, p.y, p.x]


def forward_kernel(
    spot_ref,
    tile_ref,
    tok_ref,
    cot_ref,
    wq,
    wk,
    wv,
    wo,
    wu,
    wd,
    o_rows,
    o_cot,
    o_nT,
    o_qkv,
    o_mix,
    o_P,
    o_R,
    o_down,
    o_back,
    o_W,
    o_G,
    o_vec,
    W,
    VB,
    vecs,
    rows,
    cot,
    tokbuf,
    onehot,
    nrm,
    nT,
    dd,
    ddT,
    qkv,
    mixed,
    P,
    R,
    dacc,
    nacc,
    act,
    dup,
    Gst,
    ss,
    rs,
    vss,
    vrs,
    hs,
    hr,
    asnd,
    arcv,
    first,
    load,
    outs,
    gout,
):
    p = Place()
    t = p.t
    other = {"tensor": 1 - t}
    f32, bf = jnp.float32, jnp.bfloat16

    own = [pltpu.make_async_copy(tile_ref, own_slot(p, VB, 0), first.at[NB])]
    for b in range(16):
        src, col = ((wq, wk, wv)[b % 3], b // 3) if b < 12 else (wo, b - 12)
        own.append(
            pltpu.make_async_copy(src.at[:, pl.ds(col * 128, 128)], own_slot(p, W, b), first.at[b])
        )
    for b in range(32):
        src = (wu, wd)[b % 4 // 2]
        own.append(
            pltpu.make_async_copy(
                src.at[:, pl.ds((b // 4 * 2 + b % 2) * 128, 128)],
                own_slot(p, W, 16 + b),
                first.at[16 + b],
            )
        )
    for c in own:
        c.start()

    def loader(i, a):
        return pltpu.make_async_copy((tok_ref, cot_ref)[a].at[i], tokbuf.at[a], load.at[a])

    loader(0, 0).start()
    loader(0, 1).start()
    barrier(p, True)
    for c in own:
        c.wait()
    W_steps = Gather(p, W, ss, rs)
    V_steps = Gather(p, VB, vss, vrs)

    def half_copy(i, a):
        ref = (rows, cot)[a].at[t, cut(i, CAP)]
        return pltpu.make_async_remote_copy(
            ref, ref, hs.at[i, a], hr.at[i, a], device_id=other, device_id_type=MESH
        )

    def half_wait(i, a):
        ref = (rows, cot)[a].at[1 - t, seq_rows(i)]
        pltpu.make_async_remote_copy(
            ref, ref, hs.at[i, a], hr.at[i, a], device_id=other, device_id_type=MESH
        ).wait_recv()

    def gather_part(i, _):
        def tick(q):
            W_steps.step(4 * i + q, q, low=True)
            for j, s in enumerate(VECTOR_STEPS):
                if s % 4 == q:

                    @pl.when(i == s // 4)
                    def _():
                        if j > 0:
                            V_steps.recv(0, 0, j - 1)
                        if j < 5:
                            V_steps.send(0, 0, j)

        for a in range(2):
            tick(2 * a)
            if a == 0:
                spot = jnp.broadcast_to(spot_ref[i], (128, CAP)).T[:, :1]
                hit = lax.broadcasted_iota(jnp.int32, (CAP, 2048), 1) == spot
                onehot[...] = jnp.where(hit, 1.0, 0.0).astype(bf)
            loader(i, a).wait()
            (rows, cot)[a][t, cut(i, CAP), :] = dot(onehot[...], tokbuf[a]).astype(bf)
            pl.when(i < 3)(lambda: loader(i + 1, a).start())
            tick(2 * a + 1)
            if a == 0:
                pl.when(i > 0)(lambda: half_copy(i - 1, 1).start())
            else:
                half_copy(i, 0).start()
        return 0

    lax.fori_loop(0, 4, gather_part, 0)
    half_copy(3, 1).start()

    for z in range(4):
        for y in range(2):
            vecs[:, pl.ds((z * 2 + y) * 128, 128)] = VB[0, z, y, 0] + VB[0, z, y, 1]

    def saver(k, src, dst):
        return pltpu.make_async_copy(src, dst, outs.at[k])

    saved = [saver(0, vecs, o_vec)]
    saved[0].start()

    dacc[...] = jnp.zeros_like(dacc)
    nacc[...] = jnp.zeros_like(nacc)

    for i in range(SEQ):
        W_steps.step(16 + i, i, static=16 + i)
        half_wait(i, 0)
        half_wait(i, 1)

        def norm_part(n, _):
            rs_ = cut(i * 8 + n, 32)
            r = halves(rows, rs_)
            nrm[rs_, :] = (r * inv_rms(r) * vecs[1:2, :]).astype(bf)
            dd[rs_, :] = (gate_of(r, vecs[0:1, :]) * halves(cot, rs_)).astype(bf)
            return 0

        lax.fori_loop(0, 8, norm_part, 0)
        for c in range(4):
            cs = pl.ds(c * 256, 256)
            nT[cs, seq_rows(i)] = nrm[seq_rows(i), cs].T
            ddT[cs, seq_rows(i)] = dd[seq_rows(i), cs].T
    later = [saver(1, rows, o_rows), saver(2, cot, o_cot), saver(3, nT, o_nT)]
    for c in later:
        c.start()
    saved += later[:2]
    nT_saved = later[2]

    masks, low_half = head_masks()
    mask = causal_mask()

    def attend(i, hp):
        r_ = seq_rows(i)
        q, k, v = qkv[3 * hp, r_, :], qkv[3 * hp + 1, r_, :], qkv[3 * hp + 2, r_, :]
        mix = [dot(softmax_rows(q * masks[h], k, mask).astype(bf), v) for h in (0, 1)]
        mixed[hp, r_, :] = jnp.where(low_half, mix[0], mix[1]).astype(bf)

    def pair_part(hp, _):
        y = dot(nrm[...], wblocks(W, 3 * hp, 3)).astype(bf)
        for c in range(3):
            qkv[3 * hp + c] = y[:, c * 128 : c * 128 + 128]
        for i in range(SEQ):
            W_steps.step(20 + 4 * hp + i, i)
            attend(i, hp)
        return 0

    lax.fori_loop(0, 4, pair_part, 0)
    later = [saver(4, qkv, o_qkv), saver(5, mixed, o_mix)]
    for c in later:
        c.start()
    saved += later

    def att_copy(i):
        return pltpu.make_async_remote_copy(
            P.at[seq_rows(i)],
            R.at[seq_rows(i)],
            asnd.at[i],
            arcv.at[i],
            device_id=other,
            device_id_type=MESH,
        )

    def norm_mlp(i):
        att_copy(i).wait_recv()

        def norm_part(n, _):
            rs_ = cut(i * 8 + n, 32)
            h = halves(rows, rs_) + (P[rs_, :].astype(f32) + R[rs_, :].astype(f32))
            nrm[rs_, :] = (h * inv_rms(h) * vecs[2:3, :]).astype(bf)
            return 0

        lax.fori_loop(0, 8, norm_part, 0)
        for c in range(4):
            cs = pl.ds(c * 256, 256)
            nT[cs, seq_rows(i)] = nrm[seq_rows(i), cs].T

    out_w = wblocks(W, 12, 4)

    def project_out(i):
        mix = jnp.concatenate([mixed[h, seq_rows(i), :] for h in range(4)], 1)
        P[seq_rows(i), :] = dot_nt(mix, out_w).astype(bf)

    W_steps.step(36, 0)
    project_out(0)
    project_out(1)
    att_copy(0).start()
    W_steps.step(37, 1)
    project_out(2)
    att_copy(1).start()
    project_out(3)
    att_copy(2).start()
    nT_saved.wait()
    W_steps.step(38, 2)
    norm_mlp(0)
    att_copy(3).start()
    norm_mlp(1)
    W_steps.step(39, 3)
    norm_mlp(2)
    norm_mlp(3)
    saved.append(saver(6, W.at[pl.ds(0, 16)], o_W))
    saved[-1].start()
    later = [saver(7, P, o_P), saver(8, R, o_R)]
    for c in later:
        c.start()
    saved += later

    def g_copy(m):
        slot = lax.rem(m, 2)
        return pltpu.make_async_copy(Gst.at[slot], o_G.at[pl.ds(m * 4, 4)], gout.at[slot])

    def mlp_part(m, _):
        slot = lax.rem(m, 2)
        s = 40 + 4 * m
        up_w = wblocks(W, 16 + 4 * m, 2)
        down_w = wblocks(W, 18 + 4 * m, 2)
        for ht in range(2):
            hs_ = pl.ds(ht * 512, 512)
            W_steps.step(s + ht, ht, high=True)
            u = dot(nrm[hs_, :], up_w)
            d = dot(dd[hs_, :], down_w)
            c0 = 0.7978845608028654
            u2 = u * u
            s1 = 1.0 + jnp.tanh(u * (c0 + (c0 * 0.044715) * u2))
            h = 0.5 * u
            act[hs_, :] = (h * s1).astype(bf)
            slope = s1 * (0.5 + h * (2.0 - s1) * (c0 + (3 * 0.044715 * c0) * u2))
            dup[hs_, :] = (d * slope).astype(bf)
        W_steps.step(s + 2, 2, high=True)
        for ht in range(2):
            hs_ = pl.ds(ht * 512, 512)
            dacc[hs_, :] += dot_nt(act[hs_, :], down_w)
            nacc[hs_, :] += dot_nt(dup[hs_, :], up_w)
        W_steps.step(s + 3, 3, high=True)
        W_steps.drain(m, m + 1)

        @pl.when(m >= 2)
        def _():
            g_copy(m - 2).wait()

        for ht in range(2):
            hs_ = pl.ds(ht * 512, 512)
            gu = dot(nT[hs_, :], dup[...]).astype(bf)
            Gst[slot, 0, hs_, :] = gu[:, :128]
            Gst[slot, 1, hs_, :] = gu[:, 128:]
            gd = dot(ddT[hs_, :], act[...]).astype(bf)
            Gst[slot, 2, hs_, :] = gd[:, :128]
            Gst[slot, 3, hs_, :] = gd[:, 128:]
        g_copy(m).start()
        return 0

    lax.fori_loop(0, 8, mlp_part, 0)
    for e in range(2):
        for c in range(2):
            tokbuf[e, pl.ds(c * 1024, 1024), :] = (dacc, nacc)[e][:, c * 512 : c * 512 + 512].astype(bf)
            saved.append(
                saver(9 + 2 * e + c, tokbuf.at[e, pl.ds(c * 1024, 1024)], (o_down, o_back)[e].at[c])
            )
            saved[-1].start()
    for i in range(SEQ):
        half_copy(i, 0).wait_send()
        half_copy(i, 1).wait_send()
    for i in range(SEQ):
        att_copy(i).wait_send()
    W_steps.drain(8, NB // PER)
    for j in range(5):
        V_steps.send(0, 0, j, act=lambda d: d.wait_send())
    g_copy(6).wait()
    g_copy(7).wait()
    for c in saved:
        c.wait()


def forward_call(chosen, tile, tok, cotangent, weights):
    bf, f32 = jnp.bfloat16, jnp.float32
    S = jax.ShapeDtypeStruct
    DMA = pltpu.SemaphoreType.DMA
    any_ = pl.BlockSpec(memory_space=HBM)
    vm = pltpu.VMEM
    return pl.pallas_call(
        forward_kernel,
        out_shape=(
            S((2, ROWS, 512), bf),
            S((2, ROWS, 512), bf),
            S((1024, ROWS), bf),
            S((12, ROWS, 128), bf),
            S((4, ROWS, 128), bf),
            S((ROWS, 1024), bf),
            S((ROWS, 1024), bf),
            S((2, ROWS, 512), bf),
            S((2, ROWS, 512), bf),
            S((16, 4, 2, 2, 64, 128), bf),
            S((32, 1024, 128), bf),
            S((8, 1024), f32),
        ),
        in_specs=[pl.BlockSpec(memory_space=pltpu.VMEM)] + [any_] * 9,
        out_specs=[any_] * 12,
        scratch_shapes=[
            vm((NB, 4, 2, 2, 64, 128), bf),
            vm((1, 4, 2, 2, 8, 128), f32),
            vm((8, 1024), f32),
            vm((2, ROWS, 512), bf),
            vm((2, ROWS, 512), bf),
            vm((2, 2048, 512), bf),
            vm((CAP, 2048), bf),
            vm((ROWS, 1024), bf),
            vm((1024, ROWS), bf),
            vm((ROWS, 1024), bf),
            vm((1024, ROWS), bf),
            vm((12, ROWS, 128), bf),
            vm((4, ROWS, 128), bf),
            vm((ROWS, 1024), bf),
            vm((ROWS, 1024), bf),
            vm((ROWS, 1024), f32),
            vm((ROWS, 1024), f32),
            vm((ROWS, 256), bf),
            vm((ROWS, 256), bf),
            vm((2, 4, 1024, 128), bf),
            DMA((NB, 8)),
            DMA((NB, 8)),
            DMA((1, 8)),
            DMA((1, 8)),
            DMA((4, 2)),
            DMA((4, 2)),
            DMA((4,)),
            DMA((4,)),
            DMA((NB + 1,)),
            DMA((2,)),
            DMA((13,)),
            DMA((2,)),
        ],
        compiler_params=pltpu.CompilerParams(
            collective_id=1, has_side_effects=True, vmem_limit_bytes=63 * 1024 * 1024
        ),
        name="forward",
    )(chosen, tile, tok, cotangent, *weights)


def backward_kernel(
    rows,
    cot,
    nT_in,
    qkv_in,
    mix_in,
    P_in,
    R_in,
    down_in,
    back_in,
    W_in,
    G_in,
    vec_in,
    o_newr,
    o_newg,
    o_sum,
    o_vec,
    G,
    Wa,
    qkv,
    mixed,
    nT,
    vecs,
    DR,
    NR,
    R1,
    bufs,
    buf2,
    da,
    daT,
    dmix,
    newr,
    newg,
    dhid,
    dlog,
    accs,
    GV,
    base,
    gsem,
    lsem,
    psem,
    prcv,
    qsem,
    qrcv,
    tout,
    *landing,
):
    p = Place()
    t = p.t
    other = {"tensor": 1 - t}
    f32, bf = jnp.float32, jnp.bfloat16
    wide, small = landing[:8], landing[8:]

    def g_load(c):
        return pltpu.make_async_copy(G_in.at[pl.ds(4 * c, 4)], G.at[pl.ds(4 * c, 4)], gsem.at[c])

    g_load(0).start()
    g_load(1).start()

    def stream(s, names):
        q = lax.rem(s, 2)
        out = []
        for k in names:
            if k < 2:
                src = (P_in, R_in)[k].at[cut(s, CAP)]
                dst = buf2.at[q, k]
            else:
                src = (rows, cot, down_in, back_in)[k - 2].at[:, cut(s, CAP)]
                dst = bufs.at[q, k - 2]
            out.append(pltpu.make_async_copy(src, dst, lsem.at[q, k]))
        return out

    everything = (0, 1, 2, 3, 4, 5)
    for c in stream(0, everything):
        c.start()
    fixed = [
        pltpu.make_async_copy(a, b, base.at[i])
        for i, (a, b) in enumerate(
            ((vec_in, vecs), (W_in, Wa), (qkv_in, qkv), (mix_in, mixed), (nT_in, nT))
        )
    ]
    for c in fixed[:3]:
        c.start()
    barrier(p, True)

    def pair_copy(s, e):
        return pltpu.make_async_remote_copy(
            (down_in, back_in)[e].at[:, cut(s, CAP)],
            (DR, NR)[e].at[:, cut(s, CAP)],
            psem.at[s, e],
            prcv.at[s, e],
            device_id=other,
            device_id_type=MESH,
        )

    pair_copy(0, 0).start()
    pair_copy(0, 1).start()
    steps = Scatter(p, G, o_sum, *wide)
    v_steps = Scatter(p, GV, o_vec, *small)

    accs[...] = jnp.zeros_like(accs)

    def fold(v):
        return jnp.sum(v.reshape(4, 8, 1024), 0)

    def pick(v):
        return jnp.where(t == 0, v[:, :512], v[:, 512:])

    masks, low_half = head_masks()
    seen = lax.broadcasted_iota(jnp.int32, (CAP, CAP), 0) <= lax.broadcasted_iota(
        jnp.int32, (CAP, CAP), 1
    )

    def seq_part(s, _):
        def tick(q):
            if q % 4 == 0:
                g_load(2 * s + q // 4).wait()

                @pl.when(s < 3)
                def _():
                    g_load(2 * s + q // 4 + 2).start()

            steps.step(8 * s + q, q % 4, low=True)

        tick(0)
        q = lax.rem(s, 2)

        @pl.when(s + 1 < SEQ)
        def _():
            for c in stream(s + 1, everything):
                c.start()
            pair_copy(s + 1, 0).start()
            pair_copy(s + 1, 1).start()

        pl.when(s == 0)(lambda: fixed[0].wait())
        for c in stream(s, everything):
            c.wait()
        for e in range(2):
            pair_copy(s, e).wait_recv()

        def part(n, _):
            rs_ = cut(n, 32)
            as_ = pl.ds(pl.multiple_of(s * CAP + n * 32, 32), 32)

            def mine(k):
                return jnp.concatenate([bufs[q, k, 0, rs_, :], bufs[q, k, 1, rs_, :]], 1).astype(f32)

            r, c = mine(0), mine(1)
            att = buf2[q, 0, rs_, :].astype(f32) + buf2[q, 1, rs_, :].astype(f32)
            h = r + att
            branch = att + (mine(2) + halves(DR, as_))
            dn = mine(3) + halves(NR, as_)
            inv = inv_rms(h)
            sc = dn * vecs[2:3, :]
            dh = inv * sc - h * (inv * inv * inv * jnp.mean(sc * h, -1, keepdims=True))
            gate = gate_of(r, vecs[0:1, :])
            dl = jnp.sum(c * branch, -1, keepdims=True) * (gate * (1.0 - gate))
            da[rs_, :] = (gate * c + dh).astype(bf)
            accs[2] += fold(dn * (h * inv))
            accs[0] += fold(r * dl)
            newr[as_, :] = pick(r + gate * branch).astype(bf)
            dhid[as_, :] = pick(dh)
            dlog[as_, :] = jnp.broadcast_to(dl, (32, 128))
            return 0

        lax.fori_loop(0, 4, part, 0)
        tick(1)
        lax.fori_loop(4, 8, part, 0)
        tick(2)
        for c in range(4):
            cs = pl.ds(c * 256, 256)
            daT[cs, cut(s, CAP)] = da[:, cs].T

        @pl.when(s == 0)
        def _():
            for c in fixed[1:3]:
                c.wait()
            for c in fixed[3:]:
                c.start()

        tick(3)
        dm = dot(da[...], wblocks(Wa, 12, 4)).astype(bf)
        for h in range(4):
            dmix[h] = dm[:, h * 128 : h * 128 + 128]

        def pair_back(hp):
            r_ = cut(s, CAP)
            qh, kh, vh = [qkv[3 * hp + c, r_, :] for c in range(3)]
            dmh = dmix[hp]
            outs = []
            for h in (0, 1):
                sc = jnp.where(seen, dot_nt(kh, qh * masks[h]) * (HD**-0.5), -1e30)
                e = jnp.exp(sc - jnp.max(sc, 0, keepdims=True))
                pr = e * (1.0 / jnp.sum(e, 0, keepdims=True))
                dv = dot(pr.astype(bf), dmh)
                dp = dot_nt(vh * masks[h], dmh)
                ds = (pr * (dp - jnp.sum(dp * pr, 0, keepdims=True))).astype(bf)
                outs.append((dot(ds.T, kh), dot(ds, qh), dv))
            scale = HD**-0.5
            for i, (a, b) in enumerate(zip(*outs)):
                v = jnp.where(low_half, a, b)
                qkv[3 * hp + i, r_, :] = (v if i == 2 else v * scale).astype(bf)

        for hp in range(4):
            tick(4 + hp)
            pair_back(hp)
        return 0

    lax.fori_loop(0, SEQ, seq_part, 0)
    row_outs = [pltpu.make_async_copy(newr, o_newr, tout.at[0])]
    row_outs[0].start()

    def grad_unit(leftT, a, b, first):
        y = jnp.concatenate([a, b], 1)
        for ht in range(2):
            g = dot(leftT[pl.ds(ht * 512, 512), :], y).astype(bf)
            for c in range(2):
                G[first + c, pl.ds(ht * 2, 2)] = g[:, c * 128 : c * 128 + 128].reshape(
                    2, 2, 2, 64, 128
                )

    def back_copy(s):
        return pltpu.make_async_remote_copy(
            DR.at[:, seq_rows(s)],
            R1.at[:, seq_rows(s)],
            qsem.at[s],
            qrcv.at[s],
            device_id=other,
            device_id_type=MESH,
        )

    for s in range(2):
        for c in stream(s, (2, 3)):
            c.start()
    for c in fixed[3:]:
        c.wait()
    grad_unit(daT, mixed[0], mixed[1], 32)
    grad_unit(daT, mixed[2], mixed[3], 34)

    def grad_part(n, _):
        for e in range(2):
            steps.step(32 + 4 * n + 2 * e, 2 * e)
            steps.step(33 + 4 * n + 2 * e, 2 * e + 1)
            j = 2 * n + e
            grad_unit(nT, qkv[2 * j], qkv[2 * j + 1], 36 + 2 * j)
        return 0

    lax.fori_loop(0, 3, grad_part, 0)
    for s in range(SEQ):
        steps.step(44 + s, s)
        y = 0.0
        for g in range(3):
            x = jnp.concatenate([qkv[4 * g + i, seq_rows(s), :] for i in range(4)], 1)
            y = y + dot_nt(x, wblocks(Wa, 4 * g, 4))
        y = y.astype(bf)
        DR[0, seq_rows(s), :] = y[:, :512]
        DR[1, seq_rows(s), :] = y[:, 512:]
        if s > 0:
            back_copy(s - 1).start()
    steps.step(48, 0, high=True)
    back_copy(3).start()

    route_half = jnp.where(t == 0, vecs[0:1, :512], vecs[0:1, 512:])
    for s in range(SEQ):
        steps.step(49 + s, (1 + s) % 4, high=True)
        steps.drain(2 * s, 2 * s + 2)
        q = s % 2
        for c in stream(s, (2, 3)):
            c.wait()
        back_copy(s).wait_recv()

        def part(n, _):
            rs_ = cut(n, 32)
            as_ = pl.ds(pl.multiple_of(s * CAP + n * 32, 32), 32)
            r = jnp.concatenate([bufs[q, 0, 0, rs_, :], bufs[q, 0, 1, rs_, :]], 1).astype(f32)
            dn = halves(DR, as_) + halves(R1, as_)
            inv = inv_rms(r)
            sc = dn * vecs[1:2, :]
            dr = inv * sc - r * (inv * inv * inv * jnp.mean(sc * r, -1, keepdims=True))
            accs[1] += fold(dn * (r * inv))
            dl = dlog[as_, :]
            dl = jnp.concatenate([dl, dl, dl, dl], 1)
            ch = bufs[q, 1, t, rs_, :].astype(f32)
            newg[as_, :] = (ch + (dhid[as_, :] + pick(dr) + dl * route_half)).astype(bf)
            return 0

        lax.fori_loop(0, 8, part, 0)
        if s + 2 < SEQ:
            for c in stream(s + 2, (2, 3)):
                c.start()

    for z in range(4):
        for y in range(2):
            cs = pl.ds((z * 2 + y) * 128, 128)
            tile = jnp.concatenate(
                [jnp.sum(accs[k, :, cs], 0, keepdims=True) for k in range(3)]
                + [jnp.zeros((5, 128), f32)],
                0,
            )
            GV[0, z, y, 0] = tile
            GV[0, z, y, 1] = tile
    for s in range(SEQ):
        back_copy(s).wait_send()
    row_outs.append(pltpu.make_async_copy(newg, o_newg, tout.at[1]))
    row_outs[1].start()
    v_steps.send(0, 0, 0)

    for k, s in enumerate(range(53, 67)):
        steps.step(s, s % PER, static=s)
        if k in (0, 2, 3, 5, 7):
            j = (0, 2, 3, 5, 7).index(k) + 1
            v_steps.recv(0, 0, j - 1)
            if j < 5:
                v_steps.send(0, 0, j)
    for c in row_outs:
        c.wait()
    for s in range(SEQ):
        for e in range(2):
            pair_copy(s, e).wait_send()
    for j in range(5):
        v_steps.send(0, 0, j, act=lambda d: d.wait_send())
    steps.drain(8, NB // PER)


def backward_call(kept):
    bf, f32 = jnp.bfloat16, jnp.float32
    S = jax.ShapeDtypeStruct
    DMA = pltpu.SemaphoreType.DMA
    any_ = pl.BlockSpec(memory_space=HBM)
    vspec = pl.BlockSpec(memory_space=pltpu.VMEM)
    vm = pltpu.VMEM
    return pl.pallas_call(
        backward_kernel,
        out_shape=(
            S((ROWS, 512), bf),
            S((ROWS, 512), bf),
            S((NB, 64, 128), f32),
            S((1, 8, 128), f32),
        ),
        in_specs=[any_] * 12,
        out_specs=[any_, any_, vspec, vspec],
        scratch_shapes=[
            vm((NB, 4, 2, 2, 64, 128), bf),
            vm((16, 4, 2, 2, 64, 128), bf),
            vm((12, ROWS, 128), bf),
            vm((4, ROWS, 128), bf),
            vm((1024, ROWS), bf),
            vm((8, 1024), f32),
            vm((2, ROWS, 512), bf),
            vm((2, ROWS, 512), bf),
            vm((2, ROWS, 512), bf),
            vm((2, 4, 2, CAP, 512), bf),
            vm((2, 2, CAP, 1024), bf),
            vm((CAP, 1024), bf),
            vm((1024, ROWS), bf),
            vm((4, CAP, 128), bf),
            vm((ROWS, 512), bf),
            vm((ROWS, 512), bf),
            vm((ROWS, 512), f32),
            vm((ROWS, 128), f32),
            vm((3, 8, 1024), f32),
            vm((1, 4, 2, 2, 8, 128), f32),
            DMA((5,)),
            DMA((8,)),
            DMA((2, 6)),
            DMA((4, 2)),
            DMA((4, 2)),
            DMA((4,)),
            DMA((4,)),
            DMA((2,)),
        ]
        + Scatter.landing(NB, (64, 128), bf)
        + Scatter.landing(PER, (8, 128), f32),
        compiler_params=pltpu.CompilerParams(
            collective_id=2, has_side_effects=True, vmem_limit_bytes=63 * 1024 * 1024
        ),
        name="backward",
    )(*kept)


def place_kernel(
    spot_ref,
    own_ref,
    newr,
    newg,
    tok,
    cot,
    o_tok,
    o_cot,
    g_q,
    g_k,
    g_v,
    g_out,
    g_up,
    g_down,
    old,
    out,
    new,
    came,
    went,
    own,
    nsem,
    gsem,
):
    bf = jnp.bfloat16

    def piece(n):
        return n // (2048 // SIZE), cut(n % (2048 // SIZE), SIZE)

    def load(n, a):
        i, rs = piece(n)
        return pltpu.make_async_copy((tok, cot)[a].at[i, rs], old.at[a, n], came.at[a, n])

    def store(n, a):
        i, rs = piece(n)
        return pltpu.make_async_copy(out.at[a, n], (o_tok, o_cot)[a].at[i, rs], went.at[a, n])

    pieces = SEQ * 2048 // SIZE
    news = [pltpu.make_async_copy((newr, newg)[a], new.at[a], nsem.at[a]) for a in range(2)]
    sums = pltpu.make_async_copy(own_ref, own, nsem.at[2])
    for c in news + [sums]:
        c.start()

    def start(n, _):
        load(n, 0).start()
        load(n, 1).start()
        return 0

    lax.fori_loop(0, pieces, start, 0)

    moves = []
    for b in range(NB):
        if b < 32:
            ref, k = (g_up, g_down)[b % 4 // 2], b // 4 * 2 + b % 2
        else:
            ref, k = (g_out, b - 32) if b < 36 else ((g_q, g_k, g_v)[b % 3], (b - 36) // 3)
        moves.append(
            pltpu.make_async_copy(own.at[b], ref.at[:, pl.ds(k * 128, 128)], gsem.at[b])
        )
    for c in news:
        c.wait()
    ones = jnp.ones((CAP, 128), bf)

    def place(n, _):
        i, _rs = piece(n)

        @pl.when(n == 2)
        def _():
            sums.wait()
            for c in moves:
                c.start()

        row = lax.broadcasted_iota(jnp.int32, (SIZE, CAP), 0) + n % (2048 // SIZE) * SIZE
        hit = jnp.where(row == spot_ref[i], 1.0, 0.0).astype(bf)
        kept = 1.0 - dot(hit, ones)
        kept = jnp.concatenate([kept, kept, kept, kept], 1).astype(bf)
        for a in range(2):
            moved = dot(hit, new[a, cut(i, CAP), :]).astype(bf)
            load(n, a).wait()
            out[a, n] = old[a, n] * kept + moved
            store(n, a).start()
        return 0

    lax.fori_loop(0, pieces, place, 0)

    def finish(n, _):
        store(n, 0).wait()
        store(n, 1).wait()
        return 0

    lax.fori_loop(0, pieces, finish, 0)
    for c in moves:
        c.wait()


SIZE = 1024


def place_call(spot, own, newr, newg, tok, cotangent):
    bf, f32 = jnp.bfloat16, jnp.float32
    S = jax.ShapeDtypeStruct
    DMA = pltpu.SemaphoreType.DMA
    any_ = pl.BlockSpec(memory_space=pltpu.MemorySpace.HBM)
    pieces = SEQ * 2048 // SIZE
    return pl.pallas_call(
        place_kernel,
        out_shape=(
            S((SEQ, 2048, 512), bf),
            S((SEQ, 2048, 512), bf),
            S((64, 512), f32),
            S((64, 512), f32),
            S((64, 512), f32),
            S((64, 512), f32),
            S((64, 2048), f32),
            S((64, 2048), f32),
        ),
        in_specs=[pl.BlockSpec(memory_space=pltpu.VMEM)] + [any_] * 5,
        out_specs=[any_] * 8,
        scratch_shapes=[
            pltpu.VMEM((2, pieces, SIZE, 512), bf),
            pltpu.VMEM((2, pieces, SIZE, 512), bf),
            pltpu.VMEM((2, ROWS, 512), bf),
            DMA((2, pieces)),
            DMA((2, pieces)),
            pltpu.VMEM((NB, 64, 128), f32),
            DMA((3,)),
            DMA((NB,)),
        ],
        compiler_params=pltpu.CompilerParams(vmem_limit_bytes=63 * 1024 * 1024),
        name="place_rows",
    )(spot, own, newr, newg, tok, cotangent)


def to_tile(w_route, gain_attn, gain_mlp):
    v = jnp.stack([w_route, gain_attn, gain_mlp]).astype(jnp.float32)
    v = jnp.pad(v, ((0, 5), (0, 0)))
    z = jnp.zeros_like(v)
    odd = lax.axis_index("dp") % 2
    return jnp.where(odd == 0, jnp.concatenate([v, z], 1), jnp.concatenate([z, v], 1))


def fused(
    tokens,
    routed,
    w_query,
    w_key,
    w_value,
    w_out,
    w_up,
    w_down,
    w_route,
    gain_attn,
    gain_mlp,
    cotangent,
):
    tok = tokens.reshape(SEQ, 2048, 512)
    cot = cotangent.reshape(SEQ, 2048, 512)
    spot = routed.reshape(SEQ, 1, CAP)
    tile = to_tile(w_route, gain_attn, gain_mlp)
    weights = (w_query, w_key, w_value, w_out.T, w_up, w_down.T)
    kept = list(forward_call(spot, tile, tok, cot, weights))
    kept[10] = kept[10].reshape(32, 4, 2, 2, 64, 128)
    newr, newg, own, vec = backward_call(kept)
    odd = lax.axis_index("dp") % 2
    vec = jnp.where(odd == 0, vec[0, :3, :64], vec[0, :3, 64:])
    output, grad, g_q, g_k, g_v, g_out, g_up, g_down = place_call(
        spot, own, newr, newg, tok, cot
    )
    return (
        output.reshape(tokens.shape),
        grad.reshape(tokens.shape),
        g_q,
        g_k,
        g_v,
        g_out.T,
        g_up,
        g_down.T,
        vec[0],
        vec[1],
        vec[2],
    )


def shards(tokens, routed, *rest):
    sizes = (lax.axis_size("dp"), lax.axis_size("tensor"))
    here = tokens.shape == (4, 1, 2048, 512) and routed.shape == (4, 1, 256)
    if sizes == (16, 2) and here:
        return fused(tokens, routed, *rest)
    return plain(tokens, routed, *rest)


def solution(mesh):
    rows = P("dp", "tensor")
    columns = P("tensor", "dp")
    vector = P("dp")
    stored = P(None, "dp", None, "tensor")
    return jax.shard_map(
        shards,
        mesh=mesh,
        in_specs=(
            stored,
            P(None, "dp", None),
            rows,
            rows,
            rows,
            columns,
            rows,
            columns,
            vector,
            vector,
            vector,
            stored,
        ),
        out_specs=(
            stored,
            stored,
            rows,
            rows,
            rows,
            columns,
            rows,
            columns,
            vector,
            vector,
            vector,
        ),
        check_vma=False,
    )
```

```python
import jax
import jax.numpy as jnp
from jax import lax
from jax.experimental import pallas as pl
from jax.experimental.pallas import tpu as pltpu
from jax.sharding import PartitionSpec as P

HD = 64
eps_norm = 1e-05


def dense(left, right):
    return jnp.dot(left, right, preferred_element_type=jnp.float32)


def dense_t(left, right):
    return lax.dot_general(
        left, right, (((1,), (1,)), ((), ())), preferred_element_type=jnp.float32
    )


def dense_g(left, right):
    return lax.dot_general(
        left, right, (((0,), (0,)), ((), ())), preferred_element_type=jnp.float32
    )


def rms_back(values, inv, gain, grad):
    grad_gain = jnp.sum(grad * values * inv, 0)
    scaled = grad * gain
    dot = jnp.mean(scaled * values, -1, keepdims=True)
    return inv * scaled - values * (inv * inv * inv) * dot, grad_gain


def plain(
    tokens,
    routed,
    w_query,
    w_key,
    w_value,
    w_out,
    w_up,
    w_down,
    w_route,
    gain_attn,
    gain_mlp,
    cotangent,
):
    micro, seqs, length, half_width = tokens.shape
    capacity = routed.shape[2]
    batch = micro * seqs
    total = batch * capacity
    cols = w_query.shape[1]
    hidden_cols = w_up.shape[1]
    width = half_width * lax.axis_size("tensor")
    offset = lax.axis_index("tensor") * half_width
    scale = HD ** (-0.5)
    swap = [(0, 1), (1, 0)]

    vec = jnp.stack([w_route, gain_attn, gain_mlp], 1)
    vec = jnp.pad(vec, ((0, 0), (0, 125)))
    packed = jnp.concatenate([w_query, w_key, w_value, w_up, w_out.T, w_down.T, vec], 1)
    gathered = lax.all_gather(packed, "dp", axis=0, tiled=True)
    b1, b2, b3 = cols, 2 * cols, 3 * cols
    b4 = b3 + hidden_cols
    b5 = b4 + w_out.shape[0]
    b6 = b5 + w_down.shape[0]
    fq = gathered[:, :b1]
    fk = gathered[:, b1:b2]
    fv = gathered[:, b2:b3]
    fup = gathered[:, b3:b4]
    foutT = gathered[:, b4:b5]
    fdownT = gathered[:, b5:b6]
    route = gathered[:, b6]
    route_f32 = route.astype(jnp.float32)
    gain1 = gathered[:, b6 + 1].astype(jnp.float32)
    gain2 = gathered[:, b6 + 2].astype(jnp.float32)

    tok = tokens.reshape(batch, length, half_width)
    cot = cotangent.reshape(batch, length, half_width)
    chosen = routed.reshape(batch, capacity)
    rows_half = jnp.take_along_axis(tok, chosen[:, :, None], axis=1).reshape(total, half_width)
    cot_half = jnp.take_along_axis(cot, chosen[:, :, None], axis=1).reshape(total, half_width)
    rows = lax.all_gather(rows_half, "tensor", axis=1, tiled=True)
    cot_rows = lax.all_gather(cot_half, "tensor", axis=1, tiled=True)

    rows_f = rows.astype(jnp.float32)
    cot_f = cot_rows.astype(jnp.float32)
    gate = jax.nn.sigmoid(dense(rows, route))
    inv1 = lax.rsqrt(jnp.mean(rows_f * rows_f, -1, keepdims=True) + eps_norm)
    normed = (rows_f * inv1 * gain1).astype(jnp.bfloat16)
    heads = cols // HD

    def split(x):
        return x.astype(jnp.bfloat16).reshape(batch, capacity, heads, HD).transpose(0, 2, 1, 3)

    def join(x):
        return x.transpose(0, 2, 1, 3).reshape(total, cols)

    q = split(dense(normed, fq))
    k = split(dense(normed, fk))
    v = split(dense(normed, fv))
    causal = lax.broadcasted_iota(jnp.int32, (capacity, capacity), 0) >= lax.broadcasted_iota(
        jnp.int32, (capacity, capacity), 1
    )
    scores = jnp.einsum("bhqd,bhkd->bhqk", q, k, preferred_element_type=jnp.float32) * scale
    scores = jnp.where(causal, scores, -1e30)
    peak = jnp.max(scores, -1, keepdims=True)
    expd = jnp.exp(scores - peak)
    probs = expd / jnp.sum(expd, -1, keepdims=True)
    probs_low = probs.astype(jnp.bfloat16)
    mixed = jnp.einsum("bhqk,bhkd->bhqd", probs_low, v, preferred_element_type=jnp.float32)
    mixed = join(mixed.astype(jnp.bfloat16))

    def pair_sum(x):
        low = x.astype(jnp.bfloat16)
        other = lax.ppermute(low, "tensor", swap)
        return low.astype(jnp.float32) + other.astype(jnp.float32)

    attended = pair_sum(dense_t(mixed, foutT))
    hidden = rows_f + attended
    inv2 = lax.rsqrt(jnp.mean(hidden * hidden, -1, keepdims=True) + eps_norm)
    normed2 = (hidden * inv2 * gain2).astype(jnp.bfloat16)
    up = dense(normed2, fup)
    act32, gelu_back = jax.vjp(jax.nn.gelu, up)
    act = act32.astype(jnp.bfloat16)
    down = pair_sum(dense_t(act, fdownT))
    branch = attended + down
    d_logit = jnp.sum(cot_f * branch, -1) * gate * (1.0 - gate)
    branch_half = lax.dynamic_slice_in_dim(branch, offset, half_width, 1)
    new_rows = (rows_half.astype(jnp.float32) + gate[:, None] * branch_half).astype(jnp.bfloat16)

    d_branch = gate[:, None] * cot_f
    d_down = d_branch.astype(jnp.bfloat16)
    g_downT = dense_g(d_down, act)
    d_act = dense(d_down, fdownT)
    d_upper = gelu_back(d_act)[0].astype(jnp.bfloat16)
    g_up = dense_g(normed2, d_upper)
    d_normed2 = pair_sum(dense_t(d_upper, fup))
    d_hidden, g_gain2 = rms_back(hidden, inv2, gain2, d_normed2)
    d_attended = (d_branch + d_hidden).astype(jnp.bfloat16)
    g_outT = dense_g(d_attended, mixed)
    d_mixed = split(dense(d_attended, foutT))
    d_values = jnp.einsum("bhqk,bhqd->bhkd", probs_low, d_mixed, preferred_element_type=jnp.float32)
    d_values = join(d_values.astype(jnp.bfloat16))
    d_probs = jnp.einsum("bhqd,bhkd->bhqk", d_mixed, v, preferred_element_type=jnp.float32)
    d_scores = probs * (d_probs - jnp.sum(d_probs * probs, -1, keepdims=True))
    d_scores = d_scores.astype(jnp.bfloat16)
    d_q = jnp.einsum("bhqk,bhkd->bhqd", d_scores, k, preferred_element_type=jnp.float32) * scale
    d_k = jnp.einsum("bhqk,bhqd->bhkd", d_scores, q, preferred_element_type=jnp.float32) * scale
    d_q = join(d_q.astype(jnp.bfloat16))
    d_k = join(d_k.astype(jnp.bfloat16))
    g_q = dense_g(normed, d_q)
    g_k = dense_g(normed, d_k)
    g_v = dense_g(normed, d_values)
    d_normed = pair_sum(dense_t(d_q, fq) + dense_t(d_k, fk) + dense_t(d_values, fv))
    d_rows, g_gain1 = rms_back(rows_f, inv1, gain1, d_normed)
    g_route = jnp.sum(rows_f * d_logit[:, None], 0)
    d_half = (
        lax.dynamic_slice_in_dim(d_hidden + d_rows, offset, half_width, 1)
        + d_logit[:, None] * lax.dynamic_slice_in_dim(route_f32, offset, half_width, 0)[None, :]
    )
    grad_rows = (cot_half.astype(jnp.float32) + d_half).astype(jnp.bfloat16)

    seq_ids = lax.broadcasted_iota(jnp.int32, (batch, capacity), 0)
    output = tok.at[seq_ids, chosen].set(
        new_rows.reshape(batch, capacity, half_width), unique_indices=True
    )
    input_grad = cot.at[seq_ids, chosen].set(
        grad_rows.reshape(batch, capacity, half_width), unique_indices=True
    )

    g_vec = jnp.pad(jnp.stack([g_route, g_gain1, g_gain2], 1), ((0, 0), (0, 125)))
    grads = jnp.concatenate(
        [x.astype(jnp.bfloat16) for x in (g_q, g_k, g_v, g_up, g_outT, g_downT, g_vec)], 1
    )
    own = lax.psum_scatter(grads, "dp", scatter_dimension=0, tiled=True).astype(jnp.float32)
    return (
        output.reshape(tokens.shape),
        input_grad.reshape(tokens.shape),
        own[:, :b1],
        own[:, b1:b2],
        own[:, b2:b3],
        own[:, b4:b5].T,
        own[:, b3:b4],
        own[:, b5:b6].T,
        own[:, b6],
        own[:, b6 + 1],
        own[:, b6 + 2],
    )


MESH = pl.DeviceIdType.MESH
NB = 48
PATTERN = "XYZX"
PER = 4
GATHER_LAGS = {
    "X": (0, 3, 6, 9, 12, 19),
    "Y": (0, 4, 7, 9, 13, 19),
    "Z": (0, 5, 9, 12, 15, 19),
}
SCATTER_LAGS = {
    "X": (0, 4, 7, 9, 13, 18),
    "Y": (0, 4, 8, 10, 12, 17),
    "Z": (0, 2, 5, 9, 14, 19),
}
VECTOR_STEPS = (0, 3, 6, 9, 12, 15)


class Place:
    def __init__(self):
        me = lax.axis_index("dp")
        self.x = me % 2
        self.y = (me // 2) % 2
        self.z = me // 4
        self.nx = me + 1 - 2 * self.x
        self.ny = me + 2 - 4 * self.y
        self.up = jnp.minimum(me + 4, 15)
        self.dn = jnp.maximum(me - 4, 0)
        self.t = lax.axis_index("tensor")


def both(a, b):
    return jnp.logical_and(a, b)


def greet_all(p):
    bar = pltpu.get_barrier_semaphore()

    def greet(dev):
        pl.semaphore_signal(bar, inc=1, device_id=dev, device_id_type=MESH)

    greet({"dp": p.nx})
    greet({"dp": p.ny})
    greet({"tensor": 1 - p.t})

    @pl.when(p.z < 3)
    def _():
        greet({"dp": p.up})

    @pl.when(p.z > 0)
    def _():
        greet({"dp": p.dn})


def await_all(p):
    bar = pltpu.get_barrier_semaphore()
    inner = both(p.z > 0, p.z < 3)

    @pl.when(inner)
    def _():
        pl.semaphore_wait(bar, 5)

    @pl.when(jnp.logical_not(inner))
    def _():
        pl.semaphore_wait(bar, 4)


class Steps:
    def step(self, s, pos, static=None, low=False, high=False):
        live = []
        for c, lags in self.lags.items():
            for j in range(6):
                q = (pos - lags[j]) % PER
                if PATTERN[q] == c and (static is None or 0 <= static - lags[j] < NB):
                    live.append((j, lags[j], q))
        live.sort(reverse=True)

        def do(j, lag, q, act):
            b = s - lag
            if low:
                pl.when(b >= 0)(lambda: act(b, q, j))
            elif high:
                pl.when(b < NB)(lambda: act(b, q, j))
            else:
                act(b, q, j)

        for j, lag, q in live:
            if j > 0:
                do(j, lag, q, lambda b, q, j: self.recv(b, q, j - 1))
        for j, lag, q in live:
            if j < 5:
                do(j, lag, q, self.send)

    def drain(self, first, last):
        def body(r, _):
            for pos in range(PER):
                for j in range(5):
                    self.send(r * PER + pos, pos, j, act=lambda d: d.wait_send())
            return 0

        lax.fori_loop(first, last, body, 0)


class Gather(Steps):
    lags = GATHER_LAGS

    def __init__(self, p, W, ss, rs):
        self.p, self.W, self.ss, self.rs = p, W, ss, rs

    def copy(self, ref, b, k, dev):
        return pltpu.make_async_remote_copy(
            ref, ref, self.ss.at[b, k], self.rs.at[b, k], device_id={"dp": dev}, device_id_type=MESH
        )

    def zref(self, b, c, zz):
        zz = jnp.clip(zz, 0, 3)
        return self.W.at[b, zz] if c == "Z" else self.W.at[b, zz, self.p.y, self.p.x]

    def zsend(self, b, c, hop, act):
        p = self.p

        @pl.when(both(p.z - hop + 1 >= 0, p.z < 3))
        def _():
            act(self.copy(self.zref(b, c, p.z - hop + 1), b, hop - 1, p.up))

        @pl.when(both(p.z + hop - 1 <= 3, p.z > 0))
        def _():
            act(self.copy(self.zref(b, c, p.z + hop - 1), b, 2 + hop, p.dn))

    def zrecv(self, b, c, hop):
        p = self.p

        @pl.when(p.z - hop >= 0)
        def _():
            self.copy(self.zref(b, c, p.z - hop), b, hop - 1, p.nx).wait_recv()

        @pl.when(p.z + hop <= 3)
        def _():
            self.copy(self.zref(b, c, p.z + hop), b, 2 + hop, p.nx).wait_recv()

    def stage(self, b, c, j):
        W = self.W
        x, y, z = self.p.x, self.p.y, self.p.z
        if c == "X":
            line = (7, W.at[b, :, :, x], W.at[b, :, :, 1 - x])
            return (1, 2, 3, (6, W.at[b, :, y, x], W.at[b, :, 1 - y, x]), line)[j]
        if c == "Y":
            line = (6, W.at[b, :, y], W.at[b, :, 1 - y])
            return (1, 2, 3, (7, W.at[b, :, y, x], W.at[b, :, y, 1 - x]), line)[j]
        line = (7, W.at[b, z, y, x], W.at[b, z, y, 1 - x])
        return (line, (6, W.at[b, z, y], W.at[b, z, 1 - y]), 1, 2, 3)[j]

    def send(self, b, pos, j, act=lambda d: d.start()):
        c = PATTERN[pos]
        st = self.stage(b, c, j)
        if isinstance(st, int):
            self.zsend(b, c, st, act)
        else:
            act(self.copy(st[1], b, st[0], self.p.ny if st[0] == 6 else self.p.nx))

    def recv(self, b, pos, j):
        c = PATTERN[pos]
        st = self.stage(b, c, j)
        if isinstance(st, int):
            self.zrecv(b, c, st)
        else:
            self.copy(st[2], b, st[0], self.p.nx).wait_recv()


class Scatter(Steps):
    lags = SCATTER_LAGS

    def __init__(self, p, G, out, L8, L4, LZ, P4, P2, P1, ss, rs):
        self.p, self.G, self.out, self.ss, self.rs = p, G, out, ss, rs
        self.L8, self.L4, self.LZ, self.P4, self.P2, self.P1 = L8, L4, LZ, P4, P2, P1

    def slot(self, b, pos):
        r = b // PER
        return r if PATTERN[pos] == "Z" else r * 3 + {0: 0, 1: 1, 3: 2}[pos]

    def copy(self, src, dst, b, k, dev):
        return pltpu.make_async_remote_copy(
            src, dst, self.ss.at[b, k], self.rs.at[b, k], device_id={"dp": dev}, device_id_type=MESH
        )

    def gz(self, b, c, t):
        t = jnp.clip(t, 0, 3)
        return self.G.at[b, t] if c == "Z" else self.G.at[b, t, self.p.y, self.p.x]

    def lz(self, b, pos, k):
        i = self.slot(b, pos)
        return self.P4.at[i, k] if PATTERN[pos] == "Z" else self.LZ.at[i, k]

    def add(self, ref, land):
        ref[...] = (ref[...].astype(jnp.float32) + land[...].astype(jnp.float32)).astype(ref.dtype)

    def zsend(self, b, pos, hop, act):
        p, c = self.p, PATTERN[pos]

        @pl.when(p.z + hop <= 3)
        def _():
            act(self.copy(self.gz(b, c, p.z + hop), self.lz(b, pos, hop - 1), b, hop - 1, p.up))

        @pl.when(p.z - hop >= 0)
        def _():
            act(self.copy(self.gz(b, c, p.z - hop), self.lz(b, pos, 2 + hop), b, 2 + hop, p.dn))

    def zrecv(self, b, pos, hop, final):
        p, c = self.p, PATTERN[pos]

        def take(k, t):
            land = self.lz(b, pos, k)
            self.copy(land, land, b, k, p.nx).wait_recv()
            if not final:
                self.add(self.gz(b, c, t), land)

        if not final:

            @pl.when(both(p.z >= 1, p.z - 1 + hop <= 3))
            def _():
                take(hop - 1, p.z - 1 + hop)

            @pl.when(both(p.z <= 2, p.z + 1 - hop >= 0))
            def _():
                take(2 + hop, p.z + 1 - hop)

            return
        own = self.G.at[b, p.z, p.y, p.x]
        below, above = self.lz(b, pos, 0), self.lz(b, pos, 3)
        f32 = jnp.float32

        @pl.when(p.z == 0)
        def _():
            take(3, p.z)
            self.out[b] = own[...].astype(f32) + above[...].astype(f32)

        @pl.when(p.z == 3)
        def _():
            take(0, p.z)
            self.out[b] = own[...].astype(f32) + below[...].astype(f32)

        @pl.when(both(p.z > 0, p.z < 3))
        def _():
            take(0, p.z)
            take(3, p.z)
            self.out[b] = own[...].astype(f32) + below[...].astype(f32) + above[...].astype(f32)

    def stage(self, b, pos, j):
        G = self.G
        x, y, z = self.p.x, self.p.y, self.p.z
        c, i = PATTERN[pos], self.slot(b, pos)
        if c == "X":
            first = (7, G.at[b, :, :, 1 - x], self.L8.at[i], G.at[b, :, :, x])
            return (first, (6, G.at[b, :, 1 - y, x], self.L4.at[i], G.at[b, :, y, x]), 3, 2, 1)[j]
        if c == "Y":
            first = (6, G.at[b, :, 1 - y], self.L8.at[i], G.at[b, :, y])
            return (first, (7, G.at[b, :, y, 1 - x], self.L4.at[i], G.at[b, :, y, x]), 3, 2, 1)[j]
        last = (7, G.at[b, z, y, 1 - x], self.P1.at[i], G.at[b, z, y, x])
        return (3, 2, 1, (6, G.at[b, z, 1 - y], self.P2.at[i], G.at[b, z, y]), last)[j]

    def send(self, b, pos, j, act=lambda d: d.start()):
        st = self.stage(b, pos, j)
        if isinstance(st, int):
            self.zsend(b, pos, st, act)
        else:
            act(self.copy(st[1], st[2], b, st[0], self.p.ny if st[0] == 6 else self.p.nx))

    def recv(self, b, pos, j):
        st = self.stage(b, pos, j)
        if isinstance(st, int):
            self.zrecv(b, pos, st, PATTERN[pos] != "Z" and j == 4)
        else:
            self.copy(st[2], st[2], b, st[0], self.p.nx).wait_recv()
            if j == 4:
                self.out[b] = st[3][...].astype(jnp.float32) + st[2][...].astype(jnp.float32)
            else:
                self.add(st[3], st[2])

    @staticmethod
    def landing(blocks, tail, dtype):
        n, m = blocks // PER * 3, blocks // PER
        return [
            pltpu.VMEM(shape + tail, dtype)
            for shape in ((n, 4, 2), (n, 4), (n, 6), (m, 6, 2, 2), (m, 2), (m,))
        ] + [pltpu.SemaphoreType.DMA((blocks, 8))] * 2
EPS = 1e-05
SEQ = 4
CAP = 256
ROWS = SEQ * CAP
HBM = pl.ANY


def dot(a, b):
    return jnp.dot(a, b, preferred_element_type=jnp.float32)


def dot_nt(a, b):
    return lax.dot_general(a, b, (((1,), (1,)), ((), ())), preferred_element_type=jnp.float32)


def halves(ref, rs):
    return jnp.concatenate([ref[0, rs, :], ref[1, rs, :]], 1).astype(jnp.float32)


def wblocks(W, first, count):
    return jnp.concatenate([W[first + i].reshape(1024, 128) for i in range(count)], 1)


def seq_rows(i):
    return pl.ds(i * CAP, CAP)


def cut(i, n):
    return pl.ds(pl.multiple_of(i * n, n), n)


def head_masks():
    lane = lax.broadcasted_iota(jnp.int32, (CAP, 128), 1)
    one = jnp.where(lane < HD, 1.0, 0.0)
    return [one.astype(jnp.bfloat16), (1.0 - one).astype(jnp.bfloat16)], lane < HD


def causal_mask():
    shape = (CAP, CAP)
    return lax.broadcasted_iota(jnp.int32, shape, 0) >= lax.broadcasted_iota(jnp.int32, shape, 1)


def softmax_rows(q, k, mask):
    s = jnp.where(mask, dot_nt(q, k) * (HD**-0.5), -1e30)
    e = jnp.exp(s - jnp.max(s, -1, keepdims=True))
    return e * (1.0 / jnp.sum(e, -1, keepdims=True))


def inv_rms(v):
    return lax.rsqrt(jnp.mean(v * v, -1, keepdims=True) + EPS)


def gate_of(rows_f, route):
    return jax.nn.sigmoid(jnp.sum(rows_f * route, -1, keepdims=True))


def own_slot(p, W, b):
    return W.at[b, p.z, p.y, p.x]


def forward_kernel(
    spot_ref,
    tile_ref,
    tok_ref,
    cot_ref,
    wq,
    wk,
    wv,
    wo,
    wu,
    wd,
    o_rows,
    o_cot,
    o_nT,
    o_qkv,
    o_mix,
    o_P,
    o_R,
    o_down,
    o_back,
    o_W,
    o_G,
    o_vec,
    W,
    VB,
    vecs,
    rows,
    cot,
    tokbuf,
    onehot,
    nrm,
    nT,
    dd,
    ddT,
    qkv,
    mixed,
    P,
    R,
    dacc,
    nacc,
    act,
    dup,
    Gst,
    ss,
    rs,
    vss,
    vrs,
    hs,
    hr,
    asnd,
    arcv,
    first,
    load,
    outs,
    gout,
):
    p = Place()
    t = p.t
    other = {"tensor": 1 - t}
    f32, bf = jnp.float32, jnp.bfloat16

    greet_all(p)

    own = [pltpu.make_async_copy(tile_ref, own_slot(p, VB, 0), first.at[NB])]
    for b in range(16):
        src, col = ((wq, wk, wv)[b % 3], b // 3) if b < 12 else (wo, b - 12)
        own.append(
            pltpu.make_async_copy(src.at[:, pl.ds(col * 128, 128)], own_slot(p, W, b), first.at[b])
        )
    for b in range(32):
        src = (wu, wd)[b % 4 // 2]
        own.append(
            pltpu.make_async_copy(
                src.at[:, pl.ds((b // 4 * 2 + b % 2) * 128, 128)],
                own_slot(p, W, 16 + b),
                first.at[16 + b],
            )
        )
    for c in own:
        c.start()

    def loader(i, a):
        return pltpu.make_async_copy((tok_ref, cot_ref)[a].at[i], tokbuf.at[a], load.at[a])

    loader(0, 0).start()
    loader(0, 1).start()
    await_all(p)
    for c in own:
        c.wait()
    W_steps = Gather(p, W, ss, rs)
    V_steps = Gather(p, VB, vss, vrs)

    def half_copy(i, a):
        ref = (rows, cot)[a].at[t, cut(i, CAP)]
        return pltpu.make_async_remote_copy(
            ref, ref, hs.at[i, a], hr.at[i, a], device_id=other, device_id_type=MESH
        )

    def half_wait(i, a):
        ref = (rows, cot)[a].at[1 - t, seq_rows(i)]
        pltpu.make_async_remote_copy(
            ref, ref, hs.at[i, a], hr.at[i, a], device_id=other, device_id_type=MESH
        ).wait_recv()

    def gather_part(i, _):
        def tick(q):
            W_steps.step(4 * i + q, q, low=True)
            for j, s in enumerate(VECTOR_STEPS):
                if s % 4 == q:

                    @pl.when(i == s // 4)
                    def _():
                        if j > 0:
                            V_steps.recv(0, 0, j - 1)
                        if j < 5:
                            V_steps.send(0, 0, j)

        for a in range(2):
            tick(2 * a)
            if a == 0:
                spot = jnp.broadcast_to(spot_ref[i], (128, CAP)).T[:, :1]
                hit = lax.broadcasted_iota(jnp.int32, (CAP, 2048), 1) == spot
                onehot[...] = jnp.where(hit, 1.0, 0.0).astype(bf)
            loader(i, a).wait()
            (rows, cot)[a][t, cut(i, CAP), :] = dot(onehot[...], tokbuf[a]).astype(bf)
            pl.when(i < 3)(lambda: loader(i + 1, a).start())
            tick(2 * a + 1)
            if a == 0:
                pl.when(i > 0)(lambda: half_copy(i - 1, 1).start())
            else:
                half_copy(i, 0).start()
        return 0

    lax.fori_loop(0, 4, gather_part, 0)
    half_copy(3, 1).start()

    for z in range(4):
        for y in range(2):
            vecs[:, pl.ds((z * 2 + y) * 128, 128)] = VB[0, z, y, 0] + pltpu.roll(
                VB[0, z, y, 1], 64, 1
            )

    def saver(k, src, dst):
        return pltpu.make_async_copy(src, dst, outs.at[k])

    saved = [saver(0, vecs, o_vec)]
    saved[0].start()

    dacc[...] = jnp.zeros_like(dacc)
    nacc[...] = jnp.zeros_like(nacc)

    for i in range(SEQ):
        W_steps.step(16 + i, i, static=16 + i)
        half_wait(i, 0)
        half_wait(i, 1)

        def norm_part(n, _):
            rs_ = cut(i * 8 + n, 32)
            r = halves(rows, rs_)
            nrm[rs_, :] = (r * inv_rms(r) * vecs[1:2, :]).astype(bf)
            dd[rs_, :] = (gate_of(r, vecs[0:1, :]) * halves(cot, rs_)).astype(bf)
            return 0

        lax.fori_loop(0, 8, norm_part, 0)
        for c in range(4):
            cs = pl.ds(c * 256, 256)
            nT[cs, seq_rows(i)] = nrm[seq_rows(i), cs].T
            ddT[cs, seq_rows(i)] = dd[seq_rows(i), cs].T
    later = [saver(1, rows, o_rows), saver(2, cot, o_cot), saver(3, nT, o_nT)]
    for c in later:
        c.start()
    saved += later[:2]
    nT_saved = later[2]

    masks, low_half = head_masks()
    mask = causal_mask()

    def attend(i, hp):
        r_ = seq_rows(i)
        q, k, v = qkv[3 * hp, r_, :], qkv[3 * hp + 1, r_, :], qkv[3 * hp + 2, r_, :]
        mix = [dot(softmax_rows(q * masks[h], k, mask).astype(bf), v) for h in (0, 1)]
        mixed[hp, r_, :] = jnp.where(low_half, mix[0], mix[1]).astype(bf)

    def pair_part(hp, _):
        W_steps.step(20 + 4 * hp, 0)
        W_steps.step(21 + 4 * hp, 1)
        y = dot(nrm[...], wblocks(W, 3 * hp, 3)).astype(bf)
        for c in range(3):
            qkv[3 * hp + c] = y[:, c * 128 : c * 128 + 128]
        for i in range(SEQ):
            attend(i, hp)
            if i in (0, 2):
                W_steps.step(22 + 4 * hp + i // 2, 2 + i // 2)
        return 0

    lax.fori_loop(0, 4, pair_part, 0)
    later = [saver(4, qkv, o_qkv), saver(5, mixed, o_mix)]
    for c in later:
        c.start()
    saved += later

    def att_copy(i):
        return pltpu.make_async_remote_copy(
            P.at[seq_rows(i)],
            R.at[seq_rows(i)],
            asnd.at[i],
            arcv.at[i],
            device_id=other,
            device_id_type=MESH,
        )

    def norm_mlp(i):
        att_copy(i).wait_recv()

        def norm_part(n, _):
            rs_ = cut(i * 8 + n, 32)
            h = halves(rows, rs_) + (P[rs_, :].astype(f32) + R[rs_, :].astype(f32))
            nrm[rs_, :] = (h * inv_rms(h) * vecs[2:3, :]).astype(bf)
            return 0

        lax.fori_loop(0, 8, norm_part, 0)
        for c in range(4):
            cs = pl.ds(c * 256, 256)
            nT[cs, seq_rows(i)] = nrm[seq_rows(i), cs].T

    out_w = wblocks(W, 12, 4)

    def project_out(i):
        mix = jnp.concatenate([mixed[h, seq_rows(i), :] for h in range(4)], 1)
        P[seq_rows(i), :] = dot_nt(mix, out_w).astype(bf)

    W_steps.step(36, 0)
    project_out(0)
    project_out(1)
    att_copy(0).start()
    W_steps.step(37, 1)
    project_out(2)
    att_copy(1).start()
    project_out(3)
    att_copy(2).start()
    nT_saved.wait()
    W_steps.step(38, 2)
    norm_mlp(0)
    att_copy(3).start()
    norm_mlp(1)
    W_steps.step(39, 3)
    norm_mlp(2)
    norm_mlp(3)
    saved.append(saver(6, W.at[pl.ds(0, 16)], o_W))
    saved[-1].start()
    later = [saver(7, P, o_P), saver(8, R, o_R)]
    for c in later:
        c.start()
    saved += later

    def g_copy(m):
        slot = lax.rem(m, 2)
        return pltpu.make_async_copy(Gst.at[slot], o_G.at[pl.ds(m * 4, 4)], gout.at[slot])

    partials = [
        saver(9 + n, tokbuf.at[n // 2, pl.ds(n % 2 * 1024, 1024)], (o_down, o_back)[n // 2].at[n % 2])
        for n in range(4)
    ]

    def mlp_part(m, _):
        slot = lax.rem(m, 2)
        s = 40 + 4 * m
        up_w = wblocks(W, 16 + 4 * m, 2)
        down_w = wblocks(W, 18 + 4 * m, 2)
        for ht in range(2):
            hs_ = pl.ds(ht * 512, 512)
            W_steps.step(s + ht, ht, high=True)
            u = dot(nrm[hs_, :], up_w)
            d = dot(dd[hs_, :], down_w)
            c0 = 0.7978845608028654
            u2 = u * u
            s1 = 1.0 + jnp.tanh(u * (c0 + (c0 * 0.044715) * u2))
            h = 0.5 * u
            act[hs_, :] = (h * s1).astype(bf)
            slope = s1 * (0.5 + h * (2.0 - s1) * (c0 + (3 * 0.044715 * c0) * u2))
            dup[hs_, :] = (d * slope).astype(bf)
        W_steps.step(s + 2, 2, high=True)
        for ht in range(2):
            hs_ = pl.ds(ht * 512, 512)
            dacc[hs_, :] += dot_nt(act[hs_, :], down_w)
            nacc[hs_, :] += dot_nt(dup[hs_, :], up_w)
        W_steps.step(s + 3, 3, high=True)
        W_steps.drain(m, m + 1)

        @pl.when(m == 7)
        def _():
            for n, c in enumerate(partials):
                piece = (dacc, nacc)[n // 2][:, n % 2 * 512 : n % 2 * 512 + 512]
                tokbuf[n // 2, pl.ds(n % 2 * 1024, 1024), :] = piece.astype(bf)
                c.start()

        @pl.when(m >= 2)
        def _():
            g_copy(m - 2).wait()

        for ht in range(2):
            hs_ = pl.ds(ht * 512, 512)
            gu = dot(nT[hs_, :], dup[...]).astype(bf)
            Gst[slot, 0, hs_, :] = gu[:, :128]
            Gst[slot, 1, hs_, :] = gu[:, 128:]
            gd = dot(ddT[hs_, :], act[...]).astype(bf)
            Gst[slot, 2, hs_, :] = gd[:, :128]
            Gst[slot, 3, hs_, :] = gd[:, 128:]
        g_copy(m).start()
        return 0

    lax.fori_loop(0, 8, mlp_part, 0)
    saved += partials
    for i in range(SEQ):
        half_copy(i, 0).wait_send()
        half_copy(i, 1).wait_send()
    for i in range(SEQ):
        att_copy(i).wait_send()
    W_steps.drain(8, NB // PER)
    for j in range(5):
        V_steps.send(0, 0, j, act=lambda d: d.wait_send())
    g_copy(6).wait()
    g_copy(7).wait()
    for c in saved:
        c.wait()


def forward_call(chosen, tile, tok, cotangent, weights):
    bf, f32 = jnp.bfloat16, jnp.float32
    S = jax.ShapeDtypeStruct
    DMA = pltpu.SemaphoreType.DMA
    any_ = pl.BlockSpec(memory_space=HBM)
    vm = pltpu.VMEM
    return pl.pallas_call(
        forward_kernel,
        out_shape=(
            S((2, ROWS, 512), bf),
            S((2, ROWS, 512), bf),
            S((1024, ROWS), bf),
            S((12, ROWS, 128), bf),
            S((4, ROWS, 128), bf),
            S((ROWS, 1024), bf),
            S((ROWS, 1024), bf),
            S((2, ROWS, 512), bf),
            S((2, ROWS, 512), bf),
            S((16, 4, 2, 2, 64, 128), bf),
            S((32, 1024, 128), bf),
            S((8, 1024), f32),
        ),
        in_specs=[pl.BlockSpec(memory_space=pltpu.VMEM)] + [any_] * 9,
        out_specs=[any_] * 12,
        scratch_shapes=[
            vm((NB, 4, 2, 2, 64, 128), bf),
            vm((1, 4, 2, 2, 8, 128), f32),
            vm((8, 1024), f32),
            vm((2, ROWS, 512), bf),
            vm((2, ROWS, 512), bf),
            vm((2, 2048, 512), bf),
            vm((CAP, 2048), bf),
            vm((ROWS, 1024), bf),
            vm((1024, ROWS), bf),
            vm((ROWS, 1024), bf),
            vm((1024, ROWS), bf),
            vm((12, ROWS, 128), bf),
            vm((4, ROWS, 128), bf),
            vm((ROWS, 1024), bf),
            vm((ROWS, 1024), bf),
            vm((ROWS, 1024), f32),
            vm((ROWS, 1024), f32),
            vm((ROWS, 256), bf),
            vm((ROWS, 256), bf),
            vm((2, 4, 1024, 128), bf),
            DMA((NB, 8)),
            DMA((NB, 8)),
            DMA((1, 8)),
            DMA((1, 8)),
            DMA((4, 2)),
            DMA((4, 2)),
            DMA((4,)),
            DMA((4,)),
            DMA((NB + 1,)),
            DMA((2,)),
            DMA((13,)),
            DMA((2,)),
        ],
        compiler_params=pltpu.CompilerParams(
            collective_id=1, has_side_effects=True, vmem_limit_bytes=63 * 1024 * 1024
        ),
        name="forward",
    )(chosen, tile, tok, cotangent, *weights)


def backward_kernel(
    rows,
    cot,
    nT_in,
    qkv_in,
    mix_in,
    P_in,
    R_in,
    down_in,
    back_in,
    W_in,
    G_in,
    vec_in,
    o_newr,
    o_newg,
    sum_out,
    o_vec,
    o_sum,
    G,
    Wa,
    qkv,
    mixed,
    nT,
    vecs,
    DR,
    NR,
    R1,
    bufs,
    buf2,
    da,
    daT,
    dmix,
    newr,
    newg,
    dhid,
    dlog,
    accs,
    GV,
    base,
    gsem,
    lsem,
    psem,
    prcv,
    qsem,
    qrcv,
    tout,
    *landing,
):
    p = Place()
    t = p.t
    other = {"tensor": 1 - t}
    f32, bf = jnp.float32, jnp.bfloat16
    wide, small = landing[:8], landing[8:]
    greet_all(p)

    def g_load(c):
        return pltpu.make_async_copy(G_in.at[pl.ds(4 * c, 4)], G.at[pl.ds(4 * c, 4)], gsem.at[c])

    g_load(0).start()
    g_load(1).start()

    def stream(s, names):
        q = lax.rem(s, 2)
        out = []
        for k in names:
            if k < 2:
                src = (P_in, R_in)[k].at[cut(s, CAP)]
                dst = buf2.at[q, k]
            else:
                src = (rows, cot, down_in, back_in)[k - 2].at[:, cut(s, CAP)]
                dst = bufs.at[q, k - 2]
            out.append(pltpu.make_async_copy(src, dst, lsem.at[q, k]))
        return out

    everything = (0, 1, 2, 3, 4, 5)
    for c in stream(0, everything):
        c.start()
    fixed = [
        pltpu.make_async_copy(a, b, base.at[i])
        for i, (a, b) in enumerate(
            ((vec_in, vecs), (W_in, Wa), (qkv_in, qkv), (mix_in, mixed), (nT_in, nT))
        )
    ]
    for c in fixed[:3]:
        c.start()
    await_all(p)

    def pair_copy(s, e):
        return pltpu.make_async_remote_copy(
            (down_in, back_in)[e].at[:, cut(s, CAP)],
            (DR, NR)[e].at[:, cut(s, CAP)],
            psem.at[s, e],
            prcv.at[s, e],
            device_id=other,
            device_id_type=MESH,
        )

    pair_copy(0, 0).start()
    pair_copy(0, 1).start()
    steps = Scatter(p, G, o_sum, *wide)
    v_steps = Scatter(p, GV, o_vec, *small)

    accs[...] = jnp.zeros_like(accs)

    def fold(v):
        return jnp.sum(v.reshape(4, 8, 1024), 0)

    def pick(v):
        return jnp.where(t == 0, v[:, :512], v[:, 512:])

    masks, low_half = head_masks()
    seen = lax.broadcasted_iota(jnp.int32, (CAP, CAP), 0) <= lax.broadcasted_iota(
        jnp.int32, (CAP, CAP), 1
    )

    def seq_part(s, _):
        def tick(q):
            if q % 4 == 0:
                g_load(2 * s + q // 4).wait()

                @pl.when(s < 3)
                def _():
                    g_load(2 * s + q // 4 + 2).start()

            steps.step(8 * s + q, q % 4, low=True)

        tick(0)
        q = lax.rem(s, 2)

        @pl.when(s + 1 < SEQ)
        def _():
            for c in stream(s + 1, everything):
                c.start()
            pair_copy(s + 1, 0).start()
            pair_copy(s + 1, 1).start()

        pl.when(s == 0)(lambda: fixed[0].wait())
        for c in stream(s, everything):
            c.wait()
        for e in range(2):
            pair_copy(s, e).wait_recv()

        def part(n, _):
            rs_ = cut(n, 32)
            as_ = pl.ds(pl.multiple_of(s * CAP + n * 32, 32), 32)

            def mine(k):
                return jnp.concatenate([bufs[q, k, 0, rs_, :], bufs[q, k, 1, rs_, :]], 1).astype(f32)

            r, c = mine(0), mine(1)
            att = buf2[q, 0, rs_, :].astype(f32) + buf2[q, 1, rs_, :].astype(f32)
            h = r + att
            branch = att + (mine(2) + halves(DR, as_))
            dn = mine(3) + halves(NR, as_)
            inv = inv_rms(h)
            sc = dn * vecs[2:3, :]
            dh = inv * sc - h * (inv * inv * inv * jnp.mean(sc * h, -1, keepdims=True))
            gate = gate_of(r, vecs[0:1, :])
            dl = jnp.sum(c * branch, -1, keepdims=True) * (gate * (1.0 - gate))
            da[rs_, :] = (gate * c + dh).astype(bf)
            accs[2] += fold(dn * (h * inv))
            accs[0] += fold(r * dl)
            newr[as_, :] = pick(r + gate * branch).astype(bf)
            dhid[as_, :] = pick(dh)
            dlog[as_, :] = jnp.broadcast_to(dl, (32, 128))
            return 0

        lax.fori_loop(0, 4, part, 0)
        tick(1)
        lax.fori_loop(4, 8, part, 0)
        tick(2)
        for c in range(4):
            cs = pl.ds(c * 256, 256)
            daT[cs, cut(s, CAP)] = da[:, cs].T

        @pl.when(s == 0)
        def _():
            for c in fixed[1:3]:
                c.wait()
            for c in fixed[3:]:
                c.start()

        tick(3)
        dm = dot(da[...], wblocks(Wa, 12, 4)).astype(bf)
        for h in range(4):
            dmix[h] = dm[:, h * 128 : h * 128 + 128]

        def pair_back(hp):
            r_ = cut(s, CAP)
            qh, kh, vh = [qkv[3 * hp + c, r_, :] for c in range(3)]
            dmh = dmix[hp]
            outs = []
            for h in (0, 1):
                sc = jnp.where(seen, dot_nt(kh, qh * masks[h]) * (HD**-0.5), -1e30)
                e = jnp.exp(sc - jnp.max(sc, 0, keepdims=True))
                pr = e * (1.0 / jnp.sum(e, 0, keepdims=True))
                dv = dot(pr.astype(bf), dmh)
                dp = dot_nt(vh * masks[h], dmh)
                ds = (pr * (dp - jnp.sum(dp * pr, 0, keepdims=True))).astype(bf)
                outs.append((dot(ds.T, kh), dot(ds, qh), dv))
            scale = HD**-0.5
            for i, (a, b) in enumerate(zip(*outs)):
                v = jnp.where(low_half, a, b)
                qkv[3 * hp + i, r_, :] = (v if i == 2 else v * scale).astype(bf)

        for hp in range(4):
            tick(4 + hp)
            pair_back(hp)
        return 0

    lax.fori_loop(0, SEQ, seq_part, 0)
    row_outs = [pltpu.make_async_copy(newr, o_newr, tout.at[0])]
    row_outs[0].start()

    def grad_unit(leftT, a, b, first):
        y = jnp.concatenate([a, b], 1)
        for ht in range(2):
            g = dot(leftT[pl.ds(ht * 512, 512), :], y).astype(bf)
            for c in range(2):
                G[first + c, pl.ds(ht * 2, 2)] = g[:, c * 128 : c * 128 + 128].reshape(
                    2, 2, 2, 64, 128
                )

    def back_copy(s):
        return pltpu.make_async_remote_copy(
            DR.at[:, seq_rows(s)],
            R1.at[:, seq_rows(s)],
            qsem.at[s],
            qrcv.at[s],
            device_id=other,
            device_id_type=MESH,
        )

    for s in range(2):
        for c in stream(s, (2, 3)):
            c.start()
    for c in fixed[3:]:
        c.wait()
    grad_unit(daT, mixed[0], mixed[1], 32)
    grad_unit(daT, mixed[2], mixed[3], 34)

    def grad_part(n, _):
        for e in range(2):
            steps.step(32 + 4 * n + 2 * e, 2 * e)
            steps.step(33 + 4 * n + 2 * e, 2 * e + 1)
            j = 2 * n + e
            grad_unit(nT, qkv[2 * j], qkv[2 * j + 1], 36 + 2 * j)
        return 0

    lax.fori_loop(0, 3, grad_part, 0)
    for s in range(SEQ):
        steps.step(44 + s, s)
        y = 0.0
        for g in range(3):
            x = jnp.concatenate([qkv[4 * g + i, seq_rows(s), :] for i in range(4)], 1)
            y = y + dot_nt(x, wblocks(Wa, 4 * g, 4))
        y = y.astype(bf)
        DR[0, seq_rows(s), :] = y[:, :512]
        DR[1, seq_rows(s), :] = y[:, 512:]
        if s > 0:
            back_copy(s - 1).start()
    steps.step(48, 0, high=True)
    back_copy(3).start()

    route_half = jnp.where(t == 0, vecs[0:1, :512], vecs[0:1, 512:])
    for s in range(SEQ):
        steps.step(49 + s, (1 + s) % 4, high=True)
        steps.drain(2 * s, 2 * s + 2)
        q = s % 2
        for c in stream(s, (2, 3)):
            c.wait()
        back_copy(s).wait_recv()

        def part(n, _):
            rs_ = cut(n, 32)
            as_ = pl.ds(pl.multiple_of(s * CAP + n * 32, 32), 32)
            r = jnp.concatenate([bufs[q, 0, 0, rs_, :], bufs[q, 0, 1, rs_, :]], 1).astype(f32)
            dn = halves(DR, as_) + halves(R1, as_)
            inv = inv_rms(r)
            sc = dn * vecs[1:2, :]
            dr = inv * sc - r * (inv * inv * inv * jnp.mean(sc * r, -1, keepdims=True))
            accs[1] += fold(dn * (r * inv))
            dl = dlog[as_, :]
            dl = jnp.concatenate([dl, dl, dl, dl], 1)
            ch = bufs[q, 1, t, rs_, :].astype(f32)
            newg[as_, :] = (ch + (dhid[as_, :] + pick(dr) + dl * route_half)).astype(bf)
            return 0

        lax.fori_loop(0, 8, part, 0)
        if s + 2 < SEQ:
            for c in stream(s + 2, (2, 3)):
                c.start()

    for z in range(4):
        for y in range(2):
            cs = pl.ds((z * 2 + y) * 128, 128)
            tile = jnp.concatenate(
                [jnp.sum(accs[k, :, cs], 0, keepdims=True) for k in range(3)]
                + [jnp.zeros((5, 128), f32)],
                0,
            )
            GV[0, z, y, 0] = tile
            GV[0, z, y, 1] = pltpu.roll(tile, 64, 1)
    for s in range(SEQ):
        back_copy(s).wait_send()
    row_outs.append(pltpu.make_async_copy(newg, o_newg, tout.at[1]))
    row_outs[1].start()
    v_steps.send(0, 0, 0)

    def sum_copy(e):
        part = pl.ds(32, 16) if e else pl.ds(0, 32)
        return pltpu.make_async_copy(o_sum.at[part], sum_out.at[part], tout.at[2 + e])

    for k, s in enumerate(range(53, 67)):
        steps.step(s, s % PER, static=s)
        if s == 53:
            sum_copy(0).start()
        if k in (0, 2, 3, 5, 7):
            j = (0, 2, 3, 5, 7).index(k) + 1
            v_steps.recv(0, 0, j - 1)
            if j < 5:
                v_steps.send(0, 0, j)
    sum_copy(1).start()
    for c in row_outs:
        c.wait()
    for s in range(SEQ):
        for e in range(2):
            pair_copy(s, e).wait_send()
    for j in range(5):
        v_steps.send(0, 0, j, act=lambda d: d.wait_send())
    steps.drain(8, NB // PER)
    sum_copy(0).wait()
    sum_copy(1).wait()


def backward_call(kept):
    bf, f32 = jnp.bfloat16, jnp.float32
    S = jax.ShapeDtypeStruct
    DMA = pltpu.SemaphoreType.DMA
    any_ = pl.BlockSpec(memory_space=HBM)
    vspec = pl.BlockSpec(memory_space=pltpu.VMEM)
    vm = pltpu.VMEM
    return pl.pallas_call(
        backward_kernel,
        out_shape=(
            S((ROWS, 512), bf),
            S((ROWS, 512), bf),
            S((NB, 64, 128), f32),
            S((1, 8, 128), f32),
        ),
        in_specs=[any_] * 12,
        out_specs=[any_, any_, any_, vspec],
        scratch_shapes=[
            vm((NB, 64, 128), f32),
            vm((NB, 4, 2, 2, 64, 128), bf),
            vm((16, 4, 2, 2, 64, 128), bf),
            vm((12, ROWS, 128), bf),
            vm((4, ROWS, 128), bf),
            vm((1024, ROWS), bf),
            vm((8, 1024), f32),
            vm((2, ROWS, 512), bf),
            vm((2, ROWS, 512), bf),
            vm((2, ROWS, 512), bf),
            vm((2, 4, 2, CAP, 512), bf),
            vm((2, 2, CAP, 1024), bf),
            vm((CAP, 1024), bf),
            vm((1024, ROWS), bf),
            vm((4, CAP, 128), bf),
            vm((ROWS, 512), bf),
            vm((ROWS, 512), bf),
            vm((ROWS, 512), f32),
            vm((ROWS, 128), f32),
            vm((3, 8, 1024), f32),
            vm((1, 4, 2, 2, 8, 128), f32),
            DMA((5,)),
            DMA((8,)),
            DMA((2, 6)),
            DMA((4, 2)),
            DMA((4, 2)),
            DMA((4,)),
            DMA((4,)),
            DMA((4,)),
        ]
        + Scatter.landing(NB, (64, 128), bf)
        + Scatter.landing(PER, (8, 128), f32),
        compiler_params=pltpu.CompilerParams(
            collective_id=2, has_side_effects=True, vmem_limit_bytes=63 * 1024 * 1024
        ),
        name="backward",
    )(*kept)


def place_kernel(
    spot_ref,
    own_ref,
    newr,
    newg,
    tok,
    cot,
    o_tok,
    o_cot,
    g_q,
    g_k,
    g_v,
    g_out,
    g_up,
    g_down,
    old,
    out,
    new,
    came,
    went,
    own,
    nsem,
    gsem,
):
    bf = jnp.bfloat16

    def piece(n):
        return n // (2048 // SIZE), cut(n % (2048 // SIZE), SIZE)

    def load(n, a):
        i, rs = piece(n)
        return pltpu.make_async_copy((tok, cot)[a].at[i, rs], old.at[a, n], came.at[a, n])

    def store(n, a):
        i, rs = piece(n)
        return pltpu.make_async_copy(out.at[a, n], (o_tok, o_cot)[a].at[i, rs], went.at[a, n])

    pieces = SEQ * 2048 // SIZE
    news = [pltpu.make_async_copy((newr, newg)[a], new.at[a], nsem.at[a]) for a in range(2)]
    sums = pltpu.make_async_copy(own_ref, own, nsem.at[2])
    for c in news + [sums]:
        c.start()

    def start(n, _):
        load(n, 0).start()
        load(n, 1).start()
        return 0

    lax.fori_loop(0, pieces, start, 0)

    moves = []
    for b in range(NB):
        if b < 32:
            ref, k = (g_up, g_down)[b % 4 // 2], b // 4 * 2 + b % 2
        else:
            ref, k = (g_out, b - 32) if b < 36 else ((g_q, g_k, g_v)[b % 3], (b - 36) // 3)
        moves.append(
            pltpu.make_async_copy(own.at[b], ref.at[:, pl.ds(k * 128, 128)], gsem.at[b])
        )
    for c in news:
        c.wait()
    ones = jnp.ones((CAP, 128), bf)

    def place(n, _):
        i, _rs = piece(n)

        @pl.when(n == 2)
        def _():
            sums.wait()
            for c in moves:
                c.start()

        row = lax.broadcasted_iota(jnp.int32, (SIZE, CAP), 0) + n % (2048 // SIZE) * SIZE
        hit = jnp.where(row == spot_ref[i], 1.0, 0.0).astype(bf)
        kept = 1.0 - dot(hit, ones)
        kept = jnp.concatenate([kept, kept, kept, kept], 1).astype(bf)
        for a in range(2):
            moved = dot(hit, new[a, cut(i, CAP), :]).astype(bf)
            load(n, a).wait()
            out[a, n] = old[a, n] * kept + moved
            store(n, a).start()
        return 0

    lax.fori_loop(0, pieces, place, 0)

    def finish(n, _):
        store(n, 0).wait()
        store(n, 1).wait()
        return 0

    lax.fori_loop(0, pieces, finish, 0)
    for c in moves:
        c.wait()


SIZE = 1024


def place_call(spot, own, newr, newg, tok, cotangent):
    bf, f32 = jnp.bfloat16, jnp.float32
    S = jax.ShapeDtypeStruct
    DMA = pltpu.SemaphoreType.DMA
    any_ = pl.BlockSpec(memory_space=pltpu.MemorySpace.HBM)
    pieces = SEQ * 2048 // SIZE
    return pl.pallas_call(
        place_kernel,
        out_shape=(
            S((SEQ, 2048, 512), bf),
            S((SEQ, 2048, 512), bf),
            S((64, 512), f32),
            S((64, 512), f32),
            S((64, 512), f32),
            S((64, 512), f32),
            S((64, 2048), f32),
            S((64, 2048), f32),
        ),
        in_specs=[pl.BlockSpec(memory_space=pltpu.VMEM)] + [any_] * 5,
        out_specs=[any_] * 8,
        scratch_shapes=[
            pltpu.VMEM((2, pieces, SIZE, 512), bf),
            pltpu.VMEM((2, pieces, SIZE, 512), bf),
            pltpu.VMEM((2, ROWS, 512), bf),
            DMA((2, pieces)),
            DMA((2, pieces)),
            pltpu.VMEM((NB, 64, 128), f32),
            DMA((3,)),
            DMA((NB,)),
        ],
        compiler_params=pltpu.CompilerParams(vmem_limit_bytes=63 * 1024 * 1024),
        name="place_rows",
    )(spot, own, newr, newg, tok, cotangent)


def to_tile(w_route, gain_attn, gain_mlp):
    v = jnp.stack([w_route, gain_attn, gain_mlp]).astype(jnp.float32)
    return jnp.pad(v, ((0, 5), (0, 64)))


def fused(
    tokens,
    routed,
    w_query,
    w_key,
    w_value,
    w_out,
    w_up,
    w_down,
    w_route,
    gain_attn,
    gain_mlp,
    cotangent,
):
    tok = tokens.reshape(SEQ, 2048, 512)
    cot = cotangent.reshape(SEQ, 2048, 512)
    spot = routed.reshape(SEQ, 1, CAP)
    tile = to_tile(w_route, gain_attn, gain_mlp)
    weights = (w_query, w_key, w_value, w_out.T, w_up, w_down.T)
    kept = list(forward_call(spot, tile, tok, cot, weights))
    kept[10] = kept[10].reshape(32, 4, 2, 2, 64, 128)
    newr, newg, own, vec = backward_call(kept)
    vec = vec[0, :3, :64]
    output, grad, g_q, g_k, g_v, g_out, g_up, g_down = place_call(
        spot, own, newr, newg, tok, cot
    )
    return (
        output.reshape(tokens.shape),
        grad.reshape(tokens.shape),
        g_q,
        g_k,
        g_v,
        g_out.T,
        g_up,
        g_down.T,
        vec[0],
        vec[1],
        vec[2],
    )


def shards(tokens, routed, *rest):
    sizes = (lax.axis_size("dp"), lax.axis_size("tensor"))
    here = tokens.shape == (4, 1, 2048, 512) and routed.shape == (4, 1, 256)
    if sizes == (16, 2) and here:
        return fused(tokens, routed, *rest)
    return plain(tokens, routed, *rest)


def solution(mesh):
    rows = P("dp", "tensor")
    columns = P("tensor", "dp")
    vector = P("dp")
    stored = P(None, "dp", None, "tensor")
    return jax.shard_map(
        shards,
        mesh=mesh,
        in_specs=(
            stored,
            P(None, "dp", None),
            rows,
            rows,
            rows,
            columns,
            rows,
            columns,
            vector,
            vector,
            vector,
            stored,
        ),
        out_specs=(
            stored,
            stored,
            rows,
            rows,
            rows,
            columns,
            rows,
            columns,
            vector,
            vector,
            vector,
        ),
        check_vma=False,
    )
```

```python
import jax
import jax.numpy as jnp
from jax import lax
from jax.experimental import pallas as pl
from jax.experimental.pallas import tpu as pltpu
from jax.sharding import PartitionSpec as P

HD = 64
eps_norm = 1e-05


def dense(left, right):
    return jnp.dot(left, right, preferred_element_type=jnp.float32)


def dense_t(left, right):
    return lax.dot_general(
        left, right, (((1,), (1,)), ((), ())), preferred_element_type=jnp.float32
    )


def dense_g(left, right):
    return lax.dot_general(
        left, right, (((0,), (0,)), ((), ())), preferred_element_type=jnp.float32
    )


def rms_back(values, inv, gain, grad):
    grad_gain = jnp.sum(grad * values * inv, 0)
    scaled = grad * gain
    dot = jnp.mean(scaled * values, -1, keepdims=True)
    return inv * scaled - values * (inv * inv * inv) * dot, grad_gain


def plain(
    tokens,
    routed,
    w_query,
    w_key,
    w_value,
    w_out,
    w_up,
    w_down,
    w_route,
    gain_attn,
    gain_mlp,
    cotangent,
):
    micro, seqs, length, half_width = tokens.shape
    capacity = routed.shape[2]
    batch = micro * seqs
    total = batch * capacity
    cols = w_query.shape[1]
    hidden_cols = w_up.shape[1]
    width = half_width * lax.axis_size("tensor")
    offset = lax.axis_index("tensor") * half_width
    scale = HD ** (-0.5)
    swap = [(0, 1), (1, 0)]

    vec = jnp.stack([w_route, gain_attn, gain_mlp], 1)
    vec = jnp.pad(vec, ((0, 0), (0, 125)))
    packed = jnp.concatenate([w_query, w_key, w_value, w_up, w_out.T, w_down.T, vec], 1)
    gathered = lax.all_gather(packed, "dp", axis=0, tiled=True)
    b1, b2, b3 = cols, 2 * cols, 3 * cols
    b4 = b3 + hidden_cols
    b5 = b4 + w_out.shape[0]
    b6 = b5 + w_down.shape[0]
    fq = gathered[:, :b1]
    fk = gathered[:, b1:b2]
    fv = gathered[:, b2:b3]
    fup = gathered[:, b3:b4]
    foutT = gathered[:, b4:b5]
    fdownT = gathered[:, b5:b6]
    route = gathered[:, b6]
    route_f32 = route.astype(jnp.float32)
    gain1 = gathered[:, b6 + 1].astype(jnp.float32)
    gain2 = gathered[:, b6 + 2].astype(jnp.float32)

    tok = tokens.reshape(batch, length, half_width)
    cot = cotangent.reshape(batch, length, half_width)
    chosen = routed.reshape(batch, capacity)
    rows_half = jnp.take_along_axis(tok, chosen[:, :, None], axis=1).reshape(total, half_width)
    cot_half = jnp.take_along_axis(cot, chosen[:, :, None], axis=1).reshape(total, half_width)
    rows = lax.all_gather(rows_half, "tensor", axis=1, tiled=True)
    cot_rows = lax.all_gather(cot_half, "tensor", axis=1, tiled=True)

    rows_f = rows.astype(jnp.float32)
    cot_f = cot_rows.astype(jnp.float32)
    gate = jax.nn.sigmoid(dense(rows, route))
    inv1 = lax.rsqrt(jnp.mean(rows_f * rows_f, -1, keepdims=True) + eps_norm)
    normed = (rows_f * inv1 * gain1).astype(jnp.bfloat16)
    heads = cols // HD

    def split(x):
        return x.astype(jnp.bfloat16).reshape(batch, capacity, heads, HD).transpose(0, 2, 1, 3)

    def join(x):
        return x.transpose(0, 2, 1, 3).reshape(total, cols)

    q = split(dense(normed, fq))
    k = split(dense(normed, fk))
    v = split(dense(normed, fv))
    causal = lax.broadcasted_iota(jnp.int32, (capacity, capacity), 0) >= lax.broadcasted_iota(
        jnp.int32, (capacity, capacity), 1
    )
    scores = jnp.einsum("bhqd,bhkd->bhqk", q, k, preferred_element_type=jnp.float32) * scale
    scores = jnp.where(causal, scores, -1e30)
    peak = jnp.max(scores, -1, keepdims=True)
    expd = jnp.exp(scores - peak)
    probs = expd / jnp.sum(expd, -1, keepdims=True)
    probs_low = probs.astype(jnp.bfloat16)
    mixed = jnp.einsum("bhqk,bhkd->bhqd", probs_low, v, preferred_element_type=jnp.float32)
    mixed = join(mixed.astype(jnp.bfloat16))

    def pair_sum(x):
        low = x.astype(jnp.bfloat16)
        other = lax.ppermute(low, "tensor", swap)
        return low.astype(jnp.float32) + other.astype(jnp.float32)

    attended = pair_sum(dense_t(mixed, foutT))
    hidden = rows_f + attended
    inv2 = lax.rsqrt(jnp.mean(hidden * hidden, -1, keepdims=True) + eps_norm)
    normed2 = (hidden * inv2 * gain2).astype(jnp.bfloat16)
    up = dense(normed2, fup)
    act32, gelu_back = jax.vjp(jax.nn.gelu, up)
    act = act32.astype(jnp.bfloat16)
    down = pair_sum(dense_t(act, fdownT))
    branch = attended + down
    d_logit = jnp.sum(cot_f * branch, -1) * gate * (1.0 - gate)
    branch_half = lax.dynamic_slice_in_dim(branch, offset, half_width, 1)
    new_rows = (rows_half.astype(jnp.float32) + gate[:, None] * branch_half).astype(jnp.bfloat16)

    d_branch = gate[:, None] * cot_f
    d_down = d_branch.astype(jnp.bfloat16)
    g_downT = dense_g(d_down, act)
    d_act = dense(d_down, fdownT)
    d_upper = gelu_back(d_act)[0].astype(jnp.bfloat16)
    g_up = dense_g(normed2, d_upper)
    d_normed2 = pair_sum(dense_t(d_upper, fup))
    d_hidden, g_gain2 = rms_back(hidden, inv2, gain2, d_normed2)
    d_attended = (d_branch + d_hidden).astype(jnp.bfloat16)
    g_outT = dense_g(d_attended, mixed)
    d_mixed = split(dense(d_attended, foutT))
    d_values = jnp.einsum("bhqk,bhqd->bhkd", probs_low, d_mixed, preferred_element_type=jnp.float32)
    d_values = join(d_values.astype(jnp.bfloat16))
    d_probs = jnp.einsum("bhqd,bhkd->bhqk", d_mixed, v, preferred_element_type=jnp.float32)
    d_scores = probs * (d_probs - jnp.sum(d_probs * probs, -1, keepdims=True))
    d_scores = d_scores.astype(jnp.bfloat16)
    d_q = jnp.einsum("bhqk,bhkd->bhqd", d_scores, k, preferred_element_type=jnp.float32) * scale
    d_k = jnp.einsum("bhqk,bhqd->bhkd", d_scores, q, preferred_element_type=jnp.float32) * scale
    d_q = join(d_q.astype(jnp.bfloat16))
    d_k = join(d_k.astype(jnp.bfloat16))
    g_q = dense_g(normed, d_q)
    g_k = dense_g(normed, d_k)
    g_v = dense_g(normed, d_values)
    d_normed = pair_sum(dense_t(d_q, fq) + dense_t(d_k, fk) + dense_t(d_values, fv))
    d_rows, g_gain1 = rms_back(rows_f, inv1, gain1, d_normed)
    g_route = jnp.sum(rows_f * d_logit[:, None], 0)
    d_half = (
        lax.dynamic_slice_in_dim(d_hidden + d_rows, offset, half_width, 1)
        + d_logit[:, None] * lax.dynamic_slice_in_dim(route_f32, offset, half_width, 0)[None, :]
    )
    grad_rows = (cot_half.astype(jnp.float32) + d_half).astype(jnp.bfloat16)

    seq_ids = lax.broadcasted_iota(jnp.int32, (batch, capacity), 0)
    output = tok.at[seq_ids, chosen].set(
        new_rows.reshape(batch, capacity, half_width), unique_indices=True
    )
    input_grad = cot.at[seq_ids, chosen].set(
        grad_rows.reshape(batch, capacity, half_width), unique_indices=True
    )

    g_vec = jnp.pad(jnp.stack([g_route, g_gain1, g_gain2], 1), ((0, 0), (0, 125)))
    grads = jnp.concatenate(
        [x.astype(jnp.bfloat16) for x in (g_q, g_k, g_v, g_up, g_outT, g_downT, g_vec)], 1
    )
    own = lax.psum_scatter(grads, "dp", scatter_dimension=0, tiled=True).astype(jnp.float32)
    return (
        output.reshape(tokens.shape),
        input_grad.reshape(tokens.shape),
        own[:, :b1],
        own[:, b1:b2],
        own[:, b2:b3],
        own[:, b4:b5].T,
        own[:, b3:b4],
        own[:, b5:b6].T,
        own[:, b6],
        own[:, b6 + 1],
        own[:, b6 + 2],
    )


MESH = pl.DeviceIdType.MESH
NB = 48
PATTERN = "XYZX"
PER = 4
GATHER_LAGS = {
    "X": (0, 3, 6, 9, 12, 19),
    "Y": (0, 4, 7, 9, 13, 19),
    "Z": (0, 5, 9, 12, 15, 19),
}
SCATTER_LAGS = {
    "X": (0, 4, 7, 9, 13, 18),
    "Y": (0, 4, 8, 10, 12, 17),
    "Z": (0, 2, 5, 9, 14, 19),
}
VECTOR_STEPS = (0, 3, 6, 9, 12, 15)


class Place:
    def __init__(self):
        me = lax.axis_index("dp")
        self.x = me % 2
        self.y = (me // 2) % 2
        self.z = me // 4
        self.nx = me + 1 - 2 * self.x
        self.ny = me + 2 - 4 * self.y
        self.up = jnp.minimum(me + 4, 15)
        self.dn = jnp.maximum(me - 4, 0)
        self.t = lax.axis_index("tensor")


def both(a, b):
    return jnp.logical_and(a, b)


def greet_all(p):
    bar = pltpu.get_barrier_semaphore()

    def greet(dev):
        pl.semaphore_signal(bar, inc=1, device_id=dev, device_id_type=MESH)

    greet({"dp": p.nx})
    greet({"dp": p.ny})
    greet({"tensor": 1 - p.t})

    @pl.when(p.z < 3)
    def _():
        greet({"dp": p.up})

    @pl.when(p.z > 0)
    def _():
        greet({"dp": p.dn})


def await_all(p):
    bar = pltpu.get_barrier_semaphore()
    inner = both(p.z > 0, p.z < 3)

    @pl.when(inner)
    def _():
        pl.semaphore_wait(bar, 5)

    @pl.when(jnp.logical_not(inner))
    def _():
        pl.semaphore_wait(bar, 4)


class Steps:
    def step(self, s, pos, static=None, low=False, high=False):
        live = []
        for c, lags in self.lags.items():
            for j in range(6):
                q = (pos - lags[j]) % PER
                if PATTERN[q] == c and (static is None or 0 <= static - lags[j] < NB):
                    live.append((j, lags[j], q))
        live.sort(reverse=True)

        def do(j, lag, q, act):
            b = s - lag
            if low:
                pl.when(b >= 0)(lambda: act(b, q, j))
            elif high:
                pl.when(b < NB)(lambda: act(b, q, j))
            else:
                act(b, q, j)

        for j, lag, q in live:
            if j == 0:
                do(j, lag, q, self.send)
        for j, lag, q in live:
            if j > 0:
                do(j, lag, q, lambda b, q, j: self.recv(b, q, j - 1))
            if self.relay and 0 < j < 5:
                do(j, lag, q, self.send)
        for j, lag, q in live:
            if not self.relay and 0 < j < 5:
                do(j, lag, q, self.send)

    def drain(self, first, last):
        def body(r, _):
            for pos in range(PER):
                for j in range(5):
                    self.send(r * PER + pos, pos, j, act=lambda d: d.wait_send())
            return 0

        lax.fori_loop(first, last, body, 0)


class Gather(Steps):
    lags = GATHER_LAGS
    relay = True

    def __init__(self, p, W, ss, rs):
        self.p, self.W, self.ss, self.rs = p, W, ss, rs

    def copy(self, ref, b, k, dev):
        return pltpu.make_async_remote_copy(
            ref, ref, self.ss.at[b, k], self.rs.at[b, k], device_id={"dp": dev}, device_id_type=MESH
        )

    def zref(self, b, c, zz):
        zz = jnp.clip(zz, 0, 3)
        return self.W.at[b, zz] if c == "Z" else self.W.at[b, zz, self.p.y, self.p.x]

    def zsend(self, b, c, hop, act):
        p = self.p

        @pl.when(both(p.z - hop + 1 >= 0, p.z < 3))
        def _():
            act(self.copy(self.zref(b, c, p.z - hop + 1), b, hop - 1, p.up))

        @pl.when(both(p.z + hop - 1 <= 3, p.z > 0))
        def _():
            act(self.copy(self.zref(b, c, p.z + hop - 1), b, 2 + hop, p.dn))

    def zrecv(self, b, c, hop):
        p = self.p

        @pl.when(p.z - hop >= 0)
        def _():
            self.copy(self.zref(b, c, p.z - hop), b, hop - 1, p.nx).wait_recv()

        @pl.when(p.z + hop <= 3)
        def _():
            self.copy(self.zref(b, c, p.z + hop), b, 2 + hop, p.nx).wait_recv()

    def stage(self, b, c, j):
        W = self.W
        x, y, z = self.p.x, self.p.y, self.p.z
        if c == "X":
            line = (7, W.at[b, :, :, x], W.at[b, :, :, 1 - x])
            return (1, 2, 3, (6, W.at[b, :, y, x], W.at[b, :, 1 - y, x]), line)[j]
        if c == "Y":
            line = (6, W.at[b, :, y], W.at[b, :, 1 - y])
            return (1, 2, 3, (7, W.at[b, :, y, x], W.at[b, :, y, 1 - x]), line)[j]
        line = (7, W.at[b, z, y, x], W.at[b, z, y, 1 - x])
        return (line, (6, W.at[b, z, y], W.at[b, z, 1 - y]), 1, 2, 3)[j]

    def send(self, b, pos, j, act=lambda d: d.start()):
        c = PATTERN[pos]
        st = self.stage(b, c, j)
        if isinstance(st, int):
            self.zsend(b, c, st, act)
        else:
            act(self.copy(st[1], b, st[0], self.p.ny if st[0] == 6 else self.p.nx))

    def recv(self, b, pos, j):
        c = PATTERN[pos]
        st = self.stage(b, c, j)
        if isinstance(st, int):
            self.zrecv(b, c, st)
        else:
            self.copy(st[2], b, st[0], self.p.nx).wait_recv()


class Scatter(Steps):
    lags = SCATTER_LAGS
    relay = False

    def __init__(self, p, G, out, L8, L4, LZ, P4, P2, P1, ss, rs):
        self.p, self.G, self.out, self.ss, self.rs = p, G, out, ss, rs
        self.L8, self.L4, self.LZ, self.P4, self.P2, self.P1 = L8, L4, LZ, P4, P2, P1

    def slot(self, b, pos):
        r = b // PER
        return r if PATTERN[pos] == "Z" else r * 3 + {0: 0, 1: 1, 3: 2}[pos]

    def copy(self, src, dst, b, k, dev):
        return pltpu.make_async_remote_copy(
            src, dst, self.ss.at[b, k], self.rs.at[b, k], device_id={"dp": dev}, device_id_type=MESH
        )

    def gz(self, b, c, t):
        t = jnp.clip(t, 0, 3)
        return self.G.at[b, t] if c == "Z" else self.G.at[b, t, self.p.y, self.p.x]

    def lz(self, b, pos, k):
        i = self.slot(b, pos)
        return self.P4.at[i, k] if PATTERN[pos] == "Z" else self.LZ.at[i, k]

    def add(self, ref, land):
        ref[...] = (ref[...].astype(jnp.float32) + land[...].astype(jnp.float32)).astype(ref.dtype)

    def zsend(self, b, pos, hop, act):
        p, c = self.p, PATTERN[pos]

        @pl.when(p.z + hop <= 3)
        def _():
            act(self.copy(self.gz(b, c, p.z + hop), self.lz(b, pos, hop - 1), b, hop - 1, p.up))

        @pl.when(p.z - hop >= 0)
        def _():
            act(self.copy(self.gz(b, c, p.z - hop), self.lz(b, pos, 2 + hop), b, 2 + hop, p.dn))

    def zrecv(self, b, pos, hop, final):
        p, c = self.p, PATTERN[pos]

        def take(k, t):
            land = self.lz(b, pos, k)
            self.copy(land, land, b, k, p.nx).wait_recv()
            if not final:
                self.add(self.gz(b, c, t), land)

        if not final:

            @pl.when(both(p.z >= 1, p.z - 1 + hop <= 3))
            def _():
                take(hop - 1, p.z - 1 + hop)

            @pl.when(both(p.z <= 2, p.z + 1 - hop >= 0))
            def _():
                take(2 + hop, p.z + 1 - hop)

            return
        own = self.G.at[b, p.z, p.y, p.x]
        below, above = self.lz(b, pos, 0), self.lz(b, pos, 3)
        f32 = jnp.float32

        @pl.when(p.z == 0)
        def _():
            take(3, p.z)
            self.out[b] = own[...].astype(f32) + above[...].astype(f32)

        @pl.when(p.z == 3)
        def _():
            take(0, p.z)
            self.out[b] = own[...].astype(f32) + below[...].astype(f32)

        @pl.when(both(p.z > 0, p.z < 3))
        def _():
            take(0, p.z)
            take(3, p.z)
            self.out[b] = own[...].astype(f32) + below[...].astype(f32) + above[...].astype(f32)

    def stage(self, b, pos, j):
        G = self.G
        x, y, z = self.p.x, self.p.y, self.p.z
        c, i = PATTERN[pos], self.slot(b, pos)
        if c == "X":
            first = (7, G.at[b, :, :, 1 - x], self.L8.at[i], G.at[b, :, :, x])
            return (first, (6, G.at[b, :, 1 - y, x], self.L4.at[i], G.at[b, :, y, x]), 3, 2, 1)[j]
        if c == "Y":
            first = (6, G.at[b, :, 1 - y], self.L8.at[i], G.at[b, :, y])
            return (first, (7, G.at[b, :, y, 1 - x], self.L4.at[i], G.at[b, :, y, x]), 3, 2, 1)[j]
        last = (7, G.at[b, z, y, 1 - x], self.P1.at[i], G.at[b, z, y, x])
        return (3, 2, 1, (6, G.at[b, z, 1 - y], self.P2.at[i], G.at[b, z, y]), last)[j]

    def send(self, b, pos, j, act=lambda d: d.start()):
        st = self.stage(b, pos, j)
        if isinstance(st, int):
            self.zsend(b, pos, st, act)
        else:
            act(self.copy(st[1], st[2], b, st[0], self.p.ny if st[0] == 6 else self.p.nx))

    def recv(self, b, pos, j):
        st = self.stage(b, pos, j)
        if isinstance(st, int):
            self.zrecv(b, pos, st, PATTERN[pos] != "Z" and j == 4)
        else:
            self.copy(st[2], st[2], b, st[0], self.p.nx).wait_recv()
            if j == 4:
                self.out[b] = st[3][...].astype(jnp.float32) + st[2][...].astype(jnp.float32)
            else:
                self.add(st[3], st[2])

    @staticmethod
    def landing(blocks, tail, dtype):
        n, m = blocks // PER * 3, blocks // PER
        return [
            pltpu.VMEM(shape + tail, dtype)
            for shape in ((n, 4, 2), (n, 4), (n, 6), (m, 6, 2, 2), (m, 2), (m,))
        ] + [pltpu.SemaphoreType.DMA((blocks, 8))] * 2
EPS = 1e-05
SEQ = 4
CAP = 256
ROWS = SEQ * CAP
HBM = pl.ANY


def dot(a, b):
    return jnp.dot(a, b, preferred_element_type=jnp.float32)


def dot_nt(a, b):
    return lax.dot_general(a, b, (((1,), (1,)), ((), ())), preferred_element_type=jnp.float32)


def halves(ref, rs):
    return jnp.concatenate([ref[0, rs, :], ref[1, rs, :]], 1).astype(jnp.float32)


def wblocks(W, first, count):
    return jnp.concatenate([W[first + i].reshape(1024, 128) for i in range(count)], 1)


def seq_rows(i):
    return pl.ds(i * CAP, CAP)


def cut(i, n):
    return pl.ds(pl.multiple_of(i * n, n), n)


def head_masks():
    lane = lax.broadcasted_iota(jnp.int32, (CAP, 128), 1)
    one = jnp.where(lane < HD, 1.0, 0.0)
    return [one.astype(jnp.bfloat16), (1.0 - one).astype(jnp.bfloat16)], lane < HD


def causal_mask():
    shape = (CAP, CAP)
    return lax.broadcasted_iota(jnp.int32, shape, 0) >= lax.broadcasted_iota(jnp.int32, shape, 1)


def softmax_rows(q, k, mask):
    s = jnp.where(mask, dot_nt(q, k) * (HD**-0.5), -1e30)
    e = jnp.exp(s - jnp.max(s, -1, keepdims=True))
    return e * (1.0 / jnp.sum(e, -1, keepdims=True))


def inv_rms(v):
    return lax.rsqrt(jnp.mean(v * v, -1, keepdims=True) + EPS)


def gate_of(rows_f, route):
    return jax.nn.sigmoid(jnp.sum(rows_f * route, -1, keepdims=True))


def own_slot(p, W, b):
    return W.at[b, p.z, p.y, p.x]


def forward_kernel(
    spot_ref,
    tile_ref,
    tok_ref,
    cot_ref,
    wq,
    wk,
    wv,
    wo,
    wu,
    wd,
    o_rows,
    o_cot,
    o_nT,
    o_qkv,
    o_mix,
    o_P,
    o_R,
    o_down,
    o_back,
    o_W,
    o_G,
    o_vec,
    W,
    VB,
    vecs,
    rows,
    cot,
    tokbuf,
    onehot,
    nrm,
    nT,
    dd,
    ddT,
    qkv,
    mixed,
    P,
    R,
    dacc,
    nacc,
    act,
    dup,
    Gst,
    ss,
    rs,
    vss,
    vrs,
    hs,
    hr,
    asnd,
    arcv,
    first,
    load,
    outs,
    gout,
):
    p = Place()
    t = p.t
    other = {"tensor": 1 - t}
    f32, bf = jnp.float32, jnp.bfloat16

    greet_all(p)

    own = [pltpu.make_async_copy(tile_ref, own_slot(p, VB, 0), first.at[NB])]
    for b in range(16):
        src, col = ((wq, wk, wv)[b % 3], b // 3) if b < 12 else (wo, b - 12)
        own.append(
            pltpu.make_async_copy(src.at[:, pl.ds(col * 128, 128)], own_slot(p, W, b), first.at[b])
        )
    for b in range(32):
        src = (wu, wd)[b % 4 // 2]
        own.append(
            pltpu.make_async_copy(
                src.at[:, pl.ds((b // 4 * 2 + b % 2) * 128, 128)],
                own_slot(p, W, 16 + b),
                first.at[16 + b],
            )
        )
    for c in own:
        c.start()

    def loader(i, a):
        return pltpu.make_async_copy((tok_ref, cot_ref)[a].at[i], tokbuf.at[a], load.at[a])

    loader(0, 0).start()
    loader(0, 1).start()
    await_all(p)
    for c in own:
        c.wait()
    W_steps = Gather(p, W, ss, rs)
    V_steps = Gather(p, VB, vss, vrs)

    def half_copy(i, a):
        ref = (rows, cot)[a].at[t, cut(i, CAP)]
        return pltpu.make_async_remote_copy(
            ref, ref, hs.at[i, a], hr.at[i, a], device_id=other, device_id_type=MESH
        )

    def half_wait(i, a):
        ref = (rows, cot)[a].at[1 - t, seq_rows(i)]
        pltpu.make_async_remote_copy(
            ref, ref, hs.at[i, a], hr.at[i, a], device_id=other, device_id_type=MESH
        ).wait_recv()

    def gather_part(i, _):
        def tick(q):
            W_steps.step(4 * i + q, q, low=True)
            for j, s in enumerate(VECTOR_STEPS):
                if s % 4 == q:

                    @pl.when(i == s // 4)
                    def _():
                        if j > 0:
                            V_steps.recv(0, 0, j - 1)
                        if j < 5:
                            V_steps.send(0, 0, j)

        for a in range(2):
            tick(2 * a)
            if a == 0:
                spot = jnp.broadcast_to(spot_ref[i], (128, CAP)).T[:, :1]
                hit = lax.broadcasted_iota(jnp.int32, (CAP, 2048), 1) == spot
                onehot[...] = jnp.where(hit, 1.0, 0.0).astype(bf)
            loader(i, a).wait()
            (rows, cot)[a][t, cut(i, CAP), :] = dot(onehot[...], tokbuf[a]).astype(bf)
            pl.when(i < 3)(lambda: loader(i + 1, a).start())
            tick(2 * a + 1)
            if a == 0:
                pl.when(i > 0)(lambda: half_copy(i - 1, 1).start())
            else:
                half_copy(i, 0).start()
        return 0

    lax.fori_loop(0, 4, gather_part, 0)
    half_copy(3, 1).start()

    for z in range(4):
        for y in range(2):
            vecs[:, pl.ds((z * 2 + y) * 128, 128)] = VB[0, z, y, 0] + pltpu.roll(
                VB[0, z, y, 1], 64, 1
            )

    def saver(k, src, dst):
        return pltpu.make_async_copy(src, dst, outs.at[k])

    saved = [saver(0, vecs, o_vec)]
    saved[0].start()

    dacc[...] = jnp.zeros_like(dacc)
    nacc[...] = jnp.zeros_like(nacc)

    for i in range(SEQ):
        W_steps.step(16 + i, i, static=16 + i)
        half_wait(i, 0)
        half_wait(i, 1)

        def norm_part(n, _):
            rs_ = cut(i * 8 + n, 32)
            r = halves(rows, rs_)
            nrm[rs_, :] = (r * inv_rms(r) * vecs[1:2, :]).astype(bf)
            dd[rs_, :] = (gate_of(r, vecs[0:1, :]) * halves(cot, rs_)).astype(bf)
            return 0

        lax.fori_loop(0, 8, norm_part, 0)
        for c in range(4):
            cs = pl.ds(c * 256, 256)
            nT[cs, seq_rows(i)] = nrm[seq_rows(i), cs].T
            ddT[cs, seq_rows(i)] = dd[seq_rows(i), cs].T
    later = [saver(1, rows, o_rows), saver(2, cot, o_cot), saver(3, nT, o_nT)]
    for c in later:
        c.start()
    saved += later[:2]
    nT_saved = later[2]

    masks, low_half = head_masks()
    mask = causal_mask()

    def attend(i, hp):
        r_ = seq_rows(i)
        q, k, v = qkv[3 * hp, r_, :], qkv[3 * hp + 1, r_, :], qkv[3 * hp + 2, r_, :]
        mix = [dot(softmax_rows(q * masks[h], k, mask).astype(bf), v) for h in (0, 1)]
        mixed[hp, r_, :] = jnp.where(low_half, mix[0], mix[1]).astype(bf)

    def pair_part(hp, _):
        W_steps.step(20 + 4 * hp, 0)
        W_steps.step(21 + 4 * hp, 1)
        y = dot(nrm[...], wblocks(W, 3 * hp, 3)).astype(bf)
        for c in range(3):
            qkv[3 * hp + c] = y[:, c * 128 : c * 128 + 128]
        for i in range(SEQ):
            attend(i, hp)
            if i in (0, 2):
                W_steps.step(22 + 4 * hp + i // 2, 2 + i // 2)
        return 0

    lax.fori_loop(0, 4, pair_part, 0)
    later = [saver(4, qkv, o_qkv), saver(5, mixed, o_mix)]
    for c in later:
        c.start()
    saved += later

    def att_copy(i):
        return pltpu.make_async_remote_copy(
            P.at[seq_rows(i)],
            R.at[seq_rows(i)],
            asnd.at[i],
            arcv.at[i],
            device_id=other,
            device_id_type=MESH,
        )

    def norm_mlp(i):
        att_copy(i).wait_recv()

        def norm_part(n, _):
            rs_ = cut(i * 8 + n, 32)
            h = halves(rows, rs_) + (P[rs_, :].astype(f32) + R[rs_, :].astype(f32))
            nrm[rs_, :] = (h * inv_rms(h) * vecs[2:3, :]).astype(bf)
            return 0

        lax.fori_loop(0, 8, norm_part, 0)
        for c in range(4):
            cs = pl.ds(c * 256, 256)
            nT[cs, seq_rows(i)] = nrm[seq_rows(i), cs].T

    out_w = wblocks(W, 12, 4)

    def project_out(i):
        mix = jnp.concatenate([mixed[h, seq_rows(i), :] for h in range(4)], 1)
        P[seq_rows(i), :] = dot_nt(mix, out_w).astype(bf)

    W_steps.step(36, 0)
    project_out(0)
    project_out(1)
    att_copy(0).start()
    W_steps.step(37, 1)
    project_out(2)
    att_copy(1).start()
    project_out(3)
    att_copy(2).start()
    nT_saved.wait()
    W_steps.step(38, 2)
    norm_mlp(0)
    att_copy(3).start()
    norm_mlp(1)
    W_steps.step(39, 3)
    norm_mlp(2)
    norm_mlp(3)
    saved.append(saver(6, W.at[pl.ds(0, 16)], o_W))
    saved[-1].start()
    later = [saver(7, P, o_P), saver(8, R, o_R)]
    for c in later:
        c.start()
    saved += later

    def g_copy(m):
        slot = lax.rem(m, 2)
        return pltpu.make_async_copy(Gst.at[slot], o_G.at[pl.ds(m * 4, 4)], gout.at[slot])

    partials = [
        saver(9 + n, tokbuf.at[n // 2, pl.ds(n % 2 * 1024, 1024)], (o_down, o_back)[n // 2].at[n % 2])
        for n in range(4)
    ]

    def mlp_part(m, _):
        slot = lax.rem(m, 2)
        s = 40 + 4 * m
        up_w = wblocks(W, 16 + 4 * m, 2)
        down_w = wblocks(W, 18 + 4 * m, 2)
        for ht in range(2):
            hs_ = pl.ds(ht * 512, 512)
            W_steps.step(s + ht, ht, high=True)
            u = dot(nrm[hs_, :], up_w)
            d = dot(dd[hs_, :], down_w)
            c0 = 0.7978845608028654
            u2 = u * u
            s1 = 1.0 + jnp.tanh(u * (c0 + (c0 * 0.044715) * u2))
            h = 0.5 * u
            act[hs_, :] = (h * s1).astype(bf)
            slope = s1 * (0.5 + h * (2.0 - s1) * (c0 + (3 * 0.044715 * c0) * u2))
            dup[hs_, :] = (d * slope).astype(bf)
        W_steps.step(s + 2, 2, high=True)
        for ht in range(2):
            hs_ = pl.ds(ht * 512, 512)
            dacc[hs_, :] += dot_nt(act[hs_, :], down_w)
            nacc[hs_, :] += dot_nt(dup[hs_, :], up_w)
        W_steps.step(s + 3, 3, high=True)
        W_steps.drain(m, m + 1)

        @pl.when(m == 7)
        def _():
            for n, c in enumerate(partials):
                piece = (dacc, nacc)[n // 2][:, n % 2 * 512 : n % 2 * 512 + 512]
                tokbuf[n // 2, pl.ds(n % 2 * 1024, 1024), :] = piece.astype(bf)
                c.start()

        @pl.when(m >= 2)
        def _():
            g_copy(m - 2).wait()

        for ht in range(2):
            hs_ = pl.ds(ht * 512, 512)
            gu = dot(nT[hs_, :], dup[...]).astype(bf)
            Gst[slot, 0, hs_, :] = gu[:, :128]
            Gst[slot, 1, hs_, :] = gu[:, 128:]
            gd = dot(ddT[hs_, :], act[...]).astype(bf)
            Gst[slot, 2, hs_, :] = gd[:, :128]
            Gst[slot, 3, hs_, :] = gd[:, 128:]
        g_copy(m).start()
        return 0

    lax.fori_loop(0, 8, mlp_part, 0)
    saved += partials
    for i in range(SEQ):
        half_copy(i, 0).wait_send()
        half_copy(i, 1).wait_send()
    for i in range(SEQ):
        att_copy(i).wait_send()
    W_steps.drain(8, NB // PER)
    for j in range(5):
        V_steps.send(0, 0, j, act=lambda d: d.wait_send())
    g_copy(6).wait()
    g_copy(7).wait()
    for c in saved:
        c.wait()


def forward_call(chosen, tile, tok, cotangent, weights):
    bf, f32 = jnp.bfloat16, jnp.float32
    S = jax.ShapeDtypeStruct
    DMA = pltpu.SemaphoreType.DMA
    any_ = pl.BlockSpec(memory_space=HBM)
    vm = pltpu.VMEM
    return pl.pallas_call(
        forward_kernel,
        out_shape=(
            S((2, ROWS, 512), bf),
            S((2, ROWS, 512), bf),
            S((1024, ROWS), bf),
            S((12, ROWS, 128), bf),
            S((4, ROWS, 128), bf),
            S((ROWS, 1024), bf),
            S((ROWS, 1024), bf),
            S((2, ROWS, 512), bf),
            S((2, ROWS, 512), bf),
            S((16, 4, 2, 2, 64, 128), bf),
            S((32, 1024, 128), bf),
            S((8, 1024), f32),
        ),
        in_specs=[pl.BlockSpec(memory_space=pltpu.VMEM)] + [any_] * 9,
        out_specs=[any_] * 12,
        scratch_shapes=[
            vm((NB, 4, 2, 2, 64, 128), bf),
            vm((1, 4, 2, 2, 8, 128), f32),
            vm((8, 1024), f32),
            vm((2, ROWS, 512), bf),
            vm((2, ROWS, 512), bf),
            vm((2, 2048, 512), bf),
            vm((CAP, 2048), bf),
            vm((ROWS, 1024), bf),
            vm((1024, ROWS), bf),
            vm((ROWS, 1024), bf),
            vm((1024, ROWS), bf),
            vm((12, ROWS, 128), bf),
            vm((4, ROWS, 128), bf),
            vm((ROWS, 1024), bf),
            vm((ROWS, 1024), bf),
            vm((ROWS, 1024), f32),
            vm((ROWS, 1024), f32),
            vm((ROWS, 256), bf),
            vm((ROWS, 256), bf),
            vm((2, 4, 1024, 128), bf),
            DMA((NB, 8)),
            DMA((NB, 8)),
            DMA((1, 8)),
            DMA((1, 8)),
            DMA((4, 2)),
            DMA((4, 2)),
            DMA((4,)),
            DMA((4,)),
            DMA((NB + 1,)),
            DMA((2,)),
            DMA((13,)),
            DMA((2,)),
        ],
        compiler_params=pltpu.CompilerParams(
            collective_id=1, has_side_effects=True, vmem_limit_bytes=63 * 1024 * 1024
        ),
        name="forward",
    )(chosen, tile, tok, cotangent, *weights)


def backward_kernel(
    rows,
    cot,
    nT_in,
    qkv_in,
    mix_in,
    P_in,
    R_in,
    down_in,
    back_in,
    W_in,
    G_in,
    vec_in,
    o_newr,
    o_newg,
    sum_out,
    o_vec,
    o_sum,
    G,
    Wa,
    qkv,
    mixed,
    nT,
    vecs,
    DR,
    NR,
    R1,
    bufs,
    buf2,
    da,
    daT,
    dmix,
    newr,
    newg,
    dhid,
    dlog,
    accs,
    GV,
    base,
    gsem,
    lsem,
    psem,
    prcv,
    qsem,
    qrcv,
    tout,
    *landing,
):
    p = Place()
    t = p.t
    other = {"tensor": 1 - t}
    f32, bf = jnp.float32, jnp.bfloat16
    wide, small = landing[:8], landing[8:]
    greet_all(p)

    def g_load(c):
        return pltpu.make_async_copy(G_in.at[pl.ds(4 * c, 4)], G.at[pl.ds(4 * c, 4)], gsem.at[c])

    g_load(0).start()
    g_load(1).start()

    def stream(s, names):
        q = lax.rem(s, 2)
        out = []
        for k in names:
            if k < 2:
                src = (P_in, R_in)[k].at[cut(s, CAP)]
                dst = buf2.at[q, k]
            else:
                src = (rows, cot, down_in, back_in)[k - 2].at[:, cut(s, CAP)]
                dst = bufs.at[q, k - 2]
            out.append(pltpu.make_async_copy(src, dst, lsem.at[q, k]))
        return out

    everything = (0, 1, 2, 3, 4, 5)
    for c in stream(0, everything):
        c.start()
    fixed = [
        pltpu.make_async_copy(a, b, base.at[i])
        for i, (a, b) in enumerate(
            ((vec_in, vecs), (W_in, Wa), (qkv_in, qkv), (mix_in, mixed), (nT_in, nT))
        )
    ]
    for c in fixed[:3]:
        c.start()
    await_all(p)

    def pair_copy(s, e):
        return pltpu.make_async_remote_copy(
            (down_in, back_in)[e].at[:, cut(s, CAP)],
            (DR, NR)[e].at[:, cut(s, CAP)],
            psem.at[s, e],
            prcv.at[s, e],
            device_id=other,
            device_id_type=MESH,
        )

    pair_copy(0, 0).start()
    pair_copy(0, 1).start()
    steps = Scatter(p, G, o_sum, *wide)
    v_steps = Scatter(p, GV, o_vec, *small)

    accs[...] = jnp.zeros_like(accs)

    def fold(v):
        return jnp.sum(v.reshape(4, 8, 1024), 0)

    def pick(v):
        return jnp.where(t == 0, v[:, :512], v[:, 512:])

    masks, low_half = head_masks()
    seen = lax.broadcasted_iota(jnp.int32, (CAP, CAP), 0) <= lax.broadcasted_iota(
        jnp.int32, (CAP, CAP), 1
    )

    def seq_part(s, _):
        def tick(q):
            if q % 4 == 0:
                g_load(2 * s + q // 4).wait()

                @pl.when(s < 3)
                def _():
                    g_load(2 * s + q // 4 + 2).start()

            steps.step(8 * s + q, q % 4, low=True)

        tick(0)
        q = lax.rem(s, 2)

        @pl.when(s + 1 < SEQ)
        def _():
            for c in stream(s + 1, everything):
                c.start()
            pair_copy(s + 1, 0).start()
            pair_copy(s + 1, 1).start()

        pl.when(s == 0)(lambda: fixed[0].wait())
        for c in stream(s, everything):
            c.wait()
        for e in range(2):
            pair_copy(s, e).wait_recv()

        def part(n, _):
            rs_ = cut(n, 32)
            as_ = pl.ds(pl.multiple_of(s * CAP + n * 32, 32), 32)

            def mine(k):
                return jnp.concatenate([bufs[q, k, 0, rs_, :], bufs[q, k, 1, rs_, :]], 1).astype(f32)

            r, c = mine(0), mine(1)
            att = buf2[q, 0, rs_, :].astype(f32) + buf2[q, 1, rs_, :].astype(f32)
            h = r + att
            branch = att + (mine(2) + halves(DR, as_))
            dn = mine(3) + halves(NR, as_)
            inv = inv_rms(h)
            sc = dn * vecs[2:3, :]
            dh = inv * sc - h * (inv * inv * inv * jnp.mean(sc * h, -1, keepdims=True))
            gate = gate_of(r, vecs[0:1, :])
            dl = jnp.sum(c * branch, -1, keepdims=True) * (gate * (1.0 - gate))
            da[rs_, :] = (gate * c + dh).astype(bf)
            accs[2] += fold(dn * (h * inv))
            accs[0] += fold(r * dl)
            newr[as_, :] = pick(r + gate * branch).astype(bf)
            dhid[as_, :] = pick(dh)
            dlog[as_, :] = jnp.broadcast_to(dl, (32, 128))
            return 0

        lax.fori_loop(0, 4, part, 0)
        tick(1)
        lax.fori_loop(4, 8, part, 0)
        tick(2)
        for c in range(4):
            cs = pl.ds(c * 256, 256)
            daT[cs, cut(s, CAP)] = da[:, cs].T

        @pl.when(s == 0)
        def _():
            for c in fixed[1:3]:
                c.wait()
            for c in fixed[3:]:
                c.start()

        tick(3)
        dm = dot(da[...], wblocks(Wa, 12, 4)).astype(bf)
        for h in range(4):
            dmix[h] = dm[:, h * 128 : h * 128 + 128]

        def pair_back(hp):
            r_ = cut(s, CAP)
            qh, kh, vh = [qkv[3 * hp + c, r_, :] for c in range(3)]
            dmh = dmix[hp]
            outs = []
            for h in (0, 1):
                sc = jnp.where(seen, dot_nt(kh, qh * masks[h]) * (HD**-0.5), -1e30)
                e = jnp.exp(sc - jnp.max(sc, 0, keepdims=True))
                pr = e * (1.0 / jnp.sum(e, 0, keepdims=True))
                dv = dot(pr.astype(bf), dmh)
                dp = dot_nt(vh * masks[h], dmh)
                ds = (pr * (dp - jnp.sum(dp * pr, 0, keepdims=True))).astype(bf)
                outs.append((dot(ds.T, kh), dot(ds, qh), dv))
            scale = HD**-0.5
            for i, (a, b) in enumerate(zip(*outs)):
                v = jnp.where(low_half, a, b)
                qkv[3 * hp + i, r_, :] = (v if i == 2 else v * scale).astype(bf)

        for hp in range(4):
            tick(4 + hp)
            pair_back(hp)
        return 0

    lax.fori_loop(0, SEQ, seq_part, 0)
    row_outs = [pltpu.make_async_copy(newr, o_newr, tout.at[0])]
    row_outs[0].start()

    def grad_unit(leftT, a, b, first):
        y = jnp.concatenate([a, b], 1)
        for ht in range(2):
            g = dot(leftT[pl.ds(ht * 512, 512), :], y).astype(bf)
            for c in range(2):
                G[first + c, pl.ds(ht * 2, 2)] = g[:, c * 128 : c * 128 + 128].reshape(
                    2, 2, 2, 64, 128
                )

    def back_copy(s):
        return pltpu.make_async_remote_copy(
            DR.at[:, seq_rows(s)],
            R1.at[:, seq_rows(s)],
            qsem.at[s],
            qrcv.at[s],
            device_id=other,
            device_id_type=MESH,
        )

    for s in range(2):
        for c in stream(s, (2, 3)):
            c.start()
    for c in fixed[3:]:
        c.wait()
    grad_unit(daT, mixed[0], mixed[1], 32)
    grad_unit(daT, mixed[2], mixed[3], 34)

    def grad_part(n, _):
        for e in range(2):
            steps.step(32 + 4 * n + 2 * e, 2 * e)
            steps.step(33 + 4 * n + 2 * e, 2 * e + 1)
            j = 2 * n + e
            grad_unit(nT, qkv[2 * j], qkv[2 * j + 1], 36 + 2 * j)
        return 0

    lax.fori_loop(0, 3, grad_part, 0)
    for s in range(SEQ):
        steps.step(44 + s, s)
        y = 0.0
        for g in range(3):
            x = jnp.concatenate([qkv[4 * g + i, seq_rows(s), :] for i in range(4)], 1)
            y = y + dot_nt(x, wblocks(Wa, 4 * g, 4))
        y = y.astype(bf)
        DR[0, seq_rows(s), :] = y[:, :512]
        DR[1, seq_rows(s), :] = y[:, 512:]
        if s > 0:
            back_copy(s - 1).start()
    steps.step(48, 0, high=True)
    back_copy(3).start()

    route_half = jnp.where(t == 0, vecs[0:1, :512], vecs[0:1, 512:])
    for s in range(SEQ):
        steps.step(49 + s, (1 + s) % 4, high=True)
        steps.drain(2 * s, 2 * s + 2)
        q = s % 2
        for c in stream(s, (2, 3)):
            c.wait()
        back_copy(s).wait_recv()

        def part(n, _):
            rs_ = cut(n, 32)
            as_ = pl.ds(pl.multiple_of(s * CAP + n * 32, 32), 32)
            r = jnp.concatenate([bufs[q, 0, 0, rs_, :], bufs[q, 0, 1, rs_, :]], 1).astype(f32)
            dn = halves(DR, as_) + halves(R1, as_)
            inv = inv_rms(r)
            sc = dn * vecs[1:2, :]
            dr = inv * sc - r * (inv * inv * inv * jnp.mean(sc * r, -1, keepdims=True))
            accs[1] += fold(dn * (r * inv))
            dl = dlog[as_, :]
            dl = jnp.concatenate([dl, dl, dl, dl], 1)
            ch = bufs[q, 1, t, rs_, :].astype(f32)
            newg[as_, :] = (ch + (dhid[as_, :] + pick(dr) + dl * route_half)).astype(bf)
            return 0

        lax.fori_loop(0, 8, part, 0)
        if s + 2 < SEQ:
            for c in stream(s + 2, (2, 3)):
                c.start()

    for z in range(4):
        for y in range(2):
            cs = pl.ds((z * 2 + y) * 128, 128)
            tile = jnp.concatenate(
                [jnp.sum(accs[k, :, cs], 0, keepdims=True) for k in range(3)]
                + [jnp.zeros((5, 128), f32)],
                0,
            )
            GV[0, z, y, 0] = tile
            GV[0, z, y, 1] = pltpu.roll(tile, 64, 1)
    for s in range(SEQ):
        back_copy(s).wait_send()
    row_outs.append(pltpu.make_async_copy(newg, o_newg, tout.at[1]))
    row_outs[1].start()
    v_steps.send(0, 0, 0)

    def sum_copy(e):
        part = pl.ds(32, 16) if e else pl.ds(0, 32)
        return pltpu.make_async_copy(o_sum.at[part], sum_out.at[part], tout.at[2 + e])

    for k, s in enumerate(range(53, 67)):
        steps.step(s, s % PER, static=s)
        if s == 53:
            sum_copy(0).start()
        if k in (0, 2, 3, 5, 7):
            j = (0, 2, 3, 5, 7).index(k) + 1
            v_steps.recv(0, 0, j - 1)
            if j < 5:
                v_steps.send(0, 0, j)
    sum_copy(1).start()
    for c in row_outs:
        c.wait()
    for s in range(SEQ):
        for e in range(2):
            pair_copy(s, e).wait_send()
    for j in range(5):
        v_steps.send(0, 0, j, act=lambda d: d.wait_send())
    steps.drain(8, NB // PER)
    sum_copy(0).wait()
    sum_copy(1).wait()


def backward_call(kept):
    bf, f32 = jnp.bfloat16, jnp.float32
    S = jax.ShapeDtypeStruct
    DMA = pltpu.SemaphoreType.DMA
    any_ = pl.BlockSpec(memory_space=HBM)
    vspec = pl.BlockSpec(memory_space=pltpu.VMEM)
    vm = pltpu.VMEM
    return pl.pallas_call(
        backward_kernel,
        out_shape=(
            S((ROWS, 512), bf),
            S((ROWS, 512), bf),
            S((NB, 64, 128), f32),
            S((1, 8, 128), f32),
        ),
        in_specs=[any_] * 12,
        out_specs=[any_, any_, any_, vspec],
        scratch_shapes=[
            vm((NB, 64, 128), f32),
            vm((NB, 4, 2, 2, 64, 128), bf),
            vm((16, 4, 2, 2, 64, 128), bf),
            vm((12, ROWS, 128), bf),
            vm((4, ROWS, 128), bf),
            vm((1024, ROWS), bf),
            vm((8, 1024), f32),
            vm((2, ROWS, 512), bf),
            vm((2, ROWS, 512), bf),
            vm((2, ROWS, 512), bf),
            vm((2, 4, 2, CAP, 512), bf),
            vm((2, 2, CAP, 1024), bf),
            vm((CAP, 1024), bf),
            vm((1024, ROWS), bf),
            vm((4, CAP, 128), bf),
            vm((ROWS, 512), bf),
            vm((ROWS, 512), bf),
            vm((ROWS, 512), f32),
            vm((ROWS, 128), f32),
            vm((3, 8, 1024), f32),
            vm((1, 4, 2, 2, 8, 128), f32),
            DMA((5,)),
            DMA((8,)),
            DMA((2, 6)),
            DMA((4, 2)),
            DMA((4, 2)),
            DMA((4,)),
            DMA((4,)),
            DMA((4,)),
        ]
        + Scatter.landing(NB, (64, 128), bf)
        + Scatter.landing(PER, (8, 128), f32),
        compiler_params=pltpu.CompilerParams(
            collective_id=2, has_side_effects=True, vmem_limit_bytes=63 * 1024 * 1024
        ),
        name="backward",
    )(*kept)


def place_kernel(
    spot_ref,
    own_ref,
    newr,
    newg,
    tok,
    cot,
    o_tok,
    o_cot,
    g_q,
    g_k,
    g_v,
    g_out,
    g_up,
    g_down,
    old,
    out,
    new,
    came,
    went,
    own,
    nsem,
    gsem,
):
    bf = jnp.bfloat16

    def piece(n):
        return n // (2048 // SIZE), cut(n % (2048 // SIZE), SIZE)

    def load(n, a):
        i, rs = piece(n)
        return pltpu.make_async_copy((tok, cot)[a].at[i, rs], old.at[a, n], came.at[a, n])

    def store(n, a):
        i, rs = piece(n)
        return pltpu.make_async_copy(out.at[a, n], (o_tok, o_cot)[a].at[i, rs], went.at[a, n])

    pieces = SEQ * 2048 // SIZE
    news = [pltpu.make_async_copy((newr, newg)[a], new.at[a], nsem.at[a]) for a in range(2)]
    sums = pltpu.make_async_copy(own_ref, own, nsem.at[2])
    for c in news + [sums]:
        c.start()

    def start(n, _):
        load(n, 0).start()
        load(n, 1).start()
        return 0

    lax.fori_loop(0, pieces, start, 0)

    moves = []
    for b in range(NB):
        if b < 32:
            ref, k = (g_up, g_down)[b % 4 // 2], b // 4 * 2 + b % 2
        else:
            ref, k = (g_out, b - 32) if b < 36 else ((g_q, g_k, g_v)[b % 3], (b - 36) // 3)
        moves.append(
            pltpu.make_async_copy(own.at[b], ref.at[:, pl.ds(k * 128, 128)], gsem.at[b])
        )
    for c in news:
        c.wait()
    ones = jnp.ones((CAP, 128), bf)

    def place(n, _):
        i, _rs = piece(n)

        @pl.when(n == 2)
        def _():
            sums.wait()
            for c in moves:
                c.start()

        row = lax.broadcasted_iota(jnp.int32, (SIZE, CAP), 0) + n % (2048 // SIZE) * SIZE
        hit = jnp.where(row == spot_ref[i], 1.0, 0.0).astype(bf)
        kept = 1.0 - dot(hit, ones)
        kept = jnp.concatenate([kept, kept, kept, kept], 1).astype(bf)
        for a in range(2):
            moved = dot(hit, new[a, cut(i, CAP), :]).astype(bf)
            load(n, a).wait()
            out[a, n] = old[a, n] * kept + moved
            store(n, a).start()
        return 0

    lax.fori_loop(0, pieces, place, 0)

    def finish(n, _):
        store(n, 0).wait()
        store(n, 1).wait()
        return 0

    lax.fori_loop(0, pieces, finish, 0)
    for c in moves:
        c.wait()


SIZE = 2048


def place_call(spot, own, newr, newg, tok, cotangent):
    bf, f32 = jnp.bfloat16, jnp.float32
    S = jax.ShapeDtypeStruct
    DMA = pltpu.SemaphoreType.DMA
    any_ = pl.BlockSpec(memory_space=pltpu.MemorySpace.HBM)
    pieces = SEQ * 2048 // SIZE
    return pl.pallas_call(
        place_kernel,
        out_shape=(
            S((SEQ, 2048, 512), bf),
            S((SEQ, 2048, 512), bf),
            S((64, 512), f32),
            S((64, 512), f32),
            S((64, 512), f32),
            S((64, 512), f32),
            S((64, 2048), f32),
            S((64, 2048), f32),
        ),
        in_specs=[pl.BlockSpec(memory_space=pltpu.VMEM)] + [any_] * 5,
        out_specs=[any_] * 8,
        scratch_shapes=[
            pltpu.VMEM((2, pieces, SIZE, 512), bf),
            pltpu.VMEM((2, pieces, SIZE, 512), bf),
            pltpu.VMEM((2, ROWS, 512), bf),
            DMA((2, pieces)),
            DMA((2, pieces)),
            pltpu.VMEM((NB, 64, 128), f32),
            DMA((3,)),
            DMA((NB,)),
        ],
        compiler_params=pltpu.CompilerParams(vmem_limit_bytes=63 * 1024 * 1024),
        name="place_rows",
    )(spot, own, newr, newg, tok, cotangent)


def to_tile(w_route, gain_attn, gain_mlp):
    v = jnp.stack([w_route, gain_attn, gain_mlp]).astype(jnp.float32)
    return jnp.pad(v, ((0, 5), (0, 64)))


def fused(
    tokens,
    routed,
    w_query,
    w_key,
    w_value,
    w_out,
    w_up,
    w_down,
    w_route,
    gain_attn,
    gain_mlp,
    cotangent,
):
    tok = tokens.reshape(SEQ, 2048, 512)
    cot = cotangent.reshape(SEQ, 2048, 512)
    spot = routed.reshape(SEQ, 1, CAP)
    tile = to_tile(w_route, gain_attn, gain_mlp)
    weights = (w_query, w_key, w_value, w_out.T, w_up, w_down.T)
    kept = list(forward_call(spot, tile, tok, cot, weights))
    kept[10] = kept[10].reshape(32, 4, 2, 2, 64, 128)
    newr, newg, own, vec = backward_call(kept)
    vec = vec[0, :3, :64]
    output, grad, g_q, g_k, g_v, g_out, g_up, g_down = place_call(
        spot, own, newr, newg, tok, cot
    )
    return (
        output.reshape(tokens.shape),
        grad.reshape(tokens.shape),
        g_q,
        g_k,
        g_v,
        g_out.T,
        g_up,
        g_down.T,
        vec[0],
        vec[1],
        vec[2],
    )


def shards(tokens, routed, *rest):
    sizes = (lax.axis_size("dp"), lax.axis_size("tensor"))
    here = tokens.shape == (4, 1, 2048, 512) and routed.shape == (4, 1, 256)
    if sizes == (16, 2) and here:
        return fused(tokens, routed, *rest)
    return plain(tokens, routed, *rest)


def solution(mesh):
    rows = P("dp", "tensor")
    columns = P("tensor", "dp")
    vector = P("dp")
    stored = P(None, "dp", None, "tensor")
    return jax.shard_map(
        shards,
        mesh=mesh,
        in_specs=(
            stored,
            P(None, "dp", None),
            rows,
            rows,
            rows,
            columns,
            rows,
            columns,
            vector,
            vector,
            vector,
            stored,
        ),
        out_specs=(
            stored,
            stored,
            rows,
            rows,
            rows,
            columns,
            rows,
            columns,
            vector,
            vector,
            vector,
        ),
        check_vma=False,
    )
```

```python
import jax
import jax.numpy as jnp
from jax import lax
from jax.experimental import pallas as pl
from jax.experimental.pallas import tpu as pltpu
from jax.sharding import PartitionSpec as P

HD = 64
eps_norm = 1e-05


def dense(left, right):
    return jnp.dot(left, right, preferred_element_type=jnp.float32)


def dense_t(left, right):
    return lax.dot_general(
        left, right, (((1,), (1,)), ((), ())), preferred_element_type=jnp.float32
    )


def dense_g(left, right):
    return lax.dot_general(
        left, right, (((0,), (0,)), ((), ())), preferred_element_type=jnp.float32
    )


def rms_back(values, inv, gain, grad):
    grad_gain = jnp.sum(grad * values * inv, 0)
    scaled = grad * gain
    dot = jnp.mean(scaled * values, -1, keepdims=True)
    return inv * scaled - values * (inv * inv * inv) * dot, grad_gain


def plain(
    tokens,
    routed,
    w_query,
    w_key,
    w_value,
    w_out,
    w_up,
    w_down,
    w_route,
    gain_attn,
    gain_mlp,
    cotangent,
):
    micro, seqs, length, half_width = tokens.shape
    capacity = routed.shape[2]
    batch = micro * seqs
    total = batch * capacity
    cols = w_query.shape[1]
    hidden_cols = w_up.shape[1]
    width = half_width * lax.axis_size("tensor")
    offset = lax.axis_index("tensor") * half_width
    scale = HD ** (-0.5)
    swap = [(0, 1), (1, 0)]

    vec = jnp.stack([w_route, gain_attn, gain_mlp], 1)
    vec = jnp.pad(vec, ((0, 0), (0, 125)))
    packed = jnp.concatenate([w_query, w_key, w_value, w_up, w_out.T, w_down.T, vec], 1)
    gathered = lax.all_gather(packed, "dp", axis=0, tiled=True)
    b1, b2, b3 = cols, 2 * cols, 3 * cols
    b4 = b3 + hidden_cols
    b5 = b4 + w_out.shape[0]
    b6 = b5 + w_down.shape[0]
    fq = gathered[:, :b1]
    fk = gathered[:, b1:b2]
    fv = gathered[:, b2:b3]
    fup = gathered[:, b3:b4]
    foutT = gathered[:, b4:b5]
    fdownT = gathered[:, b5:b6]
    route = gathered[:, b6]
    route_f32 = route.astype(jnp.float32)
    gain1 = gathered[:, b6 + 1].astype(jnp.float32)
    gain2 = gathered[:, b6 + 2].astype(jnp.float32)

    tok = tokens.reshape(batch, length, half_width)
    cot = cotangent.reshape(batch, length, half_width)
    chosen = routed.reshape(batch, capacity)
    rows_half = jnp.take_along_axis(tok, chosen[:, :, None], axis=1).reshape(total, half_width)
    cot_half = jnp.take_along_axis(cot, chosen[:, :, None], axis=1).reshape(total, half_width)
    rows = lax.all_gather(rows_half, "tensor", axis=1, tiled=True)
    cot_rows = lax.all_gather(cot_half, "tensor", axis=1, tiled=True)

    rows_f = rows.astype(jnp.float32)
    cot_f = cot_rows.astype(jnp.float32)
    gate = jax.nn.sigmoid(dense(rows, route))
    inv1 = lax.rsqrt(jnp.mean(rows_f * rows_f, -1, keepdims=True) + eps_norm)
    normed = (rows_f * inv1 * gain1).astype(jnp.bfloat16)
    heads = cols // HD

    def split(x):
        return x.astype(jnp.bfloat16).reshape(batch, capacity, heads, HD).transpose(0, 2, 1, 3)

    def join(x):
        return x.transpose(0, 2, 1, 3).reshape(total, cols)

    q = split(dense(normed, fq))
    k = split(dense(normed, fk))
    v = split(dense(normed, fv))
    causal = lax.broadcasted_iota(jnp.int32, (capacity, capacity), 0) >= lax.broadcasted_iota(
        jnp.int32, (capacity, capacity), 1
    )
    scores = jnp.einsum("bhqd,bhkd->bhqk", q, k, preferred_element_type=jnp.float32) * scale
    scores = jnp.where(causal, scores, -1e30)
    peak = jnp.max(scores, -1, keepdims=True)
    expd = jnp.exp(scores - peak)
    probs = expd / jnp.sum(expd, -1, keepdims=True)
    probs_low = probs.astype(jnp.bfloat16)
    mixed = jnp.einsum("bhqk,bhkd->bhqd", probs_low, v, preferred_element_type=jnp.float32)
    mixed = join(mixed.astype(jnp.bfloat16))

    def pair_sum(x):
        low = x.astype(jnp.bfloat16)
        other = lax.ppermute(low, "tensor", swap)
        return low.astype(jnp.float32) + other.astype(jnp.float32)

    attended = pair_sum(dense_t(mixed, foutT))
    hidden = rows_f + attended
    inv2 = lax.rsqrt(jnp.mean(hidden * hidden, -1, keepdims=True) + eps_norm)
    normed2 = (hidden * inv2 * gain2).astype(jnp.bfloat16)
    up = dense(normed2, fup)
    act32, gelu_back = jax.vjp(jax.nn.gelu, up)
    act = act32.astype(jnp.bfloat16)
    down = pair_sum(dense_t(act, fdownT))
    branch = attended + down
    d_logit = jnp.sum(cot_f * branch, -1) * gate * (1.0 - gate)
    branch_half = lax.dynamic_slice_in_dim(branch, offset, half_width, 1)
    new_rows = (rows_half.astype(jnp.float32) + gate[:, None] * branch_half).astype(jnp.bfloat16)

    d_branch = gate[:, None] * cot_f
    d_down = d_branch.astype(jnp.bfloat16)
    g_downT = dense_g(d_down, act)
    d_act = dense(d_down, fdownT)
    d_upper = gelu_back(d_act)[0].astype(jnp.bfloat16)
    g_up = dense_g(normed2, d_upper)
    d_normed2 = pair_sum(dense_t(d_upper, fup))
    d_hidden, g_gain2 = rms_back(hidden, inv2, gain2, d_normed2)
    d_attended = (d_branch + d_hidden).astype(jnp.bfloat16)
    g_outT = dense_g(d_attended, mixed)
    d_mixed = split(dense(d_attended, foutT))
    d_values = jnp.einsum("bhqk,bhqd->bhkd", probs_low, d_mixed, preferred_element_type=jnp.float32)
    d_values = join(d_values.astype(jnp.bfloat16))
    d_probs = jnp.einsum("bhqd,bhkd->bhqk", d_mixed, v, preferred_element_type=jnp.float32)
    d_scores = probs * (d_probs - jnp.sum(d_probs * probs, -1, keepdims=True))
    d_scores = d_scores.astype(jnp.bfloat16)
    d_q = jnp.einsum("bhqk,bhkd->bhqd", d_scores, k, preferred_element_type=jnp.float32) * scale
    d_k = jnp.einsum("bhqk,bhqd->bhkd", d_scores, q, preferred_element_type=jnp.float32) * scale
    d_q = join(d_q.astype(jnp.bfloat16))
    d_k = join(d_k.astype(jnp.bfloat16))
    g_q = dense_g(normed, d_q)
    g_k = dense_g(normed, d_k)
    g_v = dense_g(normed, d_values)
    d_normed = pair_sum(dense_t(d_q, fq) + dense_t(d_k, fk) + dense_t(d_values, fv))
    d_rows, g_gain1 = rms_back(rows_f, inv1, gain1, d_normed)
    g_route = jnp.sum(rows_f * d_logit[:, None], 0)
    d_half = (
        lax.dynamic_slice_in_dim(d_hidden + d_rows, offset, half_width, 1)
        + d_logit[:, None] * lax.dynamic_slice_in_dim(route_f32, offset, half_width, 0)[None, :]
    )
    grad_rows = (cot_half.astype(jnp.float32) + d_half).astype(jnp.bfloat16)

    seq_ids = lax.broadcasted_iota(jnp.int32, (batch, capacity), 0)
    output = tok.at[seq_ids, chosen].set(
        new_rows.reshape(batch, capacity, half_width), unique_indices=True
    )
    input_grad = cot.at[seq_ids, chosen].set(
        grad_rows.reshape(batch, capacity, half_width), unique_indices=True
    )

    g_vec = jnp.pad(jnp.stack([g_route, g_gain1, g_gain2], 1), ((0, 0), (0, 125)))
    grads = jnp.concatenate(
        [x.astype(jnp.bfloat16) for x in (g_q, g_k, g_v, g_up, g_outT, g_downT, g_vec)], 1
    )
    own = lax.psum_scatter(grads, "dp", scatter_dimension=0, tiled=True).astype(jnp.float32)
    return (
        output.reshape(tokens.shape),
        input_grad.reshape(tokens.shape),
        own[:, :b1],
        own[:, b1:b2],
        own[:, b2:b3],
        own[:, b4:b5].T,
        own[:, b3:b4],
        own[:, b5:b6].T,
        own[:, b6],
        own[:, b6 + 1],
        own[:, b6 + 2],
    )


MESH = pl.DeviceIdType.MESH
NB = 48
PATTERN = "XYZX"
PER = 4
GATHER_LAGS = {
    "X": (0, 3, 6, 9, 12, 19),
    "Y": (0, 4, 7, 9, 13, 19),
    "Z": (0, 5, 9, 12, 15, 19),
}
SCATTER_LAGS = {
    "X": (0, 4, 7, 9, 13, 18),
    "Y": (0, 4, 8, 10, 12, 17),
    "Z": (0, 2, 5, 9, 14, 19),
}
VECTOR_STEPS = (0, 3, 6, 9, 12, 15)


class Place:
    def __init__(self):
        me = lax.axis_index("dp")
        self.x = me % 2
        self.y = (me // 2) % 2
        self.z = me // 4
        self.nx = me + 1 - 2 * self.x
        self.ny = me + 2 - 4 * self.y
        self.up = jnp.minimum(me + 4, 15)
        self.dn = jnp.maximum(me - 4, 0)
        self.t = lax.axis_index("tensor")


def both(a, b):
    return jnp.logical_and(a, b)


def greet_all(p):
    bar = pltpu.get_barrier_semaphore()

    def greet(dev):
        pl.semaphore_signal(bar, inc=1, device_id=dev, device_id_type=MESH)

    greet({"dp": p.nx})
    greet({"dp": p.ny})
    greet({"tensor": 1 - p.t})

    @pl.when(p.z < 3)
    def _():
        greet({"dp": p.up})

    @pl.when(p.z > 0)
    def _():
        greet({"dp": p.dn})


def await_all(p):
    bar = pltpu.get_barrier_semaphore()
    inner = both(p.z > 0, p.z < 3)

    @pl.when(inner)
    def _():
        pl.semaphore_wait(bar, 5)

    @pl.when(jnp.logical_not(inner))
    def _():
        pl.semaphore_wait(bar, 4)


class Steps:
    def step(self, s, pos, static=None, low=False, high=False):
        live = []
        for c, lags in self.lags.items():
            for j in range(6):
                q = (pos - lags[j]) % PER
                if PATTERN[q] == c and (static is None or 0 <= static - lags[j] < NB):
                    live.append((j, lags[j], q))
        live.sort(reverse=True)

        def do(j, lag, q, act):
            b = s - lag
            if low:
                pl.when(b >= 0)(lambda: act(b, q, j))
            elif high:
                pl.when(b < NB)(lambda: act(b, q, j))
            else:
                act(b, q, j)

        for j, lag, q in live:
            if j == 0:
                do(j, lag, q, self.send)
        for j, lag, q in live:
            if j > 0:
                do(j, lag, q, lambda b, q, j: self.recv(b, q, j - 1))
            if self.relay and 0 < j < 5:
                do(j, lag, q, self.send)
        for j, lag, q in live:
            if not self.relay and 0 < j < 5:
                do(j, lag, q, self.send)

    def drain(self, first, last):
        def body(r, _):
            for pos in range(PER):
                for j in range(5):
                    self.send(r * PER + pos, pos, j, act=lambda d: d.wait_send())
            return 0

        lax.fori_loop(first, last, body, 0)


class Gather(Steps):
    lags = GATHER_LAGS
    relay = True

    def __init__(self, p, W, ss, rs):
        self.p, self.W, self.ss, self.rs = p, W, ss, rs

    def copy(self, ref, b, k, dev):
        return pltpu.make_async_remote_copy(
            ref, ref, self.ss.at[b, k], self.rs.at[b, k], device_id={"dp": dev}, device_id_type=MESH
        )

    def zref(self, b, c, zz):
        zz = jnp.clip(zz, 0, 3)
        return self.W.at[b, zz] if c == "Z" else self.W.at[b, zz, self.p.y, self.p.x]

    def zsend(self, b, c, hop, act):
        p = self.p

        @pl.when(both(p.z - hop + 1 >= 0, p.z < 3))
        def _():
            act(self.copy(self.zref(b, c, p.z - hop + 1), b, hop - 1, p.up))

        @pl.when(both(p.z + hop - 1 <= 3, p.z > 0))
        def _():
            act(self.copy(self.zref(b, c, p.z + hop - 1), b, 2 + hop, p.dn))

    def zrecv(self, b, c, hop):
        p = self.p

        @pl.when(p.z - hop >= 0)
        def _():
            self.copy(self.zref(b, c, p.z - hop), b, hop - 1, p.nx).wait_recv()

        @pl.when(p.z + hop <= 3)
        def _():
            self.copy(self.zref(b, c, p.z + hop), b, 2 + hop, p.nx).wait_recv()

    def stage(self, b, c, j):
        W = self.W
        x, y, z = self.p.x, self.p.y, self.p.z
        if c == "X":
            line = (7, W.at[b, :, :, x], W.at[b, :, :, 1 - x])
            return (1, 2, 3, (6, W.at[b, :, y, x], W.at[b, :, 1 - y, x]), line)[j]
        if c == "Y":
            line = (6, W.at[b, :, y], W.at[b, :, 1 - y])
            return (1, 2, 3, (7, W.at[b, :, y, x], W.at[b, :, y, 1 - x]), line)[j]
        line = (7, W.at[b, z, y, x], W.at[b, z, y, 1 - x])
        return (line, (6, W.at[b, z, y], W.at[b, z, 1 - y]), 1, 2, 3)[j]

    def send(self, b, pos, j, act=lambda d: d.start()):
        c = PATTERN[pos]
        st = self.stage(b, c, j)
        if isinstance(st, int):
            self.zsend(b, c, st, act)
        else:
            act(self.copy(st[1], b, st[0], self.p.ny if st[0] == 6 else self.p.nx))

    def recv(self, b, pos, j):
        c = PATTERN[pos]
        st = self.stage(b, c, j)
        if isinstance(st, int):
            self.zrecv(b, c, st)
        else:
            self.copy(st[2], b, st[0], self.p.nx).wait_recv()


class Scatter(Steps):
    lags = SCATTER_LAGS
    relay = False

    def __init__(self, p, G, out, L8, L4, LZ, P4, P2, P1, ss, rs):
        self.p, self.G, self.out, self.ss, self.rs = p, G, out, ss, rs
        self.L8, self.L4, self.LZ, self.P4, self.P2, self.P1 = L8, L4, LZ, P4, P2, P1

    def slot(self, b, pos):
        r = b // PER
        return r if PATTERN[pos] == "Z" else r * 3 + {0: 0, 1: 1, 3: 2}[pos]

    def copy(self, src, dst, b, k, dev):
        return pltpu.make_async_remote_copy(
            src, dst, self.ss.at[b, k], self.rs.at[b, k], device_id={"dp": dev}, device_id_type=MESH
        )

    def gz(self, b, c, t):
        t = jnp.clip(t, 0, 3)
        return self.G.at[b, t] if c == "Z" else self.G.at[b, t, self.p.y, self.p.x]

    def lz(self, b, pos, k):
        i = self.slot(b, pos)
        return self.P4.at[i, k] if PATTERN[pos] == "Z" else self.LZ.at[i, k]

    def add(self, ref, land):
        ref[...] = (ref[...].astype(jnp.float32) + land[...].astype(jnp.float32)).astype(ref.dtype)

    def zsend(self, b, pos, hop, act):
        p, c = self.p, PATTERN[pos]

        @pl.when(p.z + hop <= 3)
        def _():
            act(self.copy(self.gz(b, c, p.z + hop), self.lz(b, pos, hop - 1), b, hop - 1, p.up))

        @pl.when(p.z - hop >= 0)
        def _():
            act(self.copy(self.gz(b, c, p.z - hop), self.lz(b, pos, 2 + hop), b, 2 + hop, p.dn))

    def zrecv(self, b, pos, hop, final):
        p, c = self.p, PATTERN[pos]

        def take(k, t):
            land = self.lz(b, pos, k)
            self.copy(land, land, b, k, p.nx).wait_recv()
            if not final:
                self.add(self.gz(b, c, t), land)

        if not final:

            @pl.when(both(p.z >= 1, p.z - 1 + hop <= 3))
            def _():
                take(hop - 1, p.z - 1 + hop)

            @pl.when(both(p.z <= 2, p.z + 1 - hop >= 0))
            def _():
                take(2 + hop, p.z + 1 - hop)

            return
        own = self.G.at[b, p.z, p.y, p.x]
        below, above = self.lz(b, pos, 0), self.lz(b, pos, 3)
        f32 = jnp.float32

        @pl.when(p.z == 0)
        def _():
            take(3, p.z)
            self.out[b] = own[...].astype(f32) + above[...].astype(f32)

        @pl.when(p.z == 3)
        def _():
            take(0, p.z)
            self.out[b] = own[...].astype(f32) + below[...].astype(f32)

        @pl.when(both(p.z > 0, p.z < 3))
        def _():
            take(0, p.z)
            take(3, p.z)
            self.out[b] = own[...].astype(f32) + below[...].astype(f32) + above[...].astype(f32)

    def stage(self, b, pos, j):
        G = self.G
        x, y, z = self.p.x, self.p.y, self.p.z
        c, i = PATTERN[pos], self.slot(b, pos)
        if c == "X":
            first = (7, G.at[b, :, :, 1 - x], self.L8.at[i], G.at[b, :, :, x])
            return (first, (6, G.at[b, :, 1 - y, x], self.L4.at[i], G.at[b, :, y, x]), 3, 2, 1)[j]
        if c == "Y":
            first = (6, G.at[b, :, 1 - y], self.L8.at[i], G.at[b, :, y])
            return (first, (7, G.at[b, :, y, 1 - x], self.L4.at[i], G.at[b, :, y, x]), 3, 2, 1)[j]
        last = (7, G.at[b, z, y, 1 - x], self.P1.at[i], G.at[b, z, y, x])
        return (3, 2, 1, (6, G.at[b, z, 1 - y], self.P2.at[i], G.at[b, z, y]), last)[j]

    def send(self, b, pos, j, act=lambda d: d.start()):
        st = self.stage(b, pos, j)
        if isinstance(st, int):
            self.zsend(b, pos, st, act)
        else:
            act(self.copy(st[1], st[2], b, st[0], self.p.ny if st[0] == 6 else self.p.nx))

    def recv(self, b, pos, j):
        st = self.stage(b, pos, j)
        if isinstance(st, int):
            self.zrecv(b, pos, st, PATTERN[pos] != "Z" and j == 4)
        else:
            self.copy(st[2], st[2], b, st[0], self.p.nx).wait_recv()
            if j == 4:
                self.out[b] = st[3][...].astype(jnp.float32) + st[2][...].astype(jnp.float32)
            else:
                self.add(st[3], st[2])

    @staticmethod
    def landing(blocks, tail, dtype):
        n, m = blocks // PER * 3, blocks // PER
        return [
            pltpu.VMEM(shape + tail, dtype)
            for shape in ((n, 4, 2), (n, 4), (n, 6), (m, 6, 2, 2), (m, 2), (m,))
        ] + [pltpu.SemaphoreType.DMA((blocks, 8))] * 2
EPS = 1e-05
SEQ = 4
CAP = 256
ROWS = SEQ * CAP
HBM = pl.ANY


def dot(a, b):
    return jnp.dot(a, b, preferred_element_type=jnp.float32)


def dot_nt(a, b):
    return lax.dot_general(a, b, (((1,), (1,)), ((), ())), preferred_element_type=jnp.float32)


def halves(ref, rs):
    return jnp.concatenate([ref[0, rs, :], ref[1, rs, :]], 1).astype(jnp.float32)


def wblocks(W, first, count):
    return jnp.concatenate([W[first + i].reshape(1024, 128) for i in range(count)], 1)


def seq_rows(i):
    return pl.ds(i * CAP, CAP)


def cut(i, n):
    return pl.ds(pl.multiple_of(i * n, n), n)


def head_masks():
    lane = lax.broadcasted_iota(jnp.int32, (CAP, 128), 1)
    one = jnp.where(lane < HD, 1.0, 0.0)
    return [one.astype(jnp.bfloat16), (1.0 - one).astype(jnp.bfloat16)], lane < HD


def causal_mask():
    shape = (CAP, CAP)
    return lax.broadcasted_iota(jnp.int32, shape, 0) >= lax.broadcasted_iota(jnp.int32, shape, 1)


def softmax_rows(q, k, mask):
    s = jnp.where(mask, dot_nt(q, k) * (HD**-0.5), -1e30)
    e = jnp.exp(s - jnp.max(s, -1, keepdims=True))
    return e * (1.0 / jnp.sum(e, -1, keepdims=True))


def inv_rms(v):
    return lax.rsqrt(jnp.mean(v * v, -1, keepdims=True) + EPS)


def gate_of(rows_f, route):
    return jax.nn.sigmoid(jnp.sum(rows_f * route, -1, keepdims=True))


def own_slot(p, W, b):
    return W.at[b, p.z, p.y, p.x]


def forward_kernel(
    spot_ref,
    tile_ref,
    tok_ref,
    cot_ref,
    wq,
    wk,
    wv,
    wo,
    wu,
    wd,
    o_rows,
    o_cot,
    o_nT,
    o_qkv,
    o_mix,
    o_P,
    o_R,
    o_down,
    o_back,
    o_W,
    o_G,
    o_vec,
    W,
    VB,
    vecs,
    rows,
    cot,
    tokbuf,
    onehot,
    nrm,
    nT,
    dd,
    ddT,
    qkv,
    mixed,
    P,
    R,
    dacc,
    nacc,
    act,
    dup,
    Gst,
    ss,
    rs,
    vss,
    vrs,
    hs,
    hr,
    asnd,
    arcv,
    first,
    load,
    outs,
    gout,
):
    p = Place()
    t = p.t
    other = {"tensor": 1 - t}
    f32, bf = jnp.float32, jnp.bfloat16

    greet_all(p)

    own = [pltpu.make_async_copy(tile_ref, own_slot(p, VB, 0), first.at[NB])]
    for b in range(16):
        src, col = ((wq, wk, wv)[b % 3], b // 3) if b < 12 else (wo, b - 12)
        own.append(
            pltpu.make_async_copy(src.at[:, pl.ds(col * 128, 128)], own_slot(p, W, b), first.at[b])
        )
    for b in range(32):
        src = (wu, wd)[b % 4 // 2]
        own.append(
            pltpu.make_async_copy(
                src.at[:, pl.ds((b // 4 * 2 + b % 2) * 128, 128)],
                own_slot(p, W, 16 + b),
                first.at[16 + b],
            )
        )
    for c in own:
        c.start()

    def loader(i, a):
        return pltpu.make_async_copy((tok_ref, cot_ref)[a].at[i], tokbuf.at[a], load.at[a])

    loader(0, 0).start()
    loader(0, 1).start()
    await_all(p)
    for c in own:
        c.wait()
    W_steps = Gather(p, W, ss, rs)
    V_steps = Gather(p, VB, vss, vrs)

    def half_copy(i, a):
        ref = (rows, cot)[a].at[t, cut(i, CAP)]
        return pltpu.make_async_remote_copy(
            ref, ref, hs.at[i, a], hr.at[i, a], device_id=other, device_id_type=MESH
        )

    def half_wait(i, a):
        ref = (rows, cot)[a].at[1 - t, seq_rows(i)]
        pltpu.make_async_remote_copy(
            ref, ref, hs.at[i, a], hr.at[i, a], device_id=other, device_id_type=MESH
        ).wait_recv()

    def gather_part(i, _):
        def tick(q):
            W_steps.step(4 * i + q, q, low=True)
            for j, s in enumerate(VECTOR_STEPS):
                if s % 4 == q:

                    @pl.when(i == s // 4)
                    def _():
                        if j > 0:
                            V_steps.recv(0, 0, j - 1)
                        if j < 5:
                            V_steps.send(0, 0, j)

        for a in range(2):
            tick(2 * a)
            if a == 0:
                spot = jnp.broadcast_to(spot_ref[i], (128, CAP)).T[:, :1]
                hit = lax.broadcasted_iota(jnp.int32, (CAP, 2048), 1) == spot
                onehot[...] = jnp.where(hit, 1.0, 0.0).astype(bf)
            loader(i, a).wait()
            (rows, cot)[a][t, cut(i, CAP), :] = dot(onehot[...], tokbuf[a]).astype(bf)
            pl.when(i < 3)(lambda: loader(i + 1, a).start())
            tick(2 * a + 1)
            if a == 0:
                pl.when(i > 0)(lambda: half_copy(i - 1, 1).start())
            else:
                half_copy(i, 0).start()
        return 0

    lax.fori_loop(0, 4, gather_part, 0)
    half_copy(3, 1).start()

    for z in range(4):
        for y in range(2):
            vecs[:, pl.ds((z * 2 + y) * 128, 128)] = VB[0, z, y, 0] + pltpu.roll(
                VB[0, z, y, 1], 64, 1
            )

    def saver(k, src, dst):
        return pltpu.make_async_copy(src, dst, outs.at[k])

    saved = [saver(0, vecs, o_vec)]
    saved[0].start()

    dacc[...] = jnp.zeros_like(dacc)
    nacc[...] = jnp.zeros_like(nacc)

    for i in range(SEQ):
        W_steps.step(16 + i, i, static=16 + i)
        half_wait(i, 0)
        half_wait(i, 1)

        def norm_part(n, _):
            rs_ = cut(i * 8 + n, 32)
            r = halves(rows, rs_)
            nrm[rs_, :] = (r * inv_rms(r) * vecs[1:2, :]).astype(bf)
            dd[rs_, :] = (gate_of(r, vecs[0:1, :]) * halves(cot, rs_)).astype(bf)
            return 0

        lax.fori_loop(0, 8, norm_part, 0)
        for c in range(4):
            cs = pl.ds(c * 256, 256)
            nT[cs, seq_rows(i)] = nrm[seq_rows(i), cs].T
            ddT[cs, seq_rows(i)] = dd[seq_rows(i), cs].T
    later = [saver(1, rows, o_rows), saver(2, cot, o_cot), saver(3, nT, o_nT)]
    for c in later:
        c.start()
    saved += later[:2]
    nT_saved = later[2]

    masks, low_half = head_masks()
    mask = causal_mask()

    def attend(i, hp):
        r_ = seq_rows(i)
        q, k, v = qkv[3 * hp, r_, :], qkv[3 * hp + 1, r_, :], qkv[3 * hp + 2, r_, :]
        mix = [dot(softmax_rows(q * masks[h], k, mask).astype(bf), v) for h in (0, 1)]
        mixed[hp, r_, :] = jnp.where(low_half, mix[0], mix[1]).astype(bf)

    def pair_part(hp, _):
        W_steps.step(20 + 4 * hp, 0)
        W_steps.step(21 + 4 * hp, 1)
        y = dot(nrm[...], wblocks(W, 3 * hp, 3)).astype(bf)
        for c in range(3):
            qkv[3 * hp + c] = y[:, c * 128 : c * 128 + 128]
        for i in range(SEQ):
            attend(i, hp)
            if i in (0, 2):
                W_steps.step(22 + 4 * hp + i // 2, 2 + i // 2)
        return 0

    lax.fori_loop(0, 4, pair_part, 0)
    later = [saver(4, qkv, o_qkv), saver(5, mixed, o_mix)]
    for c in later:
        c.start()
    saved += later

    def att_copy(i):
        return pltpu.make_async_remote_copy(
            P.at[seq_rows(i)],
            R.at[seq_rows(i)],
            asnd.at[i],
            arcv.at[i],
            device_id=other,
            device_id_type=MESH,
        )

    def norm_mlp(i):
        att_copy(i).wait_recv()

        def norm_part(n, _):
            rs_ = cut(i * 8 + n, 32)
            h = halves(rows, rs_) + (P[rs_, :].astype(f32) + R[rs_, :].astype(f32))
            nrm[rs_, :] = (h * inv_rms(h) * vecs[2:3, :]).astype(bf)
            return 0

        lax.fori_loop(0, 8, norm_part, 0)
        for c in range(4):
            cs = pl.ds(c * 256, 256)
            nT[cs, seq_rows(i)] = nrm[seq_rows(i), cs].T

    out_w = wblocks(W, 12, 4)

    def project_out(i):
        mix = jnp.concatenate([mixed[h, seq_rows(i), :] for h in range(4)], 1)
        P[seq_rows(i), :] = dot_nt(mix, out_w).astype(bf)

    W_steps.step(36, 0)
    project_out(0)
    project_out(1)
    att_copy(0).start()
    W_steps.step(37, 1)
    project_out(2)
    att_copy(1).start()
    project_out(3)
    att_copy(2).start()
    nT_saved.wait()
    W_steps.step(38, 2)
    norm_mlp(0)
    att_copy(3).start()
    norm_mlp(1)
    W_steps.step(39, 3)
    norm_mlp(2)
    norm_mlp(3)
    saved.append(saver(6, W.at[pl.ds(0, 16)], o_W))
    saved[-1].start()
    later = [saver(7, P, o_P), saver(8, R, o_R)]
    for c in later:
        c.start()
    saved += later

    def g_copy(m):
        slot = lax.rem(m, 2)
        return pltpu.make_async_copy(Gst.at[slot], o_G.at[pl.ds(m * 4, 4)], gout.at[slot])

    partials = [
        saver(9 + n, tokbuf.at[n // 2, pl.ds(n % 2 * 1024, 1024)], (o_down, o_back)[n // 2].at[n % 2])
        for n in range(4)
    ]

    def mlp_part(m, _):
        slot = lax.rem(m, 2)
        s = 40 + 4 * m
        up_w = wblocks(W, 16 + 4 * m, 2)
        down_w = wblocks(W, 18 + 4 * m, 2)
        for ht in range(2):
            hs_ = pl.ds(ht * 512, 512)
            W_steps.step(s + ht, ht, high=True)
            u = dot(nrm[hs_, :], up_w)
            d = dot(dd[hs_, :], down_w)
            c0 = 0.7978845608028654
            u2 = u * u
            s1 = 1.0 + jnp.tanh(u * (c0 + (c0 * 0.044715) * u2))
            h = 0.5 * u
            act[hs_, :] = (h * s1).astype(bf)
            slope = s1 * (0.5 + h * (2.0 - s1) * (c0 + (3 * 0.044715 * c0) * u2))
            dup[hs_, :] = (d * slope).astype(bf)
        W_steps.step(s + 2, 2, high=True)
        for ht in range(2):
            hs_ = pl.ds(ht * 512, 512)
            dacc[hs_, :] += dot_nt(act[hs_, :], down_w)
            nacc[hs_, :] += dot_nt(dup[hs_, :], up_w)
        W_steps.step(s + 3, 3, high=True)
        W_steps.drain(m, m + 1)

        @pl.when(m == 7)
        def _():
            for n, c in enumerate(partials):
                piece = (dacc, nacc)[n // 2][:, n % 2 * 512 : n % 2 * 512 + 512]
                tokbuf[n // 2, pl.ds(n % 2 * 1024, 1024), :] = piece.astype(bf)
                c.start()

        @pl.when(m >= 2)
        def _():
            g_copy(m - 2).wait()

        for ht in range(2):
            hs_ = pl.ds(ht * 512, 512)
            gu = dot(nT[hs_, :], dup[...]).astype(bf)
            Gst[slot, 0, hs_, :] = gu[:, :128]
            Gst[slot, 1, hs_, :] = gu[:, 128:]
            gd = dot(ddT[hs_, :], act[...]).astype(bf)
            Gst[slot, 2, hs_, :] = gd[:, :128]
            Gst[slot, 3, hs_, :] = gd[:, 128:]
        g_copy(m).start()
        return 0

    lax.fori_loop(0, 8, mlp_part, 0)
    saved += partials
    for i in range(SEQ):
        half_copy(i, 0).wait_send()
        half_copy(i, 1).wait_send()
    for i in range(SEQ):
        att_copy(i).wait_send()
    W_steps.drain(8, NB // PER)
    for j in range(5):
        V_steps.send(0, 0, j, act=lambda d: d.wait_send())
    g_copy(6).wait()
    g_copy(7).wait()
    for c in saved:
        c.wait()


def forward_call(chosen, tile, tok, cotangent, weights):
    bf, f32 = jnp.bfloat16, jnp.float32
    S = jax.ShapeDtypeStruct
    DMA = pltpu.SemaphoreType.DMA
    any_ = pl.BlockSpec(memory_space=HBM)
    vm = pltpu.VMEM
    return pl.pallas_call(
        forward_kernel,
        out_shape=(
            S((2, ROWS, 512), bf),
            S((2, ROWS, 512), bf),
            S((1024, ROWS), bf),
            S((12, ROWS, 128), bf),
            S((4, ROWS, 128), bf),
            S((ROWS, 1024), bf),
            S((ROWS, 1024), bf),
            S((2, ROWS, 512), bf),
            S((2, ROWS, 512), bf),
            S((16, 4, 2, 2, 64, 128), bf),
            S((32, 1024, 128), bf),
            S((8, 1024), f32),
        ),
        in_specs=[pl.BlockSpec(memory_space=pltpu.VMEM)] + [any_] * 9,
        out_specs=[any_] * 12,
        scratch_shapes=[
            vm((NB, 4, 2, 2, 64, 128), bf),
            vm((1, 4, 2, 2, 8, 128), f32),
            vm((8, 1024), f32),
            vm((2, ROWS, 512), bf),
            vm((2, ROWS, 512), bf),
            vm((2, 2048, 512), bf),
            vm((CAP, 2048), bf),
            vm((ROWS, 1024), bf),
            vm((1024, ROWS), bf),
            vm((ROWS, 1024), bf),
            vm((1024, ROWS), bf),
            vm((12, ROWS, 128), bf),
            vm((4, ROWS, 128), bf),
            vm((ROWS, 1024), bf),
            vm((ROWS, 1024), bf),
            vm((ROWS, 1024), f32),
            vm((ROWS, 1024), f32),
            vm((ROWS, 256), bf),
            vm((ROWS, 256), bf),
            vm((2, 4, 1024, 128), bf),
            DMA((NB, 8)),
            DMA((NB, 8)),
            DMA((1, 8)),
            DMA((1, 8)),
            DMA((4, 2)),
            DMA((4, 2)),
            DMA((4,)),
            DMA((4,)),
            DMA((NB + 1,)),
            DMA((2,)),
            DMA((13,)),
            DMA((2,)),
        ],
        compiler_params=pltpu.CompilerParams(
            collective_id=1, has_side_effects=True, vmem_limit_bytes=63 * 1024 * 1024
        ),
        name="forward",
    )(chosen, tile, tok, cotangent, *weights)


def backward_kernel(
    rows,
    cot,
    nT_in,
    qkv_in,
    mix_in,
    P_in,
    R_in,
    down_in,
    back_in,
    W_in,
    G_in,
    vec_in,
    o_newr,
    o_newg,
    sum_out,
    o_vec,
    o_sum,
    G,
    Wa,
    qkv,
    mixed,
    nT,
    vecs,
    DR,
    NR,
    R1,
    bufs,
    buf2,
    da,
    daT,
    dmix,
    newr,
    newg,
    dhid,
    dlog,
    accs,
    GV,
    base,
    gsem,
    lsem,
    psem,
    prcv,
    qsem,
    qrcv,
    tout,
    *landing,
):
    p = Place()
    t = p.t
    other = {"tensor": 1 - t}
    f32, bf = jnp.float32, jnp.bfloat16
    wide, small = landing[:8], landing[8:]
    greet_all(p)

    def g_load(c):
        return pltpu.make_async_copy(G_in.at[pl.ds(4 * c, 4)], G.at[pl.ds(4 * c, 4)], gsem.at[c])

    g_load(0).start()
    g_load(1).start()

    def stream(s, names):
        q = lax.rem(s, 2)
        out = []
        for k in names:
            if k < 2:
                src = (P_in, R_in)[k].at[cut(s, CAP)]
                dst = buf2.at[q, k]
            else:
                src = (rows, cot, down_in, back_in)[k - 2].at[:, cut(s, CAP)]
                dst = bufs.at[q, k - 2]
            out.append(pltpu.make_async_copy(src, dst, lsem.at[q, k]))
        return out

    everything = (0, 1, 2, 3, 4, 5)
    for c in stream(0, everything):
        c.start()
    fixed = [
        pltpu.make_async_copy(a, b, base.at[i])
        for i, (a, b) in enumerate(
            ((vec_in, vecs), (W_in, Wa), (qkv_in, qkv), (mix_in, mixed), (nT_in, nT))
        )
    ]
    for c in fixed[:3]:
        c.start()
    await_all(p)

    def pair_copy(s, e):
        return pltpu.make_async_remote_copy(
            (down_in, back_in)[e].at[:, cut(s, CAP)],
            (DR, NR)[e].at[:, cut(s, CAP)],
            psem.at[s, e],
            prcv.at[s, e],
            device_id=other,
            device_id_type=MESH,
        )

    pair_copy(0, 0).start()
    pair_copy(0, 1).start()
    steps = Scatter(p, G, o_sum, *wide)
    v_steps = Scatter(p, GV, o_vec, *small)

    accs[...] = jnp.zeros_like(accs)

    def fold(v):
        return jnp.sum(v.reshape(4, 8, 1024), 0)

    def pick(v):
        return jnp.where(t == 0, v[:, :512], v[:, 512:])

    masks, low_half = head_masks()
    seen = lax.broadcasted_iota(jnp.int32, (CAP, CAP), 0) <= lax.broadcasted_iota(
        jnp.int32, (CAP, CAP), 1
    )

    def seq_part(s, _):
        def tick(q):
            if q % 4 == 0:
                g_load(2 * s + q // 4).wait()

                @pl.when(s < 3)
                def _():
                    g_load(2 * s + q // 4 + 2).start()

            steps.step(8 * s + q, q % 4, low=True)

        tick(0)
        q = lax.rem(s, 2)

        @pl.when(s + 1 < SEQ)
        def _():
            for c in stream(s + 1, everything):
                c.start()
            pair_copy(s + 1, 0).start()
            pair_copy(s + 1, 1).start()

        pl.when(s == 0)(lambda: fixed[0].wait())
        for c in stream(s, everything):
            c.wait()
        for e in range(2):
            pair_copy(s, e).wait_recv()

        def part(n, _):
            rs_ = cut(n, 32)
            as_ = pl.ds(pl.multiple_of(s * CAP + n * 32, 32), 32)

            def mine(k):
                return jnp.concatenate([bufs[q, k, 0, rs_, :], bufs[q, k, 1, rs_, :]], 1).astype(f32)

            r, c = mine(0), mine(1)
            att = buf2[q, 0, rs_, :].astype(f32) + buf2[q, 1, rs_, :].astype(f32)
            h = r + att
            branch = att + (mine(2) + halves(DR, as_))
            dn = mine(3) + halves(NR, as_)
            inv = inv_rms(h)
            sc = dn * vecs[2:3, :]
            dh = inv * sc - h * (inv * inv * inv * jnp.mean(sc * h, -1, keepdims=True))
            gate = gate_of(r, vecs[0:1, :])
            dl = jnp.sum(c * branch, -1, keepdims=True) * (gate * (1.0 - gate))
            da[rs_, :] = (gate * c + dh).astype(bf)
            accs[2] += fold(dn * (h * inv))
            accs[0] += fold(r * dl)
            newr[as_, :] = pick(r + gate * branch).astype(bf)
            dhid[as_, :] = pick(dh)
            dlog[as_, :] = jnp.broadcast_to(dl, (32, 128))
            return 0

        lax.fori_loop(0, 4, part, 0)
        tick(1)
        lax.fori_loop(4, 8, part, 0)
        tick(2)
        for c in range(4):
            cs = pl.ds(c * 256, 256)
            daT[cs, cut(s, CAP)] = da[:, cs].T

        @pl.when(s == 0)
        def _():
            for c in fixed[1:3]:
                c.wait()
            for c in fixed[3:]:
                c.start()

        tick(3)
        dm = dot(da[...], wblocks(Wa, 12, 4)).astype(bf)
        for h in range(4):
            dmix[h] = dm[:, h * 128 : h * 128 + 128]

        def pair_back(hp):
            r_ = cut(s, CAP)
            qh, kh, vh = [qkv[3 * hp + c, r_, :] for c in range(3)]
            dmh = dmix[hp]
            outs = []
            for h in (0, 1):
                sc = jnp.where(seen, dot_nt(kh, qh * masks[h]) * (HD**-0.5), -1e30)
                e = jnp.exp(sc - jnp.max(sc, 0, keepdims=True))
                pr = e * (1.0 / jnp.sum(e, 0, keepdims=True))
                dv = dot(pr.astype(bf), dmh)
                dp = dot_nt(vh * masks[h], dmh)
                ds = (pr * (dp - jnp.sum(dp * pr, 0, keepdims=True))).astype(bf)
                outs.append((dot(ds.T, kh), dot(ds, qh), dv))
            scale = HD**-0.5
            for i, (a, b) in enumerate(zip(*outs)):
                v = jnp.where(low_half, a, b)
                qkv[3 * hp + i, r_, :] = (v if i == 2 else v * scale).astype(bf)

        for hp in range(4):
            tick(4 + hp)
            pair_back(hp)
        return 0

    lax.fori_loop(0, SEQ, seq_part, 0)
    row_outs = [pltpu.make_async_copy(newr, o_newr, tout.at[0])]
    row_outs[0].start()

    def grad_unit(leftT, a, b, first):
        y = jnp.concatenate([a, b], 1)
        for ht in range(2):
            g = dot(leftT[pl.ds(ht * 512, 512), :], y).astype(bf)
            for c in range(2):
                G[first + c, pl.ds(ht * 2, 2)] = g[:, c * 128 : c * 128 + 128].reshape(
                    2, 2, 2, 64, 128
                )

    def back_copy(s):
        return pltpu.make_async_remote_copy(
            DR.at[:, seq_rows(s)],
            R1.at[:, seq_rows(s)],
            qsem.at[s],
            qrcv.at[s],
            device_id=other,
            device_id_type=MESH,
        )

    for s in range(2):
        for c in stream(s, (2, 3)):
            c.start()
    for c in fixed[3:]:
        c.wait()
    grad_unit(daT, mixed[0], mixed[1], 32)
    grad_unit(daT, mixed[2], mixed[3], 34)

    def grad_part(n, _):
        for e in range(2):
            steps.step(32 + 4 * n + 2 * e, 2 * e)
            steps.step(33 + 4 * n + 2 * e, 2 * e + 1)
            j = 2 * n + e
            grad_unit(nT, qkv[2 * j], qkv[2 * j + 1], 36 + 2 * j)
        return 0

    lax.fori_loop(0, 3, grad_part, 0)
    for s in range(SEQ):
        steps.step(44 + s, s)
        y = 0.0
        for g in range(3):
            x = jnp.concatenate([qkv[4 * g + i, seq_rows(s), :] for i in range(4)], 1)
            y = y + dot_nt(x, wblocks(Wa, 4 * g, 4))
        y = y.astype(bf)
        DR[0, seq_rows(s), :] = y[:, :512]
        DR[1, seq_rows(s), :] = y[:, 512:]
        if s > 0:
            back_copy(s - 1).start()
    steps.step(48, 0, high=True)
    back_copy(3).start()

    route_half = jnp.where(t == 0, vecs[0:1, :512], vecs[0:1, 512:])
    for s in range(SEQ):
        steps.step(49 + s, (1 + s) % 4, high=True)
        steps.drain(2 * s, 2 * s + 2)
        q = s % 2
        for c in stream(s, (2, 3)):
            c.wait()
        back_copy(s).wait_recv()

        def part(n, _):
            rs_ = cut(n, 32)
            as_ = pl.ds(pl.multiple_of(s * CAP + n * 32, 32), 32)
            r = jnp.concatenate([bufs[q, 0, 0, rs_, :], bufs[q, 0, 1, rs_, :]], 1).astype(f32)
            dn = halves(DR, as_) + halves(R1, as_)
            inv = inv_rms(r)
            sc = dn * vecs[1:2, :]
            dr = inv * sc - r * (inv * inv * inv * jnp.mean(sc * r, -1, keepdims=True))
            accs[1] += fold(dn * (r * inv))
            dl = dlog[as_, :]
            dl = jnp.concatenate([dl, dl, dl, dl], 1)
            ch = bufs[q, 1, t, rs_, :].astype(f32)
            newg[as_, :] = (ch + (dhid[as_, :] + pick(dr) + dl * route_half)).astype(bf)
            return 0

        lax.fori_loop(0, 8, part, 0)
        if s + 2 < SEQ:
            for c in stream(s + 2, (2, 3)):
                c.start()

    for z in range(4):
        for y in range(2):
            cs = pl.ds((z * 2 + y) * 128, 128)
            tile = jnp.concatenate(
                [jnp.sum(accs[k, :, cs], 0, keepdims=True) for k in range(3)]
                + [jnp.zeros((5, 128), f32)],
                0,
            )
            GV[0, z, y, 0] = tile
            GV[0, z, y, 1] = pltpu.roll(tile, 64, 1)
    for s in range(SEQ):
        back_copy(s).wait_send()
    row_outs.append(pltpu.make_async_copy(newg, o_newg, tout.at[1]))
    row_outs[1].start()
    v_steps.send(0, 0, 0)

    def sum_copy(e):
        part = pl.ds(32, 16) if e else pl.ds(0, 32)
        return pltpu.make_async_copy(o_sum.at[part], sum_out.at[part], tout.at[2 + e])

    for k, s in enumerate(range(53, 67)):
        steps.step(s, s % PER, static=s)
        if s == 53:
            sum_copy(0).start()
        if k in (0, 2, 3, 5, 7):
            j = (0, 2, 3, 5, 7).index(k) + 1
            v_steps.recv(0, 0, j - 1)
            if j < 5:
                v_steps.send(0, 0, j)
    sum_copy(1).start()
    for c in row_outs:
        c.wait()
    for s in range(SEQ):
        for e in range(2):
            pair_copy(s, e).wait_send()
    for j in range(5):
        v_steps.send(0, 0, j, act=lambda d: d.wait_send())
    steps.drain(8, NB // PER)
    sum_copy(0).wait()
    sum_copy(1).wait()


def backward_call(kept):
    bf, f32 = jnp.bfloat16, jnp.float32
    S = jax.ShapeDtypeStruct
    DMA = pltpu.SemaphoreType.DMA
    any_ = pl.BlockSpec(memory_space=HBM)
    vspec = pl.BlockSpec(memory_space=pltpu.VMEM)
    vm = pltpu.VMEM
    return pl.pallas_call(
        backward_kernel,
        out_shape=(
            S((ROWS, 512), bf),
            S((ROWS, 512), bf),
            S((NB, 64, 128), f32),
            S((1, 8, 128), f32),
        ),
        in_specs=[any_] * 12,
        out_specs=[any_, any_, any_, vspec],
        scratch_shapes=[
            vm((NB, 64, 128), f32),
            vm((NB, 4, 2, 2, 64, 128), bf),
            vm((16, 4, 2, 2, 64, 128), bf),
            vm((12, ROWS, 128), bf),
            vm((4, ROWS, 128), bf),
            vm((1024, ROWS), bf),
            vm((8, 1024), f32),
            vm((2, ROWS, 512), bf),
            vm((2, ROWS, 512), bf),
            vm((2, ROWS, 512), bf),
            vm((2, 4, 2, CAP, 512), bf),
            vm((2, 2, CAP, 1024), bf),
            vm((CAP, 1024), bf),
            vm((1024, ROWS), bf),
            vm((4, CAP, 128), bf),
            vm((ROWS, 512), bf),
            vm((ROWS, 512), bf),
            vm((ROWS, 512), f32),
            vm((ROWS, 128), f32),
            vm((3, 8, 1024), f32),
            vm((1, 4, 2, 2, 8, 128), f32),
            DMA((5,)),
            DMA((8,)),
            DMA((2, 6)),
            DMA((4, 2)),
            DMA((4, 2)),
            DMA((4,)),
            DMA((4,)),
            DMA((4,)),
        ]
        + Scatter.landing(NB, (64, 128), bf)
        + Scatter.landing(PER, (8, 128), f32),
        compiler_params=pltpu.CompilerParams(
            collective_id=2, has_side_effects=True, vmem_limit_bytes=63 * 1024 * 1024
        ),
        name="backward",
    )(*kept)


def place_kernel(
    spot_ref,
    vec_ref,
    own_ref,
    newr,
    newg,
    tok,
    cot,
    o_tok,
    o_cot,
    g_q,
    g_k,
    g_v,
    g_out,
    g_up,
    g_down,
    g_route,
    g_attn,
    g_mlp,
    old,
    out,
    new,
    came,
    went,
    own,
    nsem,
    gsem,
):
    bf = jnp.bfloat16
    for k, ref in enumerate((g_route, g_attn, g_mlp)):
        ref[...] = vec_ref[0, k, :64]

    def piece(n):
        return n // (2048 // SIZE), cut(n % (2048 // SIZE), SIZE)

    def load(n, a):
        i, rs = piece(n)
        return pltpu.make_async_copy((tok, cot)[a].at[i, rs], old.at[a, n], came.at[a, n])

    def store(n, a):
        i, rs = piece(n)
        return pltpu.make_async_copy(out.at[a, n], (o_tok, o_cot)[a].at[i, rs], went.at[a, n])

    pieces = SEQ * 2048 // SIZE
    news = [pltpu.make_async_copy((newr, newg)[a], new.at[a], nsem.at[a]) for a in range(2)]
    sums = pltpu.make_async_copy(own_ref, own, nsem.at[2])
    for c in news + [sums]:
        c.start()

    def start(n, _):
        load(n, 0).start()
        load(n, 1).start()
        return 0

    lax.fori_loop(0, pieces, start, 0)

    moves = []
    for b in range(NB):
        if b < 32:
            ref, k = (g_up, g_down)[b % 4 // 2], b // 4 * 2 + b % 2
        else:
            ref, k = (g_out, b - 32) if b < 36 else ((g_q, g_k, g_v)[b % 3], (b - 36) // 3)
        moves.append(
            pltpu.make_async_copy(own.at[b], ref.at[:, pl.ds(k * 128, 128)], gsem.at[b])
        )
    for c in news:
        c.wait()
    ones = jnp.ones((CAP, 128), bf)

    def place(n, _):
        i, _rs = piece(n)

        @pl.when(n == 2)
        def _():
            sums.wait()
            for c in moves:
                c.start()

        row = lax.broadcasted_iota(jnp.int32, (SIZE, CAP), 0) + n % (2048 // SIZE) * SIZE
        hit = jnp.where(row == spot_ref[i], 1.0, 0.0).astype(bf)
        kept = 1.0 - dot(hit, ones)
        kept = jnp.concatenate([kept, kept, kept, kept], 1).astype(bf)
        for a in range(2):
            moved = dot(hit, new[a, cut(i, CAP), :]).astype(bf)
            load(n, a).wait()
            out[a, n] = old[a, n] * kept + moved
            store(n, a).start()
        return 0

    lax.fori_loop(0, pieces, place, 0)

    def finish(n, _):
        store(n, 0).wait()
        store(n, 1).wait()
        return 0

    lax.fori_loop(0, pieces, finish, 0)
    for c in moves:
        c.wait()


SIZE = 2048


def place_call(spot, vec, own, newr, newg, tok, cotangent):
    bf, f32 = jnp.bfloat16, jnp.float32
    S = jax.ShapeDtypeStruct
    DMA = pltpu.SemaphoreType.DMA
    any_ = pl.BlockSpec(memory_space=pltpu.MemorySpace.HBM)
    vspec = pl.BlockSpec(memory_space=pltpu.VMEM)
    pieces = SEQ * 2048 // SIZE
    return pl.pallas_call(
        place_kernel,
        out_shape=(
            S((SEQ, 2048, 512), bf),
            S((SEQ, 2048, 512), bf),
            S((64, 512), f32),
            S((64, 512), f32),
            S((64, 512), f32),
            S((64, 512), f32),
            S((64, 2048), f32),
            S((64, 2048), f32),
            S((64,), f32),
            S((64,), f32),
            S((64,), f32),
        ),
        in_specs=[vspec, vspec] + [any_] * 5,
        out_specs=[any_] * 8 + [vspec] * 3,
        scratch_shapes=[
            pltpu.VMEM((2, pieces, SIZE, 512), bf),
            pltpu.VMEM((2, pieces, SIZE, 512), bf),
            pltpu.VMEM((2, ROWS, 512), bf),
            DMA((2, pieces)),
            DMA((2, pieces)),
            pltpu.VMEM((NB, 64, 128), f32),
            DMA((3,)),
            DMA((NB,)),
        ],
        compiler_params=pltpu.CompilerParams(vmem_limit_bytes=63 * 1024 * 1024),
        name="place_rows",
    )(spot, vec, own, newr, newg, tok, cotangent)


def to_tile(w_route, gain_attn, gain_mlp):
    v = jnp.stack([w_route, gain_attn, gain_mlp]).astype(jnp.float32)
    return jnp.pad(v, ((0, 5), (0, 64)))


def fused(
    tokens,
    routed,
    w_query,
    w_key,
    w_value,
    w_out,
    w_up,
    w_down,
    w_route,
    gain_attn,
    gain_mlp,
    cotangent,
):
    tok = tokens.reshape(SEQ, 2048, 512)
    cot = cotangent.reshape(SEQ, 2048, 512)
    spot = routed.reshape(SEQ, 1, CAP)
    tile = to_tile(w_route, gain_attn, gain_mlp)
    weights = (w_query, w_key, w_value, w_out.T, w_up, w_down.T)
    kept = list(forward_call(spot, tile, tok, cot, weights))
    kept[10] = kept[10].reshape(32, 4, 2, 2, 64, 128)
    newr, newg, own, vec = backward_call(kept)
    output, grad, g_q, g_k, g_v, g_out, g_up, g_down, *g_vec = place_call(
        spot, vec, own, newr, newg, tok, cot
    )
    return (
        output.reshape(tokens.shape),
        grad.reshape(tokens.shape),
        g_q,
        g_k,
        g_v,
        g_out.T,
        g_up,
        g_down.T,
        *g_vec,
    )


def shards(tokens, routed, *rest):
    sizes = (lax.axis_size("dp"), lax.axis_size("tensor"))
    here = tokens.shape == (4, 1, 2048, 512) and routed.shape == (4, 1, 256)
    if sizes == (16, 2) and here:
        return fused(tokens, routed, *rest)
    return plain(tokens, routed, *rest)


def solution(mesh):
    rows = P("dp", "tensor")
    columns = P("tensor", "dp")
    vector = P("dp")
    stored = P(None, "dp", None, "tensor")
    return jax.shard_map(
        shards,
        mesh=mesh,
        in_specs=(
            stored,
            P(None, "dp", None),
            rows,
            rows,
            rows,
            columns,
            rows,
            columns,
            vector,
            vector,
            vector,
            stored,
        ),
        out_specs=(
            stored,
            stored,
            rows,
            rows,
            rows,
            columns,
            rows,
            columns,
            vector,
            vector,
            vector,
        ),
        check_vma=False,
    )
```
